32 devices in a mesh: tok: 4 (over z), head: 8 (over y, x, core).
Axes of the slice: x: 2, y: 2, z: 4, core: 2. Of those that a mesh axis runs over, the one named last changes fastest.
Arguments:
- block_input: bfloat16 [4, 1536, 2048], P('tok', 'head'), may hold values from -6 to 6
- segment_ids: int32 [4, 1536], P('tok'), may hold values from 0 to 3, as said below
- positions: int32 [4, 1536], P('tok'), may hold values from 0 to 1023, as said below
- attention_gain: float32 [2048], replicated, may hold values from 0.5 to 1.5
- query_down: bfloat16 [2048, 1024], replicated, may hold values from -0.125 to 0.125
- query_gain: float32 [1024], replicated, may hold values from 0.5 to 1.5
- query_up: bfloat16 [1024, 4096], P(None, 'head'), may hold values from -0.1875 to 0.1875
- key_proj: bfloat16 [2048, 256], replicated, may hold values from -0.125 to 0.125
- value_proj: bfloat16 [2048, 256], replicated, may hold values from -0.125 to 0.125
- out_proj: bfloat16 [4096, 2048], P('head'), may hold values from -0.375 to 0.375
- feed_gain: float32 [2048], replicated, may hold values from 0.5 to 1.5
- gate_weight: bfloat16 [2048, 5632], P(None, 'head'), may hold values from -0.125 to 0.125
- up_weight: bfloat16 [2048, 5632], P(None, 'head'), may hold values from -0.125 to 0.125
- down_weight: bfloat16 [5632, 2048], P('head'), may hold values from -0.078125 to 0.078125
- out_grad: bfloat16 [4, 1536, 2048], P('tok', 'head'), may hold values from -6 to 6
Outputs:
- block_output: bfloat16 [4, 1536, 2048], P('tok', 'head')
- input_gradient: float32 [4, 1536, 2048], P('tok', 'head')
- attention_gain_gradient: float32 [2048], replicated
- query_down_gradient: float32 [2048, 1024], replicated
- query_gain_gradient: float32 [1024], replicated
- query_up_gradient: float32 [1024, 4096], P(None, 'head')
- key_proj_gradient: float32 [2048, 256], replicated
- value_proj_gradient: float32 [2048, 256], replicated
- out_proj_gradient: float32 [4096, 2048], P('head')
- feed_gain_gradient: float32 [2048], replicated
- gate_weight_gradient: float32 [2048, 5632], P(None, 'head')
- up_weight_gradient: float32 [2048, 5632], P(None, 'head')
- down_weight_gradient: float32 [5632, 2048], P('head')
The draws below stay inside these ranges and needn't reach their ends.
Inputs may be any that keep to these rules, and one draw needn't show every extreme that they name: `segment_ids`: within each pack the ids start at 0 and never fall; the first document of every pack has min(1536, max(1024, 768)) tokens, and every pack has the same number of documents. Within a document the positions rise by one from token to token; the first document of every pack starts at 0.
All inputs are finite; a program needn't handle non-finite values.
Results may differ from the reference program's by a relative error of at most 0.023.
Values may be sent and summed in bfloat16 or wider, within the bound.
No kernel may reach another device: no remote copies, remote signals or barrier semaphores. Data moves between devices by JAX's collectives and lax.ppermute only.
A program may use at most 256 MiB of HBM per device.

```python
import math
import jax
import jax.numpy as jnp
from jax import lax

D = 2048
HEADS = 16
HEAD_DIM = 256
QRANK = 1024
FF = 5632
DOC_MIN = 1024
PACK = 1536
PACKS = 4


def pack_layout(key):
    first_length = min(PACK, max(DOC_MIN, PACK // 2))
    remain = PACK - first_length
    order = jnp.arange(PACK).astype(jnp.int32)
    starts = jnp.zeros((PACKS, PACK), jnp.bool_)
    if remain > 0:
        starts = starts | (order[None, :] == first_length)
    if remain >= 6:
        third = remain // 3
        cut_one = first_length + 1 + jax.random.randint(jax.random.fold_in(key, 11), (PACKS, 1), 0, third - 1)
        cut_two = first_length + third + 1 + jax.random.randint(jax.random.fold_in(key, 13), (PACKS, 1), 0, third - 1)
        starts = starts | (order[None, :] == cut_one) | (order[None, :] == cut_two)
    segments = jnp.cumsum(starts.astype(jnp.int32), axis=1).astype(jnp.int32)
    begins = lax.cummax(jnp.where(starts, order[None, :], 0).astype(jnp.int32), axis=1)
    offsets = jax.random.randint(jax.random.fold_in(key, 12), (PACKS, 4), 0, first_length - remain + 1)
    offsets = jnp.where(jnp.arange(4)[None, :] == 0, 0, offsets).astype(jnp.int32)
    places = order[None, :] - begins + jnp.take_along_axis(offsets, segments, axis=1)
    return (segments, places.astype(jnp.int32))


def draw_segment_ids(key, part):
    return pack_layout(key)[0]


def draw_positions(key, part):
    return pack_layout(key)[1]


def block_scale(key, shape, shards, smallest, largest):
    loudness = 1.0
    for position, blocks in shards:
        draws = jax.random.uniform(jax.random.fold_in(jax.random.fold_in(key, 6), position), (blocks,), jnp.float32, smallest / len(shards), largest / len(shards))
        loudness = loudness * jnp.repeat(jnp.exp(draws), shape[position] // blocks).reshape((-1,) + (1,) * (len(shape) - 1 - position))
    return loudness


def gaussian(key, shape, scale, limit, shards=(), kind=jnp.bfloat16):
    factor_of = block_scale(key, shape, shards, -0.22, 0.18) if shards else 1.0
    values = jax.random.normal(key, shape, jnp.float32) * scale * factor_of
    return jnp.minimum(jnp.maximum(values, -limit), limit).astype(kind)


def setup_inputs(seed: int = 0) -> dict:
    seeds = jax.random.split(jax.random.key(seed), 16)
    block_input = gaussian(seeds[0], (PACKS, PACK, D), 1.0, 6.0, ((0, 4), (1, 8)))
    segment_ids = draw_segment_ids(jax.random.fold_in(seeds[15], 71), 0)
    positions = draw_positions(jax.random.fold_in(seeds[15], 71), 0)
    attention_gain = jnp.clip(1.0 + 0.1 * jax.random.normal(seeds[3], (D,), jnp.float32), 0.5, 1.5)
    query_down = gaussian(seeds[4], (D, QRANK), D ** -0.5, 0.125)
    query_gain = jnp.clip(1.0 + 0.1 * jax.random.normal(seeds[5], (QRANK,), jnp.float32), 0.5, 1.5)
    query_up = gaussian(seeds[6], (QRANK, HEADS * HEAD_DIM), QRANK ** -0.5, 0.1875, ((1, 8),))
    key_proj = gaussian(seeds[7], (D, HEAD_DIM), D ** -0.5, 0.125)
    value_proj = gaussian(seeds[8], (D, HEAD_DIM), D ** -0.5, 0.125)
    out_proj = gaussian(seeds[9], (HEADS * HEAD_DIM, D), (HEADS * HEAD_DIM // 16) ** -0.5, 0.375, ((0, 8),))
    feed_gain = jnp.clip(1.0 + 0.1 * jax.random.normal(seeds[10], (D,), jnp.float32), 0.5, 1.5)
    gate_weight = gaussian(seeds[11], (D, FF), D ** -0.5, 0.125, ((1, 8),))
    up_weight = gaussian(seeds[12], (D, FF), D ** -0.5, 0.125, ((1, 8),))
    down_weight = gaussian(seeds[13], (FF, D), FF ** -0.5, 0.078125, ((0, 8),))
    out_grad = gaussian(seeds[14], (PACKS, PACK, D), 1.0, 6.0, ((0, 4), (1, 8)))
    return {"block_input": block_input, "segment_ids": segment_ids, "positions": positions, "attention_gain": attention_gain, "query_down": query_down, "query_gain": query_gain, "query_up": query_up, "key_proj": key_proj, "value_proj": value_proj, "out_proj": out_proj, "feed_gain": feed_gain, "gate_weight": gate_weight, "up_weight": up_weight, "down_weight": down_weight, "out_grad": out_grad}


@jax.custom_vjp
def low(v):
    return lax.optimization_barrier(v.astype(jnp.bfloat16)).astype(jnp.float32)

@jax.custom_vjp
def low_back(v):
    return v

def low_keep(v):
    return (low(v), None)

def low_pass(kept, grad):
    return (grad,)

def back_keep(v):
    return (v, None)

def back_low(kept, grad):
    return (low(grad),)
low.defvjp(low_keep, low_pass)
low_back.defvjp(back_keep, back_low)
norm_epsilon = 1e-05
rope_base = 10000.0
highest = lax.Precision.HIGHEST

def product(left, right):
    return jnp.dot(left, right, precision=highest)

def normalize(value, gain):
    scale = lax.rsqrt(lax.optimization_barrier(jnp.mean(value * value, axis=-1, keepdims=True)) + norm_epsilon)
    return value * scale * gain

def rotation(places, head_width):
    half = head_width // 2
    steps = jnp.arange(half).astype(jnp.float32) * (2.0 / head_width)
    inverse = jnp.exp(steps * -math.log(rope_base))
    angles = places.astype(jnp.float32)[:, None] * inverse[None, :]
    return (jnp.cos(angles), jnp.sin(angles))

def rotate(value, cosine, sine):
    half = value.shape[-1] // 2
    first = value[..., :half]
    second = value[..., half:]
    return jnp.concatenate([first * cosine - second * sine, second * cosine + first * sine], axis=-1)

def attend(queries, keys, values, segments):
    length = queries.shape[0]
    order = jnp.arange(length)
    allowed = (order[None, :] <= order[:, None]) & (segments[None, :] == segments[:, None])
    scores = low_back(jnp.einsum('qhd,kd->hqk', queries, keys, precision=highest) * (1.0 / math.sqrt(HEAD_DIM)))
    scores = jnp.where(allowed[None], scores, -1e+30)
    top = lax.optimization_barrier(jnp.max(scores, axis=-1, keepdims=True))
    weights = jnp.exp(scores - top)
    probs = weights / lax.optimization_barrier(jnp.sum(weights, axis=-1, keepdims=True))
    mixed = jnp.einsum('hqk,kd->qhd', low(probs), values, precision=highest)
    return low(low_back(mixed))

def forward(params, rows_in, segments, places):
    attention_gain, query_down, query_gain, query_up, key_proj, value_proj, out_proj, feed_gain, gate_weight, up_weight, down_weight = params
    length = rows_in.shape[0]
    normed_in = low(normalize(rows_in, attention_gain))
    latent = low_back(product(normed_in, query_down))
    latent_normed = low(normalize(latent, query_gain))
    cosine, sine = rotation(places, HEAD_DIM)
    query_pre = low_back(product(latent_normed, query_up)).reshape(length, HEADS, HEAD_DIM)
    queries = low(rotate(query_pre, cosine[:, None], sine[:, None]))
    key_pre = low_back(product(normed_in, key_proj))
    keys = low(rotate(key_pre, cosine, sine))
    values = low(low_back(product(normed_in, value_proj)))
    mixed = jax.checkpoint(attend)(queries, keys, values, segments)
    attention = low_back(product(mixed.reshape(length, HEADS * HEAD_DIM), out_proj))
    middle = rows_in + attention
    normed_mid = low(normalize(middle, feed_gain))
    gate = low_back(product(normed_mid, gate_weight))
    upward = low_back(product(normed_mid, up_weight))
    hidden = low(jax.nn.silu(gate) * upward)
    return middle + product(hidden, down_weight)

def reference(block_input, segment_ids, positions, attention_gain, query_down, query_gain, query_up, key_proj, value_proj, out_proj, feed_gain, gate_weight, up_weight, down_weight, out_grad):
    params = tuple((item.astype(jnp.float32) for item in (attention_gain, query_down, query_gain, query_up, key_proj, value_proj, out_proj, feed_gain, gate_weight, up_weight, down_weight)))

    def one_pack(totals, inputs):
        rows_in, segments, places, cotangent = inputs

        def layer(values_in, weights):
            return forward(weights, values_in, segments, places)
        result, pullback = jax.vjp(layer, rows_in.astype(jnp.float32), params)
        input_grad, weight_grads = pullback(cotangent.astype(jnp.float32))
        totals = tuple((left + right for left, right in zip(totals, weight_grads)))
        return (totals, (result.astype(jnp.bfloat16), input_grad))
    zeros = tuple((jnp.zeros(item.shape, jnp.float32) for item in params))
    grads, (outputs, input_gradient) = lax.scan(one_pack, zeros, (block_input, segment_ids, positions, out_grad))
    return (outputs, input_gradient, grads[0], grads[1], grads[2], grads[3], grads[4], grads[5], grads[6], grads[7], grads[8], grads[9], grads[10])
```

```python
import functools
import math

import jax
import jax.numpy as jnp
from jax import lax
from jax.experimental import pallas as pl
from jax.experimental.pallas import tpu as pltpu
from jax.sharding import PartitionSpec as P

norm_epsilon = 1e-05
rope_base = 10000.0
first_document = 1024
bf16 = jnp.bfloat16
f32 = jnp.float32


def inverse_rms(value):
    return lax.rsqrt(jnp.mean(value * value, axis=-1, keepdims=True) + norm_epsilon)


def norm_backward(value, gain, upper):
    scale = inverse_rms(value)
    scaled = upper * gain
    lower = scale * scaled - value * (scale * scale * scale) * jnp.mean(
        scaled * value, axis=-1, keepdims=True
    )
    return (lower, jnp.sum(upper * value * scale, axis=0))


def rotation(places, head_width):
    half = head_width // 2
    steps = jnp.arange(half).astype(f32) * (2.0 / head_width)
    inverse = jnp.exp(steps * -math.log(rope_base))
    angles = places.astype(f32)[:, None] * inverse[None, :]
    return (jnp.cos(angles), jnp.sin(angles))


def rotate(value, cosine, sine):
    half = value.shape[-1] // 2
    first = value[..., :half]
    second = value[..., half:]
    return jnp.concatenate(
        [first * cosine - second * sine, second * cosine + first * sine], axis=-1
    )


def dot(left, right):
    return jnp.dot(left, right, preferred_element_type=f32)


def right_transposed(left, right):
    return lax.dot_general(left, right, (((1,), (1,)), ((), ())), preferred_element_type=f32)


def left_transposed(left, right):
    return lax.dot_general(left, right, (((0,), (0,)), ((), ())), preferred_element_type=f32)


def add_low(left, right):
    return (left.astype(f32) + right.astype(f32)).astype(bf16)


class Clock:
    def __init__(self):
        self.last = ()

    def __call__(self, *values):
        held = lax.optimization_barrier(values + self.last)
        self.last = (held[0],)
        return held[0] if len(values) == 1 else held[: len(values)]


class Plane:
    def __init__(self, size):
        self.size = size
        self.fast = size == 8 and lax.axis_size("tok") == 4
        self.me = lax.axis_index("head")
        if self.fast:
            even = [index % 2 == 0 for index in range(size)]
            self.hop_a = [(i, i ^ (2 if even[i] else 4)) for i in range(size)]
            self.hop_b = [(i, i ^ (4 if even[i] else 2)) for i in range(size)]
            self.hop_c = [(i, i ^ 1) for i in range(size)]
            mask_a = jnp.where(self.me % 2 == 0, 2, 4)
            other = self.me ^ 1
            order = [
                self.me,
                other,
                self.me ^ mask_a,
                other ^ (6 - mask_a),
                self.me ^ (6 - mask_a),
                other ^ mask_a,
                self.me ^ 6,
                other ^ 6,
            ]
            self.table = jnp.stack(order).astype(jnp.int32)
            self.groups = [(0, 2), (2, 6), (6, 8)]
        else:
            self.table = jnp.arange(size, dtype=jnp.int32)
            self.groups = [(0, size)]

    def move(self, value, hop):
        return lax.ppermute(value, "head", hop)

    def gather(self, rows):
        whole = lax.all_gather(rows, "head", axis=0, tiled=True)
        return list(jnp.split(whole, self.size, axis=0))

    def scatter(self, pieces):
        whole = jnp.concatenate(pieces, axis=0)
        return lax.psum_scatter(whole, "head", scatter_dimension=0, tiled=True).astype(f32)

    def total(self, value):
        if not self.fast:
            return lax.psum(value, "head")
        for bit in (1, 2, 4):
            value = value + self.move(value, [(i, i ^ bit) for i in range(8)])
        return value


class Line:
    def __init__(self, size):
        self.size = size
        self.me = lax.axis_index("tok")
        half = size // 2
        self.stages = [([(k, k + 1), (size - 1 - k, size - 2 - k)], None) for k in range(half - 1)]
        self.stages.append(([(half - 1, half), (half, half - 1)], None))
        for k in reversed(range(half - 1)):
            self.stages.append(([(k + 1, k), (size - 2 - k, size - 1 - k)], k))

    def start(self, stage, value):
        return lax.ppermute(value, "tok", self.stages[stage][0])

    def finish(self, stage, value, came, plus=add_low):
        outward = self.stages[stage][1]
        if outward is None:
            return plus(value, came)
        mine = (self.me == outward) | (self.me == self.size - 1 - outward)
        return jnp.where(mine, came, value)

    def total(self, value, plus=add_low):
        for stage in range(len(self.stages)):
            value = self.finish(stage, value, self.start(stage, value), plus)
        return value


class Belt:
    inward = [(0, 1), (3, 2)]
    middle = [(1, 2), (2, 1)]
    outward = [(1, 0), (2, 3)]

    def __init__(self, line, clock):
        self.clock = clock
        self.inner = jnp.where((line.me == 1) | (line.me == 2), 1, 0).astype(jnp.int32).reshape(1)

    def move(self, value, pairs):
        return lax.ppermute(value, "tok", pairs)

    def begin(self, value):
        value = self.clock(value)
        return {"own": value, "came": self.move(value, self.inward)}

    def cross(self, item):
        item["came"] = self.clock(item["came"])
        item["own"] = self.clock(add_rows(item["own"], item["came"]))
        item["came"] = self.move(item["own"], self.middle)

    def back(self, item, value=None):
        item["came"] = self.clock(item["came"])
        if value is None:
            item["own"] = self.clock(add_rows(item["own"], item["came"]))
            item["came"] = self.move(item["own"], self.outward)
            return None
        both = self.clock(add_or_begin(self.inner, item["own"], item["came"], value))
        came = self.move(both, self.inward + self.outward)
        item["own"], item["came"] = both, came
        return {"own": value, "came": came}

    def end(self, item, size, at=0, past=None):
        item["came"] = self.clock(item["came"])
        return self.clock(settle(self.inner, item["own"], item["came"], size, at, past))


def query_blocks(length):
    first = min(length, max(first_document, length // 2))
    block = 256
    return [
        (start, min(block, length - start), 0 if start < first else first)
        for start in range(0, length, block)
    ]


def allowed(seg_column, seg_row, start, rows, low, high):
    query_order = start + lax.broadcasted_iota(jnp.int32, (rows, high - low), 0)
    key_order = low + lax.broadcasted_iota(jnp.int32, (rows, high - low), 1)
    same = seg_column[start : start + rows, :] == seg_row[:, low:high]
    return (key_order <= query_order) & same


def weights_of(stacked, keys, permit, heads, scale):
    scores = right_transposed(stacked, keys) * scale
    scores = jnp.where(jnp.concatenate([permit] * heads, axis=0), scores, -1e30)
    top = jnp.max(scores, axis=-1, keepdims=True)
    weights = jnp.exp(scores - top)
    return weights, jnp.sum(weights, axis=-1, keepdims=True)


def stack_heads(ref, start, rows, heads, width):
    return jnp.concatenate(
        [ref[start : start + rows, h * width : (h + 1) * width] for h in range(heads)], axis=0
    )


def attend_forward_kernel(count, heads, width, rank, scale, *refs):
    table = refs[0]
    pieces = refs[1 : 1 + count]
    weight, cosine, sine, seg_column, seg_row = refs[1 + count : 6 + count]
    queries, keys, values, mixed, mixed_there = refs[6 + count :]
    length = queries.shape[0]
    rows = length // count
    half = width // 2
    for r in range(count):
        there = pl.ds(pl.multiple_of(table[r] * rows, rows), rows)
        keys[there, :] = pieces[r][:, rank : rank + width]
        values[there, :] = pieces[r][:, rank + width :]
        flat = dot(pieces[r][:, :rank], weight[...])
        cos = cosine[there, :]
        sin = sine[there, :]
        for h in range(heads):
            first = flat[:, h * width : h * width + half]
            second = flat[:, h * width + half : (h + 1) * width]
            queries[there, h * width : h * width + half] = (first * cos - second * sin).astype(bf16)
            queries[there, h * width + half : (h + 1) * width] = (
                second * cos + first * sin
            ).astype(bf16)
    for start, size, low in query_blocks(length):
        high = start + size
        stacked = stack_heads(queries, start, size, heads, width)
        permit = allowed(seg_column, seg_row, start, size, low, high)
        weights, total = weights_of(stacked, keys[low:high, :], permit, heads, scale)
        probs = (weights / total).astype(bf16)
        result = dot(probs, values[low:high, :]).astype(bf16)
        for h in range(heads):
            mixed[start:high, h * width : (h + 1) * width] = result[h * size : (h + 1) * size]
    for r in range(count):
        there = pl.ds(pl.multiple_of(table[r] * rows, rows), rows)
        mixed_there[r * rows : (r + 1) * rows, :] = mixed[there, :]


def brief():
    return pl.CostEstimate(flops=1024, bytes_accessed=1024, transcendentals=0)


def vmem():
    return pl.BlockSpec(memory_space=pltpu.VMEM)


def smem():
    return pl.BlockSpec(memory_space=pltpu.SMEM)


def attend_forward(table, pieces, weight, cosine, sine, segments, heads, width, scale):
    count = len(pieces)
    length = cosine.shape[0]
    rank = weight.shape[0]
    shapes = [
        jax.ShapeDtypeStruct((length, heads * width), bf16),
        jax.ShapeDtypeStruct((length, width), bf16),
        jax.ShapeDtypeStruct((length, width), bf16),
        jax.ShapeDtypeStruct((length, heads * width), bf16),
        jax.ShapeDtypeStruct((length, heads * width), bf16),
    ]
    return pl.pallas_call(
        functools.partial(attend_forward_kernel, count, heads, width, rank, scale),
        out_shape=shapes,
        in_specs=[smem()] + [vmem()] * (count + 5),
        out_specs=[vmem()] * 5,
        compiler_params=pltpu.CompilerParams(vmem_limit_bytes=48 << 20),
        cost_estimate=brief(),
        name="attend_forward",
    )(table, *pieces, weight, cosine, sine, segments[:, None], segments[None, :])


def attend_backward_kernel(parts, heads, width, scale, *refs):
    table = refs[0]
    grads_in = refs[1 : 1 + parts]
    queries, keys, values, cosine, sine, seg_column, seg_row = refs[1 + parts : 8 + parts]
    query_there, pair_there, outer, query_out, key_total, value_total = refs[8 + parts :]
    length = queries.shape[0]
    count = table.shape[0]
    rows = length // count
    half = width // 2

    def there(r):
        return pl.ds(pl.multiple_of(table[r] * rows, rows), rows)

    r = 0
    for part in grads_in:
        for k in range(part.shape[0] // rows):
            outer[there(r), :] = part[k * rows : (k + 1) * rows, :]
            r += 1
    key_total[...] = jnp.zeros_like(key_total)
    value_total[...] = jnp.zeros_like(value_total)
    for start, size, low in query_blocks(length):
        high = start + size
        stacked = stack_heads(queries, start, size, heads, width)
        grads = stack_heads(outer, start, size, heads, width)
        permit = allowed(seg_column, seg_row, start, size, low, high)
        weights, total = weights_of(stacked, keys[low:high, :], permit, heads, scale)
        probs = weights / total
        prob_grad = right_transposed(grads, values[low:high, :])
        centre = jnp.sum(probs * prob_grad, axis=-1, keepdims=True)
        score_grad = (probs * (prob_grad - centre)).astype(bf16)
        query_grad = dot(score_grad, keys[low:high, :]) * scale
        key_total[low:high, :] += left_transposed(score_grad, stacked) * scale
        value_total[low:high, :] += left_transposed(probs.astype(bf16), grads)
        cos = cosine[start:high, :]
        sin = sine[start:high, :]
        for h in range(heads):
            first = query_grad[h * size : (h + 1) * size, :half]
            second = query_grad[h * size : (h + 1) * size, half:]
            query_out[start:high, h * width : h * width + half] = (
                first * cos + second * sin
            ).astype(bf16)
            query_out[start:high, h * width + half : (h + 1) * width] = (
                second * cos - first * sin
            ).astype(bf16)
    for r in range(count):
        here = slice(r * rows, (r + 1) * rows)
        query_there[here, :] = query_out[there(r), :]
        pair_there[here, :width] = key_total[there(r), :].astype(bf16)
        pair_there[here, width:] = value_total[there(r), :].astype(bf16)


def attend_backward(table, grads, queries, keys, values, cosine, sine, segments, heads, scale):
    parts = len(grads)
    length, width = keys.shape
    shapes = [
        jax.ShapeDtypeStruct((length, heads * width), bf16),
        jax.ShapeDtypeStruct((length, 2 * width), bf16),
    ]
    return pl.pallas_call(
        functools.partial(attend_backward_kernel, parts, heads, width, scale),
        out_shape=shapes,
        in_specs=[smem()] + [vmem()] * (parts + 7),
        out_specs=[vmem()] * 2,
        scratch_shapes=[
            pltpu.VMEM((length, heads * width), bf16),
            pltpu.VMEM((length, heads * width), bf16),
            pltpu.VMEM((length, width), f32),
            pltpu.VMEM((length, width), f32),
        ],
        compiler_params=pltpu.CompilerParams(vmem_limit_bytes=44 << 20),
        cost_estimate=brief(),
        name="attend_backward",
    )(
        table,
        *grads,
        queries,
        keys,
        values,
        cosine,
        sine,
        segments[:, None],
        segments[None, :],
    )


def rows_product_kernel(*refs):
    pieces, weight, out = refs[:-2], refs[-2], refs[-1]
    rows = pieces[0].shape[0]
    for p in range(0, len(pieces), 2):
        here = jnp.concatenate([pieces[p][...], pieces[p + 1][...]], axis=0)
        out[p * rows : (p + 2) * rows, :] = right_transposed(here, weight[...]).astype(out.dtype)


def rows_product(pieces, weight, kind):
    return pl.pallas_call(
        rows_product_kernel,
        out_shape=jax.ShapeDtypeStruct(
            (len(pieces) * pieces[0].shape[0], weight.shape[0]), kind
        ),
        in_specs=[vmem()] * (len(pieces) + 1),
        out_specs=vmem(),
        compiler_params=pltpu.CompilerParams(vmem_limit_bytes=32 << 20),
        cost_estimate=brief(),
        name="rows_product",
    )(*pieces, weight)


def latent_share_kernel(low, size, query_grads, pairs, weight, *refs):
    outs = refs[:-3]
    held, beside, sems = refs[-3:]
    rows = outs[0].shape[0]
    rank = weight.shape[0]
    here = pl.ds(low * rows, size)
    copies = [
        pltpu.make_async_copy(query_grads.at[here, :], held, sems.at[0]),
        pltpu.make_async_copy(pairs.at[here, :], beside, sems.at[1]),
    ]
    for copy in copies:
        copy.start()
    for copy in copies:
        copy.wait()
    for p in range(0, size // rows, 2):
        total = right_transposed(held[p * rows : (p + 2) * rows, :], weight[...])
        for k in range(2):
            outs[p + k][:, :rank] = total[k * rows : (k + 1) * rows].astype(bf16)
            outs[p + k][:, rank:] = beside[(p + k) * rows : (p + k + 1) * rows, :]


def latent_shares(clock, query_grads, pairs, weight, count):
    rows = query_grads.shape[0] // count
    rank, inner = weight.shape
    extra = pairs.shape[1]

    def share(low, high):
        size = (high - low) * rows
        return pl.pallas_call(
            functools.partial(latent_share_kernel, low, size),
            out_shape=[jax.ShapeDtypeStruct((rows, rank + extra), bf16)] * (high - low),
            in_specs=[any_space(), any_space(), vmem()],
            out_specs=[vmem()] * (high - low),
            scratch_shapes=[
                pltpu.VMEM((size, inner), bf16),
                pltpu.VMEM((size, extra), bf16),
                pltpu.SemaphoreType.DMA((2,)),
            ],
            compiler_params=pltpu.CompilerParams(vmem_limit_bytes=32 << 20),
            cost_estimate=brief(),
            name="latent_share",
        )(*clock(query_grads, pairs), weight)

    return share


def join_kernel(count, *refs):
    pieces, whole = refs[:count], refs[count]
    rows = pieces[0].shape[0]
    for r in range(count):
        whole[r * rows : (r + 1) * rows, :] = pieces[r][...]


def join(pieces):
    count = len(pieces)
    rows, columns = pieces[0].shape
    step = min(columns, 512)
    return pl.pallas_call(
        functools.partial(join_kernel, count),
        grid=(columns // step,),
        out_shape=jax.ShapeDtypeStruct((count * rows, columns), bf16),
        in_specs=[pl.BlockSpec((rows, step), lambda j: (0, j))] * count,
        out_specs=pl.BlockSpec((count * rows, step), lambda j: (0, j)),
        compiler_params=pltpu.CompilerParams(vmem_limit_bytes=17 << 20),
        cost_estimate=brief(),
        name="join",
    )(*pieces)


def any_space():
    return pl.BlockSpec(memory_space=pl.ANY)


def share_kernel(low, size, terms, transposed, *refs):
    lefts = refs[:terms]
    weights = refs[terms : 2 * terms]
    outs = refs[2 * terms : -terms - 1]
    held, sems = refs[-terms - 1 : -1], refs[-1]
    rows = outs[0].shape[0]
    copies = []
    for t in range(terms):
        copy = pltpu.make_async_copy(lefts[t].at[pl.ds(low * rows, size), :], held[t], sems.at[t])
        copy.start()
        copies.append(copy)
    for copy in copies:
        copy.wait()
    product = right_transposed if transposed else dot
    for p in range(size // (2 * rows)):
        here = pl.ds(2 * p * rows, 2 * rows)
        total = product(held[0][here, :], weights[0][...])
        for t in range(1, terms):
            total = total + product(held[t][here, :], weights[t][...])
        outs[2 * p][...] = total[:rows].astype(bf16)
        outs[2 * p + 1][...] = total[rows:].astype(bf16)


def shares(clock, lefts, weights, count, transposed):
    rows = lefts[0].shape[0] // count
    inner = lefts[0].shape[1]
    columns = weights[0].shape[0] if transposed else weights[0].shape[1]
    terms = len(lefts)

    def share(low, high):
        size = (high - low) * rows
        return pl.pallas_call(
            functools.partial(share_kernel, low, size, terms, transposed),
            out_shape=[jax.ShapeDtypeStruct((rows, columns), bf16)] * (high - low),
            in_specs=[any_space()] * terms + [vmem()] * terms,
            out_specs=[vmem()] * (high - low),
            scratch_shapes=[pltpu.VMEM((size, inner), bf16)] * terms
            + [pltpu.SemaphoreType.DMA((terms,))],
            compiler_params=pltpu.CompilerParams(vmem_limit_bytes=40 << 20),
            cost_estimate=brief(),
            name="share",
        )(*clock(*lefts, lefts[0])[:terms], *weights)

    return share


def feed_kernel(pairs, first, *refs):
    pieces = refs[: 2 * pairs]
    upper, gate_weight, up_weight = refs[2 * pairs : 2 * pairs + 3]
    rest = refs[2 * pairs + 3 :]
    outs, held, buffers, sems = rest[-8:-5], rest[-5], rest[-4:-1], rest[-1]
    rows = pieces[0].shape[0]

    def rows_of(p):
        return pl.ds((first + p) * 2 * rows, 2 * rows)

    loads = []
    for p in range(pairs):
        load = pltpu.make_async_copy(upper.at[rows_of(p), :], held.at[p], sems.at[3, p])
        load.start()
        loads.append(load)
    copies = []
    for p in range(pairs):
        here = jnp.concatenate([pieces[2 * p][...], pieces[2 * p + 1][...]], axis=0)
        gate = right_transposed(here, gate_weight[...])
        upward = right_transposed(here, up_weight[...])
        loads[p].wait()
        hidden_grad = held[p]
        sigmoid = jax.nn.sigmoid(gate)
        swish = gate * sigmoid
        results = (
            swish * upward,
            hidden_grad * upward * sigmoid * (1.0 + gate * (1.0 - sigmoid)),
            hidden_grad * swish,
        )
        for k, result in enumerate(results):
            buffers[k][p] = result.astype(bf16)
            copy = pltpu.make_async_copy(buffers[k].at[p], outs[k].at[rows_of(p), :], sems.at[k, p])
            copy.start()
            copies.append(copy)
    for copy in copies:
        copy.wait()


def feed(pieces, low, high, upper, gate_weight, up_weight, count, past):
    rows, dim = pieces[0].shape
    units = gate_weight.shape[0]
    pairs = (high - low) // 2
    operands = list(pieces[low:high]) + [upper, gate_weight, up_weight]
    specs = [vmem()] * (high - low) + [any_space()] + [vmem()] * 2
    aliases = {}
    if past is not None:
        aliases = {len(operands) + k: k for k in range(3)}
        operands += list(past)
        specs += [any_space()] * 3
    size = (high - low) * rows
    return pl.pallas_call(
        functools.partial(feed_kernel, pairs, low // 2),
        out_shape=[jax.ShapeDtypeStruct((count * rows, units), bf16)] * 3,
        in_specs=specs,
        out_specs=[any_space()] * 3,
        scratch_shapes=[pltpu.VMEM((pairs, 2 * rows, units), f32)]
        + [pltpu.VMEM((pairs, 2 * rows, units), bf16)] * 3
        + [pltpu.SemaphoreType.DMA((4, pairs))],
        input_output_aliases=aliases,
        compiler_params=pltpu.CompilerParams(vmem_limit_bytes=28 << 20),
        cost_estimate=brief(),
        name="feed",
    )(*operands)


def sum_kernel(*refs):
    total = refs[0][...].astype(f32)
    for ref in refs[1:-1]:
        total = total + ref[...].astype(f32)
    refs[-1][...] = total.astype(bf16)


def call(kernel, shapes, operands, name, scalars=0, limit=24, scratch=()):
    single = not isinstance(shapes, list)
    return pl.pallas_call(
        kernel,
        out_shape=shapes,
        in_specs=[smem()] * scalars + [vmem()] * (len(operands) - scalars),
        out_specs=vmem() if single else [vmem()] * len(shapes),
        scratch_shapes=list(scratch),
        compiler_params=pltpu.CompilerParams(vmem_limit_bytes=limit << 20),
        cost_estimate=brief(),
        name=name,
    )(*operands)


def shaped(shape, kind):
    return jax.ShapeDtypeStruct(shape, kind)


def add_rows(*values):
    return call(sum_kernel, shaped(values[0].shape, bf16), values, "add_rows")


def add_or_begin_kernel(inner, own, came, value, out):
    @pl.when(inner[0] == 1)
    def _():
        out[...] = (own[...].astype(f32) + came[...].astype(f32)).astype(bf16)

    @pl.when(inner[0] == 0)
    def _():
        out[...] = value[...]


def add_or_begin(inner, own, came, value):
    return call(
        add_or_begin_kernel,
        shaped(own.shape, bf16),
        [inner, own, came, value],
        "add_or_begin",
        scalars=1,
    )


def settle_kernel(at, *refs):
    inner, own, came = refs[:3]
    out, buffer, sem = refs[-3:]
    rows = own.shape[0]

    @pl.when(inner[0] == 1)
    def _():
        buffer[...] = own[...].astype(f32)

    @pl.when(inner[0] == 0)
    def _():
        buffer[...] = came[...].astype(f32)

    copy = pltpu.make_async_copy(buffer, out.at[pl.ds(at, rows), :], sem)
    copy.start()
    copy.wait()


def settle(inner, own, came, size, at, past):
    rows, columns = own.shape
    operands = [inner, own, came]
    specs = [smem(), vmem(), vmem()]
    aliases = {}
    if past is not None:
        aliases = {3: 0}
        operands.append(past)
        specs.append(any_space())
    return pl.pallas_call(
        functools.partial(settle_kernel, at),
        out_shape=shaped((size, columns), f32),
        in_specs=specs,
        out_specs=any_space(),
        scratch_shapes=[pltpu.VMEM((rows, columns), f32), pltpu.SemaphoreType.DMA],
        input_output_aliases=aliases,
        compiler_params=pltpu.CompilerParams(vmem_limit_bytes=24 << 20),
        cost_estimate=brief(),
        name="settle",
    )(*operands)


def product_kernel(left, right, *outs):
    total = left_transposed(left[...], right[...]).astype(bf16)
    rows = outs[0].shape[0]
    for k, out in enumerate(outs):
        out[...] = total[k * rows : (k + 1) * rows]


def weight_product(left, right, parts, step=512):
    tokens, units = left.shape
    columns = right.shape[1]
    step = min(step, columns)
    rows = units // parts
    return pl.pallas_call(
        product_kernel,
        grid=(columns // step,),
        out_shape=[shaped((rows, columns), bf16)] * parts,
        in_specs=[
            pl.BlockSpec((tokens, units), lambda j: (0, 0)),
            pl.BlockSpec((tokens, step), lambda j: (0, j)),
        ],
        out_specs=[pl.BlockSpec((rows, step), lambda j: (0, j))] * parts,
        compiler_params=pltpu.CompilerParams(vmem_limit_bytes=26 << 20),
        cost_estimate=brief(),
        name="weight_product",
    )(left, right)


def rotated(first, second, cosine, sine):
    return first * cosine - second * sine, second * cosine + first * sine


def enter_kernel(rank, width, x, gain, down, latent_gain, key, value, cosine, sine, *outs):
    normed, latent, packed = outs
    half = width // 2
    rows = x[...].astype(f32)
    low = (rows * inverse_rms(rows) * gain[...]).astype(bf16)
    normed[...] = low
    inner = dot(low, down[...])
    latent[...] = inner
    packed[:, :rank] = (inner * inverse_rms(inner) * latent_gain[...]).astype(bf16)
    keys = dot(low, key[...])
    first, second = rotated(keys[:, :half], keys[:, half:], cosine[...], sine[...])
    packed[:, rank : rank + half] = first.astype(bf16)
    packed[:, rank + half : rank + width] = second.astype(bf16)
    packed[:, rank + width :] = dot(low, value[...]).astype(bf16)


def enter(x, gain, down, latent_gain, key, value, cosine, sine):
    rows, dim = x.shape
    rank, width = down.shape[1], key.shape[1]
    return call(
        functools.partial(enter_kernel, rank, width),
        [shaped((rows, dim), bf16), shaped((rows, rank), f32), shaped((rows, rank + 2 * width), bf16)],
        [x, gain[None], down, latent_gain[None], key, value, cosine, sine],
        "enter",
    )


def summed(parts):
    total = parts[0][...].astype(f32)
    for part in parts[1:]:
        total = total + part[...].astype(f32)
    return total


def middle_kernel(x, gain, *refs):
    parts, (middle, normed) = refs[:-2], refs[-2:]
    total = x[...].astype(f32) + summed(parts)
    middle[...] = total
    normed[...] = (total * inverse_rms(total) * gain[...]).astype(bf16)


def middle_rows(x, gain, parts):
    shape = x.shape
    return call(
        middle_kernel,
        [shaped(shape, f32), shaped(shape, bf16)],
        [x, gain[None], *parts],
        "middle_rows",
    )


def lower_norm(value, gain, upper):
    scale = inverse_rms(value)
    scaled = upper * gain
    lower = scale * scaled - value * (scale * scale * scale) * jnp.mean(
        scaled * value, axis=-1, keepdims=True
    )
    return lower, jnp.sum(upper * value * scale, axis=0, keepdims=True)


def middle_back_kernel(middle, gain, cotangent, *refs):
    parts, (total, low, gain_part) = refs[:-3], refs[-3:]
    lower, gain_part[...] = lower_norm(middle[...], gain[...], summed(parts))
    result = cotangent[...].astype(f32) + lower
    total[...] = result
    low[...] = result.astype(bf16)


def middle_back(middle, gain, cotangent, parts):
    shape = middle.shape
    return call(
        middle_back_kernel,
        [shaped(shape, f32), shaped(shape, bf16), shaped((1, shape[1]), f32)],
        [middle, gain[None], cotangent, *parts],
        "middle_back",
    )


def latent_back_kernel(latent, gain, cosine, sine, *refs):
    parts, (packed, gain_part) = refs[:-2], refs[-2:]
    rank = latent.shape[1]
    total = summed(parts)
    lower, gain_part[...] = lower_norm(latent[...], gain[...], total[:, :rank])
    width = (total.shape[1] - rank) // 2
    half = width // 2
    packed[:, :rank] = lower.astype(bf16)
    first, second = rotated(
        total[:, rank : rank + half], total[:, rank + half : rank + width], cosine[...], -sine[...]
    )
    packed[:, rank : rank + half] = first.astype(bf16)
    packed[:, rank + half : rank + width] = second.astype(bf16)
    packed[:, rank + width :] = total[:, rank + width :].astype(bf16)


def latent_back(latent, gain, cosine, sine, parts):
    shape = parts[0].shape
    return call(
        latent_back_kernel,
        [shaped(shape, bf16), shaped((1, latent.shape[1]), f32)],
        [latent, gain[None], cosine, sine, *parts],
        "latent_back",
    )


def leave_kernel(packed, down, key, value, x, gain, upper, result, gain_part):
    rank, width = down.shape[1], key.shape[1]
    total = right_transposed(packed[:, :rank], down[...])
    total = total + right_transposed(packed[:, rank : rank + width], key[...])
    total = total + right_transposed(packed[:, rank + width :], value[...])
    lower, gain_part[...] = lower_norm(x[...].astype(f32), gain[...], total)
    result[...] = upper[...] + lower


def leave(packed, down, key, value, x, gain, upper):
    return call(
        leave_kernel,
        [shaped(x.shape, f32), shaped((1, x.shape[1]), f32)],
        [packed, down, key, value, x, gain[None], upper],
        "leave",
    )


def shared_kernel(count, table, normed, grads, *outs):
    rows = outs[0].shape[0]
    for r in range(count):
        there = pl.ds(pl.multiple_of(table[r] * rows, rows), rows)
        outs[r][...] = left_transposed(normed[:, there], grads[...]).astype(bf16)


def shared_shares(table, normed, grads):
    count = table.shape[0]
    rows = normed.shape[1] // count
    columns = grads.shape[1]
    return list(
        pl.pallas_call(
            functools.partial(shared_kernel, count),
            out_shape=[jax.ShapeDtypeStruct((rows, columns), bf16)] * count,
            in_specs=[smem(), vmem(), vmem()],
            out_specs=[vmem()] * count,
            compiler_params=pltpu.CompilerParams(vmem_limit_bytes=40 << 20),
            cost_estimate=brief(),
            name="shared_shares",
        )(table, normed, grads)
    )


def unpack_kernel(count, parts, table, *refs):
    pieces = refs[:count]
    outs = refs[count : count + len(parts)]
    buffers = refs[count + len(parts) : -1]
    sems = refs[-1]
    rows = pieces[0].shape[0]
    flying = []
    for r in range(count):
        slot = r % 2
        if r >= 2:
            for copy in flying[r - 2]:
                copy.wait()
        there = pl.ds(pl.multiple_of(table[r] * rows, rows), rows)
        copies = []
        for k, (low, high) in enumerate(parts):
            buffers[k][slot] = pieces[r][:, low:high].astype(f32)
            copy = pltpu.make_async_copy(
                buffers[k].at[slot], outs[k].at[there, :], sems.at[k, slot]
            )
            copy.start()
            copies.append(copy)
        flying.append(copies)
    for copies in flying[-2:]:
        for copy in copies:
            copy.wait()


def unpack(table, pieces, parts):
    count = len(pieces)
    rows = pieces[0].shape[0]
    return pl.pallas_call(
        functools.partial(unpack_kernel, count, parts),
        out_shape=[jax.ShapeDtypeStruct((count * rows, high - low), f32) for low, high in parts],
        in_specs=[smem()] + [vmem()] * count,
        out_specs=[any_space()] * len(parts),
        scratch_shapes=[pltpu.VMEM((2, rows, high - low), f32) for low, high in parts]
        + [pltpu.SemaphoreType.DMA((len(parts), 2))],
        compiler_params=pltpu.CompilerParams(vmem_limit_bytes=40 << 20),
        cost_estimate=brief(),
        name="unpack",
    )(table, *pieces)


def body(
    packs,
    group,
    block_input,
    segment_ids,
    positions,
    attention_gain,
    query_down,
    query_gain,
    query_up,
    key_proj,
    value_proj,
    out_proj,
    feed_gain,
    gate_weight,
    up_weight,
    down_weight,
    out_grad,
):
    plane = Plane(group)
    line = Line(packs)
    rows = block_input.shape[1]
    segments = segment_ids[0]
    places = positions[0]
    width = key_proj.shape[1]
    rank = query_down.shape[1]
    heads = query_up.shape[1] // width
    scale = 1.0 / math.sqrt(width)
    first_row = plane.me * rows

    gate_rows, up_rows = gate_weight.T, up_weight.T
    clock = Clock()
    belt = Belt(line, clock)
    fast = plane.fast
    move = plane.move
    hop_a, hop_b, hop_c = (plane.hop_a, plane.hop_b, plane.hop_c) if fast else (None,) * 3
    cotangent_rows = out_grad[0]

    x = block_input[0]
    if fast:
        cot_a = move(cotangent_rows, hop_a)
        cot_o = move(cotangent_rows, hop_c)
    own_places = lax.dynamic_slice_in_dim(places, first_row, rows, 0)
    own_cosine, own_sine = rotation(own_places, width)
    normed_rows, latent, packed = enter(
        x, attention_gain, query_down, query_gain, key_proj, value_proj, own_cosine, own_sine
    )
    cosine, sine = rotation(places, width)
    if fast:
        packed = clock(packed)
        a, b, s_o = move(packed, hop_a), move(packed, hop_b), move(packed, hop_c)
        cosine, sine = clock(cosine, sine)
        a, cot_a = clock(a, cot_a)
        c, a_o = move(a, hop_b), move(a, hop_c)
        cot_ao = move(cot_a, hop_c)
        b = clock(b)
        b_o = move(b, hop_c)
        c = clock(c)
        c_o = move(c, hop_c)
        cotangent_rows, cot_a = clock(cotangent_rows, cot_a)
        cot_b = move(cotangent_rows, hop_b)
        cot_c = move(cot_a, hop_b)
        pieces = [packed, s_o, a, a_o, b, b_o, c, c_o]
    else:
        pieces = plane.gather(packed)
    queries, keys, values, mixed, mixed_there = attend_forward(
        plane.table, pieces, query_up, cosine, sine, segments, heads, width, scale
    )

    def first_part(share):
        c, c_send = clock(*share(6, 8))
        c_came = move(c_send, hop_c)
        return c, c_came

    def second_part(share, c, c_came):
        c = clock(add_rows(c, clock(c_came)))
        c_in = move(c, hop_b)
        a, a_send, b, b_send = clock(*share(2, 6))
        b_came, a_came = move(b_send, hop_c), move(a_send, hop_c)
        b = clock(add_rows(b, clock(b_came)))
        b_in = move(b, hop_b)
        own, own_send = clock(*share(0, 2))
        own_came = move(own_send, hop_c)
        return c_in, a, a_came, b_in, own, own_came

    def third_part(c_in, a, a_came, b_in, own, own_came):
        c_in, a_came = clock(c_in, a_came)
        a = clock(add_rows(a, a_came, c_in))
        a_in = move(a, hop_a)
        return [own, own_came, b_in, a_in]

    share = shares(clock, [mixed_there], [out_proj], group, False)
    if fast:
        state = second_part(share, *first_part(share))
        cot_b, cot_c = clock(cot_b, cot_c)
        cot_bo, cot_co = move(cot_b, hop_c), move(cot_c, hop_c)
        parts = third_part(*state)
        cot_bo, cot_co = clock(cot_bo, cot_co)
        cot_pieces = [cotangent_rows, cot_o, cot_a, cot_ao, cot_b, cot_bo, cot_c, cot_co]
        hidden_grad = clock(rows_product(cot_pieces, down_weight, f32))
        parts = clock(*parts)
    else:
        cot_pieces = plane.gather(cotangent_rows)
        hidden_grad = rows_product(cot_pieces, down_weight, f32)
        parts = [plane.scatter(share(0, group))]
    middle, normed_mid_rows = middle_rows(x, feed_gain, parts)

    def feed_group(pieces, low, high, past):
        return clock(*feed(pieces, low, high, hidden_grad, gate_rows, up_rows, group, past))

    if fast:
        normed_mid_rows = clock(normed_mid_rows)
        a, b = move(normed_mid_rows, hop_a), move(normed_mid_rows, hop_b)
        s_o = move(normed_mid_rows, hop_c)
        cot_pieces[1] = clock(cot_pieces[1])
        cotangent = clock(join(cot_pieces))
        s_o = clock(s_o)
        mid_pieces = [normed_mid_rows, s_o]
        past = feed_group(mid_pieces, 0, 2, None)
        a, b = clock(a, b)
        c = move(a, hop_b)
        a_o, b_o = move(a, hop_c), move(b, hop_c)
        a_o, b_o = clock(a_o, b_o)
        mid_pieces += [a, a_o, b, b_o]
        past = feed_group(mid_pieces, 2, 6, past)
        c = clock(c)
        c_o = clock(move(c, hop_c))
        mid_pieces += [c, c_o]
        past = feed_group(mid_pieces, 6, 8, past)
    else:
        cotangent = join(cot_pieces)
        mid_pieces = plane.gather(normed_mid_rows)
        past = feed_group(mid_pieces, 0, group, None)
    hidden, gate_grad, upward_grad = past
    units = hidden.shape[1]
    dim = x.shape[1]

    share = shares(clock, [gate_grad, upward_grad], [gate_rows, up_rows], group, False)
    if fast:
        c, c_came = first_part(share)
        down_one, down_two = clock(*weight_product(clock(hidden), cotangent, 2))
        down_one, down_two = belt.begin(down_one), belt.begin(down_two)
        state = second_part(share, c, c_came)
        normed_mid = clock(join(mid_pieces))
        parts = third_part(*state)
        gate_one, gate_two = clock(*weight_product(clock(gate_grad), normed_mid, 2))
        parts = clock(*parts)
    else:
        normed_mid = join(mid_pieces)
        parts = [plane.scatter(share(0, group))]
    middle_grad, attention_grad, feed_gain_part = middle_back(
        middle, feed_gain, cotangent_rows, parts
    )
    if fast:
        attention_grad = clock(attention_grad)
        a, b = move(attention_grad, hop_a), move(attention_grad, hop_b)
        s_o = move(attention_grad, hop_c)
        up_one, up_two = clock(*weight_product(clock(upward_grad), normed_mid, 2))
        outer = [clock(rows_product([attention_grad, clock(s_o)], out_proj, bf16))]
        belt.cross(down_one)
        a, b = clock(a, b)
        c = move(a, hop_b)
        a_o, b_o = move(a, hop_c), move(b, hop_c)
        a_o, b_o = clock(a_o, b_o)
        outer.append(clock(rows_product([a, a_o, b, b_o], out_proj, bf16)))
        c = clock(c)
        c_o = clock(move(c, hop_c))
        outer.append(rows_product([c, c_o], out_proj, bf16))
        grad_pieces = [attention_grad, s_o, a, a_o, b, b_o, c, c_o]
    else:
        grad_pieces = plane.gather(attention_grad)
        outer = [rows_product(grad_pieces, out_proj, bf16)]

    query_pre_grad, pair_grads = clock(
        *attend_backward(
            plane.table, outer, queries, keys, values, cosine, sine, segments, heads, scale
        )
    )

    def out_proj_sum(number):
        return weight_product(clock(mixed_there), join(grad_pieces), number)

    def query_up_sum():
        return weight_product(join(pieces)[:, :rank], clock(query_pre_grad), 1)[0]

    share = latent_shares(clock, query_pre_grad, pair_grads, query_up, group)
    if fast:
        c, c_came = first_part(share)
        state = second_part(share, c, c_came)
        gate_one = belt.back(down_one, gate_one)
        belt.cross(down_two)
        parts = third_part(*state)
        out_one, out_two = clock(*out_proj_sum(2))
        parts = clock(*parts)
    else:
        parts = [plane.scatter(share(0, group))]

    packed_grad, query_gain_part = clock(
        *latent_back(latent, query_gain, own_cosine, own_sine, parts)
    )

    shared_pieces = shared_shares(plane.table, normed_rows, packed_grad)
    feed_share = shares(clock, [hidden], [down_weight], group, False)
    if fast:
        shared_pieces = clock(*shared_pieces)

        def share(low, high):
            return shared_pieces[low:high]

        state = second_part(share, *first_part(share))
        gate_two = belt.back(down_two, gate_two)
        down_gradient = belt.end(down_one, units)
        belt.cross(gate_one)
        parts = third_part(*state)
        query_sum = clock(query_up_sum())
        input_gradient, attention_gain_part = clock(
            *leave(
                clock(packed_grad),
                query_down,
                key_proj,
                value_proj,
                x,
                attention_gain,
                middle_grad,
            )
        )
        parts = clock(*parts)
        shared = belt.begin(clock(add_rows(*parts)))
        up_one = belt.back(gate_one, up_one)
        down_gradient = belt.end(down_two, units, units // 2, down_gradient)
        belt.cross(gate_two)
        belt.cross(shared)
        state = second_part(feed_share, *first_part(feed_share))
        parts = third_part(*state)
        up_two = belt.back(gate_two, up_two)
        gate_gradient = belt.end(gate_one, units)
        belt.cross(up_one)
        belt.back(shared)
        parts = clock(*parts)
        out_one = belt.begin(out_one)
        block_output = clock(add_rows(middle, *parts))
        gains = jnp.concatenate([attention_gain_part, query_gain_part, feed_gain_part], axis=1)
        gains = line.total(plane.total(gains), lambda left, right: left + right)[0]
        belt.back(up_one)
        gate_gradient = belt.end(gate_two, units, units // 2, gate_gradient)
        belt.cross(up_two)
        own = clock(jnp.where(belt.inner[0] == 1, shared["own"], clock(shared["came"])))
        a, b, s_o = move(own, hop_a), move(own, hop_b), move(own, hop_c)
        out_two = belt.begin(out_two)
        query_sum = belt.begin(query_sum)
        belt.cross(out_one)
        a, b = clock(a, b)
        c, a_o, b_o = move(a, hop_b), move(a, hop_c), move(b, hop_c)
        belt.back(up_two)
        up_gradient = belt.end(up_one, units)
        belt.cross(out_two)
        c = clock(c)
        c_o = clock(move(c, hop_c))
        belt.back(out_one)
        belt.cross(query_sum)
        up_gradient = belt.end(up_two, units, units // 2, up_gradient)
        belt.back(out_two)
        size = heads * width
        proj_gradient = belt.end(out_one, size)
        belt.back(query_sum)
        proj_gradient = belt.end(out_two, size, size // 2, proj_gradient)
        query_up_gradient = belt.end(query_sum, rank)
        shared_all = [own, s_o, a, a_o, b, b_o, c, c_o]
    else:
        input_gradient, attention_gain_part = leave(
            packed_grad, query_down, key_proj, value_proj, x, attention_gain, middle_grad
        )
        block_output = add_rows(middle, plane.scatter(feed_share(0, group)))
        gains = jnp.concatenate([attention_gain_part, query_gain_part, feed_gain_part], axis=1)
        gains = line.total(plane.total(gains), lambda left, right: left + right)[0]
        shared = line.total(plane.scatter(list(shared_pieces)).astype(bf16))
        shared_all = plane.gather(shared)
        down_gradient, gate_gradient, up_gradient, proj_gradient, query_up_gradient = (
            line.total(value).astype(f32)
            for value in (
                weight_product(hidden, cotangent, 1)[0],
                weight_product(gate_grad, normed_mid, 1)[0],
                weight_product(upward_grad, normed_mid, 1)[0],
                out_proj_sum(1)[0],
                query_up_sum(),
            )
        )
    query_down_gradient, key_proj_gradient, value_proj_gradient = unpack(
        plane.table,
        shared_all,
        ((0, rank), (rank, rank + width), (rank + width, rank + 2 * width)),
    )
    return (
        block_output[None],
        input_gradient[None],
        gains[:dim],
        query_down_gradient,
        gains[dim : dim + rank],
        query_up_gradient,
        key_proj_gradient,
        value_proj_gradient,
        proj_gradient,
        gains[dim + rank :],
        gate_gradient.T,
        up_gradient.T,
        down_gradient,
    )


def solution(mesh):
    in_specs = (
        P("tok", "head", None),
        P("tok", None),
        P("tok", None),
        P(),
        P(),
        P(),
        P(None, "head"),
        P(),
        P(),
        P("head", None),
        P(),
        P(None, "head"),
        P(None, "head"),
        P("head", None),
        P("tok", "head", None),
    )
    out_specs = (
        P("tok", "head", None),
        P("tok", "head", None),
        P(),
        P(),
        P(),
        P(None, "head"),
        P(),
        P(),
        P("head", None),
        P(),
        P(None, "head"),
        P(None, "head"),
        P("head", None),
    )
    sizes = dict(mesh.shape)
    return jax.shard_map(
        functools.partial(body, sizes["tok"], sizes["head"]),
        mesh=mesh,
        in_specs=in_specs,
        out_specs=out_specs,
        check_vma=False,
    )
```

```python
import functools
import math

import jax
import jax.numpy as jnp
from jax import lax
from jax.experimental import pallas as pl
from jax.experimental.pallas import tpu as pltpu
from jax.sharding import PartitionSpec as P

norm_epsilon = 1e-05
rope_base = 10000.0
first_document = 1024
bf16 = jnp.bfloat16
f32 = jnp.float32


def inverse_rms(value):
    return lax.rsqrt(jnp.mean(value * value, axis=-1, keepdims=True) + norm_epsilon)


def norm_backward(value, gain, upper):
    scale = inverse_rms(value)
    scaled = upper * gain
    lower = scale * scaled - value * (scale * scale * scale) * jnp.mean(
        scaled * value, axis=-1, keepdims=True
    )
    return (lower, jnp.sum(upper * value * scale, axis=0))


def rotation(places, head_width):
    half = head_width // 2
    steps = jnp.arange(half).astype(f32) * (2.0 / head_width)
    inverse = jnp.exp(steps * -math.log(rope_base))
    angles = places.astype(f32)[:, None] * inverse[None, :]
    return (jnp.cos(angles), jnp.sin(angles))


def rotate(value, cosine, sine):
    half = value.shape[-1] // 2
    first = value[..., :half]
    second = value[..., half:]
    return jnp.concatenate(
        [first * cosine - second * sine, second * cosine + first * sine], axis=-1
    )


def dot(left, right):
    return jnp.dot(left, right, preferred_element_type=f32)


def right_transposed(left, right):
    return lax.dot_general(left, right, (((1,), (1,)), ((), ())), preferred_element_type=f32)


def left_transposed(left, right):
    return lax.dot_general(left, right, (((0,), (0,)), ((), ())), preferred_element_type=f32)


def add_low(left, right):
    return (left.astype(f32) + right.astype(f32)).astype(bf16)


class Clock:
    def __init__(self):
        self.last = ()

    def all(self, *values):
        held = lax.optimization_barrier(values + self.last)
        self.last = (held[0],)
        return held[: len(values)]

    def __call__(self, *values):
        held = self.all(*values)
        return held[0] if len(values) == 1 else held


class Plane:
    def __init__(self, size):
        self.size = size
        self.fast = size == 8 and lax.axis_size("tok") == 4
        self.me = lax.axis_index("head")
        if self.fast:
            even = [index % 2 == 0 for index in range(size)]
            self.hop_a = [(i, i ^ (2 if even[i] else 4)) for i in range(size)]
            self.hop_b = [(i, i ^ (4 if even[i] else 2)) for i in range(size)]
            self.hop_c = [(i, i ^ 1) for i in range(size)]
            mask_a = jnp.where(self.me % 2 == 0, 2, 4)
            other = self.me ^ 1
            order = [
                self.me,
                other,
                self.me ^ mask_a,
                other ^ (6 - mask_a),
                self.me ^ (6 - mask_a),
                other ^ mask_a,
                self.me ^ 6,
                other ^ 6,
            ]
            self.table = jnp.stack(order).astype(jnp.int32)
            self.groups = [(0, 2), (2, 6), (6, 8)]
        else:
            self.table = jnp.arange(size, dtype=jnp.int32)
            self.groups = [(0, size)]

    def move(self, value, hop):
        return lax.ppermute(value, "head", hop)

    def gather(self, rows):
        whole = lax.all_gather(rows, "head", axis=0, tiled=True)
        return list(jnp.split(whole, self.size, axis=0))

    def scatter(self, pieces):
        whole = jnp.concatenate(pieces, axis=0)
        return lax.psum_scatter(whole, "head", scatter_dimension=0, tiled=True).astype(f32)

    def total(self, value):
        if not self.fast:
            return lax.psum(value, "head")
        for bit in (1, 2, 4):
            value = value + self.move(value, [(i, i ^ bit) for i in range(8)])
        return value


class Line:
    def __init__(self, size):
        self.size = size
        self.me = lax.axis_index("tok")
        half = size // 2
        self.stages = [([(k, k + 1), (size - 1 - k, size - 2 - k)], None) for k in range(half - 1)]
        self.stages.append(([(half - 1, half), (half, half - 1)], None))
        for k in reversed(range(half - 1)):
            self.stages.append(([(k + 1, k), (size - 2 - k, size - 1 - k)], k))

    def start(self, stage, value):
        return lax.ppermute(value, "tok", self.stages[stage][0])

    def finish(self, stage, value, came, plus=add_low):
        outward = self.stages[stage][1]
        if outward is None:
            return plus(value, came)
        mine = (self.me == outward) | (self.me == self.size - 1 - outward)
        return jnp.where(mine, came, value)

    def total(self, value, plus=add_low):
        for stage in range(len(self.stages)):
            value = self.finish(stage, value, self.start(stage, value), plus)
        return value


class Belt:
    inward = [(0, 1), (3, 2)]
    middle = [(1, 2), (2, 1)]
    outward = [(1, 0), (2, 3)]

    def __init__(self, line, clock):
        self.clock = clock
        self.inner = jnp.where((line.me == 1) | (line.me == 2), 1, 0).astype(jnp.int32).reshape(1)

    def move(self, value, pairs):
        return lax.ppermute(value, "tok", pairs)

    def begin(self, value):
        value = self.clock(value)
        return {"own": value, "came": self.move(value, self.inward)}

    def cross(self, item):
        item["came"] = self.clock(item["came"])
        item["own"] = self.clock(add_rows(item["own"], item["came"]))
        item["came"] = self.move(item["own"], self.middle)

    def back(self, item, value=None):
        item["came"] = self.clock(item["came"])
        if value is None:
            item["own"] = self.clock(add_rows(item["own"], item["came"]))
            item["came"] = self.move(item["own"], self.outward)
            return None
        both = self.clock(add_or_begin(self.inner, item["own"], item["came"], value))
        came = self.move(both, self.inward + self.outward)
        item["own"], item["came"] = both, came
        return {"own": value, "came": came}

    def land(self, item):
        item["came"] = self.clock(item["came"])

    def end(self, item, size, at=0, past=None, low=0, high=None):
        return settle(self.inner, item["own"], item["came"], size, at, past, low, high)


def query_blocks(length):
    first = min(length, max(first_document, length // 2))
    block = 256
    return [
        (start, min(block, length - start), 0 if start < first else first)
        for start in range(0, length, block)
    ]


def allowed(seg_column, seg_row, start, rows, low, high):
    query_order = start + lax.broadcasted_iota(jnp.int32, (rows, high - low), 0)
    key_order = low + lax.broadcasted_iota(jnp.int32, (rows, high - low), 1)
    same = seg_column[start : start + rows, :] == seg_row[:, low:high]
    return (key_order <= query_order) & same


def weights_of(stacked, keys, permit, heads, scale):
    scores = right_transposed(stacked, keys) * scale
    scores = jnp.where(jnp.concatenate([permit] * heads, axis=0), scores, -1e30)
    top = jnp.max(scores, axis=-1, keepdims=True)
    weights = jnp.exp(scores - top)
    return weights, jnp.sum(weights, axis=-1, keepdims=True)


def stack_heads(ref, start, rows, heads, width):
    return jnp.concatenate(
        [ref[start : start + rows, h * width : (h + 1) * width] for h in range(heads)], axis=0
    )


def attend_forward_kernel(count, heads, width, rank, scale, *refs):
    table = refs[0]
    pieces = refs[1 : 1 + count]
    weight, cosine, sine, seg_column, seg_row = refs[1 + count : 6 + count]
    latents, queries, keys, values, mixed_there, mixed = refs[6 + count :]
    length = queries.shape[0]
    rows = length // count
    half = width // 2
    for r in range(count):
        there = pl.ds(pl.multiple_of(table[r] * rows, rows), rows)
        latents[there, :] = pieces[r][:, :rank]
        keys[there, :] = pieces[r][:, rank : rank + width]
        values[there, :] = pieces[r][:, rank + width :]
        flat = dot(pieces[r][:, :rank], weight[...])
        cos = cosine[there, :]
        sin = sine[there, :]
        for h in range(heads):
            first = flat[:, h * width : h * width + half]
            second = flat[:, h * width + half : (h + 1) * width]
            queries[there, h * width : h * width + half] = (first * cos - second * sin).astype(bf16)
            queries[there, h * width + half : (h + 1) * width] = (
                second * cos + first * sin
            ).astype(bf16)
    for start, size, low in query_blocks(length):
        high = start + size
        stacked = stack_heads(queries, start, size, heads, width)
        permit = allowed(seg_column, seg_row, start, size, low, high)
        weights, total = weights_of(stacked, keys[low:high, :], permit, heads, scale)
        probs = (weights / total).astype(bf16)
        result = dot(probs, values[low:high, :]).astype(bf16)
        for h in range(heads):
            mixed[start:high, h * width : (h + 1) * width] = result[h * size : (h + 1) * size]
    for r in range(count):
        there = pl.ds(pl.multiple_of(table[r] * rows, rows), rows)
        mixed_there[r * rows : (r + 1) * rows, :] = mixed[there, :]


def brief():
    return pl.CostEstimate(flops=1024, bytes_accessed=1024, transcendentals=0)


def vmem():
    return pl.BlockSpec(memory_space=pltpu.VMEM)


def smem():
    return pl.BlockSpec(memory_space=pltpu.SMEM)


def attend_forward(table, pieces, weight, cosine, sine, segments, heads, width, scale):
    count = len(pieces)
    length = cosine.shape[0]
    rank = weight.shape[0]
    shapes = [
        jax.ShapeDtypeStruct((length, rank), bf16),
        jax.ShapeDtypeStruct((length, heads * width), bf16),
        jax.ShapeDtypeStruct((length, width), bf16),
        jax.ShapeDtypeStruct((length, width), bf16),
        jax.ShapeDtypeStruct((length, heads * width), bf16),
    ]
    return pl.pallas_call(
        functools.partial(attend_forward_kernel, count, heads, width, rank, scale),
        out_shape=shapes,
        in_specs=[smem()] + [vmem()] * (count + 5),
        out_specs=[vmem()] * 5,
        scratch_shapes=[pltpu.VMEM((length, heads * width), bf16)],
        compiler_params=pltpu.CompilerParams(vmem_limit_bytes=48 << 20),
        cost_estimate=brief(),
        name="attend_forward",
    )(table, *pieces, weight, cosine, sine, segments[:, None], segments[None, :])


def attend_backward_kernel(parts, heads, width, scale, *refs):
    table = refs[0]
    grads_in = refs[1 : 1 + parts]
    queries, keys, values, cosine, sine, seg_column, seg_row = refs[1 + parts : 8 + parts]
    query_out, pair_out, outer, key_total, value_total = refs[8 + parts :]
    length = queries.shape[0]
    count = table.shape[0]
    rows = length // count
    half = width // 2

    def there(r):
        return pl.ds(pl.multiple_of(table[r] * rows, rows), rows)

    r = 0
    for part in grads_in:
        for k in range(part.shape[0] // rows):
            outer[there(r), :] = part[k * rows : (k + 1) * rows, :]
            r += 1
    key_total[...] = jnp.zeros_like(key_total)
    value_total[...] = jnp.zeros_like(value_total)
    for start, size, low in query_blocks(length):
        high = start + size
        stacked = stack_heads(queries, start, size, heads, width)
        grads = stack_heads(outer, start, size, heads, width)
        permit = allowed(seg_column, seg_row, start, size, low, high)
        weights, total = weights_of(stacked, keys[low:high, :], permit, heads, scale)
        probs = weights / total
        prob_grad = right_transposed(grads, values[low:high, :])
        centre = jnp.sum(probs * prob_grad, axis=-1, keepdims=True)
        score_grad = (probs * (prob_grad - centre)).astype(bf16)
        query_grad = dot(score_grad, keys[low:high, :]) * scale
        key_total[low:high, :] += left_transposed(score_grad, stacked) * scale
        value_total[low:high, :] += left_transposed(probs.astype(bf16), grads)
        cos = cosine[start:high, :]
        sin = sine[start:high, :]
        for h in range(heads):
            first = query_grad[h * size : (h + 1) * size, :half]
            second = query_grad[h * size : (h + 1) * size, half:]
            query_out[start:high, h * width : h * width + half] = (
                first * cos + second * sin
            ).astype(bf16)
            query_out[start:high, h * width + half : (h + 1) * width] = (
                second * cos - first * sin
            ).astype(bf16)
    pair_out[:, :width] = key_total[...].astype(bf16)
    pair_out[:, width:] = value_total[...].astype(bf16)


def attend_backward(table, grads, queries, keys, values, cosine, sine, segments, heads, scale):
    parts = len(grads)
    length, width = keys.shape
    shapes = [
        jax.ShapeDtypeStruct((length, heads * width), bf16),
        jax.ShapeDtypeStruct((length, 2 * width), bf16),
    ]
    return pl.pallas_call(
        functools.partial(attend_backward_kernel, parts, heads, width, scale),
        out_shape=shapes,
        in_specs=[smem()] + [vmem()] * (parts + 7),
        out_specs=[vmem()] * 2,
        scratch_shapes=[
            pltpu.VMEM((length, heads * width), bf16),
            pltpu.VMEM((length, width), f32),
            pltpu.VMEM((length, width), f32),
        ],
        compiler_params=pltpu.CompilerParams(vmem_limit_bytes=44 << 20),
        cost_estimate=brief(),
        name="attend_backward",
    )(
        table,
        *grads,
        queries,
        keys,
        values,
        cosine,
        sine,
        segments[:, None],
        segments[None, :],
    )


def rows_product_kernel(*refs):
    pieces, weight, out = refs[:-2], refs[-2], refs[-1]
    rows = pieces[0].shape[0]
    for p in range(0, len(pieces), 2):
        here = jnp.concatenate([pieces[p][...], pieces[p + 1][...]], axis=0)
        out[p * rows : (p + 2) * rows, :] = right_transposed(here, weight[...]).astype(out.dtype)


def rows_product(pieces, weight, kind):
    return pl.pallas_call(
        rows_product_kernel,
        out_shape=jax.ShapeDtypeStruct(
            (len(pieces) * pieces[0].shape[0], weight.shape[0]), kind
        ),
        in_specs=[vmem()] * (len(pieces) + 1),
        out_specs=vmem(),
        compiler_params=pltpu.CompilerParams(vmem_limit_bytes=36 << 20),
        cost_estimate=brief(),
        name="rows_product",
    )(*pieces, weight)


def latent_share_kernel(low, size, table, query_grads, pairs, weight, *refs):
    outs = refs[:-3]
    held, beside, sems = refs[-3:]
    rows = outs[0].shape[0]
    rank = weight.shape[0]
    copies = []
    for k in range(size // rows):
        there = pl.ds(pl.multiple_of(table[low + k] * rows, rows), rows)
        here = pl.ds(k * rows, rows)
        copies += [
            pltpu.make_async_copy(query_grads.at[there, :], held.at[here, :], sems.at[0, k]),
            pltpu.make_async_copy(pairs.at[there, :], beside.at[here, :], sems.at[1, k]),
        ]
    for copy in copies:
        copy.start()
    for copy in copies:
        copy.wait()
    for p in range(0, size // rows, 2):
        total = right_transposed(held[p * rows : (p + 2) * rows, :], weight[...])
        for k in range(2):
            outs[p + k][:, :rank] = total[k * rows : (k + 1) * rows].astype(bf16)
            outs[p + k][:, rank:] = beside[(p + k) * rows : (p + k + 1) * rows, :]


def latent_shares(table, query_grads, pairs, weight):
    count = table.shape[0]
    rows = query_grads.shape[0] // count
    rank, inner = weight.shape
    extra = pairs.shape[1]

    def share(clock, low, high):
        size = (high - low) * rows
        return pl.pallas_call(
            functools.partial(latent_share_kernel, low, size),
            out_shape=[jax.ShapeDtypeStruct((rows, rank + extra), bf16)] * (high - low),
            in_specs=[smem(), any_space(), any_space(), vmem()],
            out_specs=[vmem()] * (high - low),
            scratch_shapes=[
                pltpu.VMEM((size, inner), bf16),
                pltpu.VMEM((size, extra), bf16),
                pltpu.SemaphoreType.DMA((2, high - low)),
            ],
            compiler_params=pltpu.CompilerParams(vmem_limit_bytes=36 << 20),
            cost_estimate=brief(),
            name="latent_share",
        )(table, *clock(query_grads, pairs), weight)

    return share


def join_kernel(count, *refs):
    pieces, whole = refs[:count], refs[count]
    rows = pieces[0].shape[0]
    for r in range(count):
        whole[r * rows : (r + 1) * rows, :] = pieces[r][...]


def join(pieces):
    count = len(pieces)
    rows, columns = pieces[0].shape
    step = min(columns, 512)
    return pl.pallas_call(
        functools.partial(join_kernel, count),
        grid=(columns // step,),
        out_shape=jax.ShapeDtypeStruct((count * rows, columns), bf16),
        in_specs=[pl.BlockSpec((rows, step), lambda j: (0, j))] * count,
        out_specs=pl.BlockSpec((count * rows, step), lambda j: (0, j)),
        compiler_params=pltpu.CompilerParams(vmem_limit_bytes=17 << 20),
        cost_estimate=brief(),
        name="join",
    )(*pieces)


def any_space():
    return pl.BlockSpec(memory_space=pl.ANY)


def share_kernel(low, size, terms, *refs):
    lefts = refs[:terms]
    weights = refs[terms : 2 * terms]
    outs = refs[2 * terms : -terms - 1]
    held, sems = refs[-terms - 1 : -1], refs[-1]
    rows = outs[0].shape[0]
    copies = []
    for t in range(terms):
        copy = pltpu.make_async_copy(lefts[t].at[pl.ds(low * rows, size), :], held[t], sems.at[t])
        copy.start()
        copies.append(copy)
    for copy in copies:
        copy.wait()
    for p in range(size // (2 * rows)):
        here = pl.ds(2 * p * rows, 2 * rows)
        total = dot(held[0][here, :], weights[0][...])
        for t in range(1, terms):
            total = total + dot(held[t][here, :], weights[t][...])
        outs[2 * p][...] = total[:rows].astype(bf16)
        outs[2 * p + 1][...] = total[rows:].astype(bf16)


def shares(lefts, weights, count):
    rows = lefts[0].shape[0] // count
    inner = lefts[0].shape[1]
    columns = weights[0].shape[1]
    terms = len(lefts)

    def share(clock, low, high):
        size = (high - low) * rows
        return pl.pallas_call(
            functools.partial(share_kernel, low, size, terms),
            out_shape=[jax.ShapeDtypeStruct((rows, columns), bf16)] * (high - low),
            in_specs=[any_space()] * terms + [vmem()] * terms,
            out_specs=[vmem()] * (high - low),
            scratch_shapes=[pltpu.VMEM((size, inner), bf16)] * terms
            + [pltpu.SemaphoreType.DMA((terms,))],
            compiler_params=pltpu.CompilerParams(vmem_limit_bytes=36 << 20),
            cost_estimate=brief(),
            name="share",
        )(*clock.all(*lefts), *weights)

    return share


def feed_kernel(pairs, first, *refs):
    pieces = refs[: 2 * pairs]
    upper, gate_weight, up_weight = refs[2 * pairs : 2 * pairs + 3]
    rest = refs[2 * pairs + 3 :]
    outs, held, buffers, sems = rest[-8:-5], rest[-5], rest[-4:-1], rest[-1]
    rows = pieces[0].shape[0]

    def rows_of(p):
        return pl.ds((first + p) * 2 * rows, 2 * rows)

    loads = []
    for p in range(pairs):
        load = pltpu.make_async_copy(upper.at[rows_of(p), :], held.at[p], sems.at[3, p])
        load.start()
        loads.append(load)
    copies = []
    for p in range(pairs):
        here = jnp.concatenate([pieces[2 * p][...], pieces[2 * p + 1][...]], axis=0)
        gate = right_transposed(here, gate_weight[...])
        upward = right_transposed(here, up_weight[...])
        loads[p].wait()
        hidden_grad = held[p]
        sigmoid = jax.nn.sigmoid(gate)
        swish = gate * sigmoid
        results = (
            swish * upward,
            hidden_grad * upward * sigmoid * (1.0 + gate * (1.0 - sigmoid)),
            hidden_grad * swish,
        )
        for k, result in enumerate(results):
            buffers[k][p] = result.astype(bf16)
            copy = pltpu.make_async_copy(buffers[k].at[p], outs[k].at[rows_of(p), :], sems.at[k, p])
            copy.start()
            copies.append(copy)
    for copy in copies:
        copy.wait()


def feed(pieces, low, high, upper, gate_weight, up_weight, count, past):
    rows, dim = pieces[low].shape
    units = gate_weight.shape[0]
    pairs = (high - low) // 2
    operands = list(pieces[low:high]) + [upper, gate_weight, up_weight]
    specs = [vmem()] * (high - low) + [any_space()] + [vmem()] * 2
    aliases = {}
    if past is not None:
        aliases = {len(operands) + k: k for k in range(3)}
        operands += list(past)
        specs += [any_space()] * 3
    size = (high - low) * rows
    return pl.pallas_call(
        functools.partial(feed_kernel, pairs, low // 2),
        out_shape=[jax.ShapeDtypeStruct((count * rows, units), bf16)] * 3,
        in_specs=specs,
        out_specs=[any_space()] * 3,
        scratch_shapes=[pltpu.VMEM((pairs, 2 * rows, units), f32)]
        + [pltpu.VMEM((pairs, 2 * rows, units), bf16)] * 3
        + [pltpu.SemaphoreType.DMA((4, pairs))],
        input_output_aliases=aliases,
        compiler_params=pltpu.CompilerParams(vmem_limit_bytes=28 << 20),
        cost_estimate=brief(),
        name="feed",
    )(*operands)


def sum_kernel(*refs):
    total = refs[0][...].astype(f32)
    for ref in refs[1:-1]:
        total = total + ref[...].astype(f32)
    refs[-1][...] = total.astype(bf16)


def call(kernel, shapes, operands, name, scalars=0, limit=24, scratch=()):
    single = not isinstance(shapes, list)
    return pl.pallas_call(
        kernel,
        out_shape=shapes,
        in_specs=[smem()] * scalars + [vmem()] * (len(operands) - scalars),
        out_specs=vmem() if single else [vmem()] * len(shapes),
        scratch_shapes=list(scratch),
        compiler_params=pltpu.CompilerParams(vmem_limit_bytes=limit << 20),
        cost_estimate=brief(),
        name=name,
    )(*operands)


def shaped(shape, kind):
    return jax.ShapeDtypeStruct(shape, kind)


def add_rows(*values):
    return call(sum_kernel, shaped(values[0].shape, bf16), values, "add_rows")


def add_or_begin_kernel(inner, own, came, value, out):
    @pl.when(inner[0] == 1)
    def _():
        out[...] = (own[...].astype(f32) + came[...].astype(f32)).astype(bf16)

    @pl.when(inner[0] == 0)
    def _():
        out[...] = value[...]


def add_or_begin(inner, own, came, value):
    return call(
        add_or_begin_kernel,
        shaped(own.shape, bf16),
        [inner, own, came, value],
        "add_or_begin",
        scalars=1,
    )


def settle_kernel(low, at, *refs):
    inner, own, came = refs[:3]
    out, buffer, sem = refs[-3:]
    rows = buffer.shape[0]

    @pl.when(inner[0] == 1)
    def _():
        buffer[...] = own[low : low + rows, :].astype(f32)

    @pl.when(inner[0] == 0)
    def _():
        buffer[...] = came[low : low + rows, :].astype(f32)

    copy = pltpu.make_async_copy(buffer, out.at[pl.ds(at, rows), :], sem)
    copy.start()
    copy.wait()


def settle(inner, own, came, size, at=0, past=None, low=0, high=None):
    columns = own.shape[1]
    rows = (high or own.shape[0]) - low
    operands = [inner, own, came]
    specs = [smem(), vmem(), vmem()]
    aliases = {}
    if past is not None:
        aliases = {3: 0}
        operands.append(past)
        specs.append(any_space())
    return pl.pallas_call(
        functools.partial(settle_kernel, low, at),
        out_shape=shaped((size, columns), f32),
        in_specs=specs,
        out_specs=any_space(),
        scratch_shapes=[pltpu.VMEM((rows, columns), f32), pltpu.SemaphoreType.DMA],
        input_output_aliases=aliases,
        compiler_params=pltpu.CompilerParams(vmem_limit_bytes=16 << 20),
        cost_estimate=brief(),
        name="settle",
    )(*operands)


def product_kernel(first, left, right, *refs):
    outs = refs[first:]
    total = left_transposed(left[...], right[...]).astype(bf16)
    if first:
        total = jnp.concatenate([refs[0][...], total], axis=0)
    low = 0
    for out in outs:
        rows = out.shape[0]
        out[...] = total[low : low + rows]
        low += rows


def weight_product(left, right, rows, above=None, step=512):
    tokens, units = left.shape
    columns = right.shape[1]
    step = min(step, columns)
    operands = [left, right]
    specs = [
        pl.BlockSpec((tokens, units), lambda j: (0, 0)),
        pl.BlockSpec((tokens, step), lambda j: (0, j)),
    ]
    if above is not None:
        operands.append(above)
        specs.append(pl.BlockSpec((above.shape[0], step), lambda j: (0, j)))
    return pl.pallas_call(
        functools.partial(product_kernel, len(operands) - 2),
        grid=(columns // step,),
        out_shape=[shaped((one, columns), bf16) for one in rows],
        in_specs=specs,
        out_specs=[pl.BlockSpec((one, step), lambda j: (0, j)) for one in rows],
        compiler_params=pltpu.CompilerParams(vmem_limit_bytes=30 << 20),
        cost_estimate=brief(),
        name="weight_product",
    )(*operands)


def pack_last_kernel(above, wide, below, out):
    top = above.shape[0]
    rows, columns = wide.shape
    parts = out.shape[1] // columns
    step = rows // parts
    out[:top, :] = above[...]
    for j in range(parts):
        out[top : top + step, j * columns : (j + 1) * columns] = wide[j * step : (j + 1) * step, :]
    out[top + step :, :] = below[...]


def pack_last(above, wide, below):
    columns = above.shape[1]
    rows = above.shape[0] + wide.size // columns + below.shape[0]
    return call(
        pack_last_kernel, shaped((rows, columns), bf16), [above, wide, below], "pack_last"
    )


def settle_last_kernel(top, inner, own, came, wide, below):
    rows, columns = wide.shape
    parts = own.shape[1] // columns
    step = rows // parts

    def write(source):
        for j in range(parts):
            wide[j * step : (j + 1) * step, :] = source[
                top : top + step, j * columns : (j + 1) * columns
            ].astype(f32)
        below[...] = source[top + step :, :].astype(f32)

    @pl.when(inner[0] == 1)
    def _():
        write(own)

    @pl.when(inner[0] == 0)
    def _():
        write(came)


def settle_last(inner, own, came, top, rows, columns):
    total, dim = own.shape
    left = total - top - rows * columns // dim
    return call(
        functools.partial(settle_last_kernel, top),
        [shaped((rows, columns), f32), shaped((left, dim), f32)],
        [inner, own, came],
        "settle_last",
        scalars=1,
    )


def pack_kernel(count, *refs):
    total = summed(refs[:count]).astype(bf16)
    beside, out = refs[count:]
    rows, columns = total.shape
    tall = rows * 3 // 4
    out[:tall, :columns] = total[:tall]
    third = columns // 3
    for j in range(3):
        low = j * (rows - tall)
        out[low : low + rows - tall, columns:] = total[tall:, j * third : (j + 1) * third]
    out[tall:, :] = beside[...]


def pack(parts, beside):
    rows, columns = parts[0].shape
    tall = rows * 3 // 4
    return call(
        functools.partial(pack_kernel, len(parts)),
        shaped((tall + beside.shape[0], beside.shape[1]), bf16),
        [*parts, beside],
        "pack",
    )


def pick_kernel(inner, own, came, out):
    rows = out.shape[0]

    @pl.when(inner[0] == 1)
    def _():
        out[...] = own[:rows, :]

    @pl.when(inner[0] == 0)
    def _():
        out[...] = came[:rows, :]


def pick(inner, own, came, rows):
    return call(
        pick_kernel,
        shaped((rows, own.shape[1]), bf16),
        [inner, own, came],
        "pick",
        scalars=1,
    )


def widen_kernel(*refs):
    out = refs[-1]
    low = 0
    for x in refs[:-1]:
        rows = x.shape[0]
        out[low : low + rows, :] = x[...].astype(f32)
        low += rows


def widen(parts, step=512):
    rows = sum(part.shape[0] for part in parts)
    columns = parts[0].shape[1]
    return pl.pallas_call(
        widen_kernel,
        grid=(columns // step,),
        out_shape=shaped((rows, columns), f32),
        in_specs=[pl.BlockSpec((part.shape[0], step), lambda j: (0, j)) for part in parts],
        out_specs=pl.BlockSpec((rows, step), lambda j: (0, j)),
        compiler_params=pltpu.CompilerParams(vmem_limit_bytes=16 << 20),
        cost_estimate=brief(),
        name="widen",
    )(*parts)


def settle_two_kernel(inner, own, came, above, below):
    rows = above.shape[0]

    @pl.when(inner[0] == 1)
    def _():
        above[...] = own[:rows, :].astype(f32)
        below[...] = own[rows:, :].astype(f32)

    @pl.when(inner[0] == 0)
    def _():
        above[...] = came[:rows, :].astype(f32)
        below[...] = came[rows:, :].astype(f32)


def settle_two(inner, own, came, rows):
    total, columns = own.shape
    return call(
        settle_two_kernel,
        [shaped((rows, columns), f32), shaped((total - rows, columns), f32)],
        [inner, own, came],
        "settle_two",
        scalars=1,
    )


def rotated(first, second, cosine, sine):
    return first * cosine - second * sine, second * cosine + first * sine


def enter_kernel(rank, width, x, gain, down, latent_gain, key, value, cosine, sine, *outs):
    normed, latent, packed = outs
    half = width // 2
    rows = x[...].astype(f32)
    low = (rows * inverse_rms(rows) * gain[...]).astype(bf16)
    normed[...] = low
    inner = dot(low, down[...])
    latent[...] = inner
    packed[:, :rank] = (inner * inverse_rms(inner) * latent_gain[...]).astype(bf16)
    keys = dot(low, key[...])
    first, second = rotated(keys[:, :half], keys[:, half:], cosine[...], sine[...])
    packed[:, rank : rank + half] = first.astype(bf16)
    packed[:, rank + half : rank + width] = second.astype(bf16)
    packed[:, rank + width :] = dot(low, value[...]).astype(bf16)


def enter(x, gain, down, latent_gain, key, value, cosine, sine):
    rows, dim = x.shape
    rank, width = down.shape[1], key.shape[1]
    return call(
        functools.partial(enter_kernel, rank, width),
        [shaped((rows, dim), bf16), shaped((rows, rank), f32), shaped((rows, rank + 2 * width), bf16)],
        [x, gain[None], down, latent_gain[None], key, value, cosine, sine],
        "enter",
        limit=60,
    )


def summed(parts):
    total = parts[0][...].astype(f32)
    for part in parts[1:]:
        total = total + part[...].astype(f32)
    return total


def middle_kernel(x, gain, *refs):
    parts, (middle, normed) = refs[:-2], refs[-2:]
    total = x[...].astype(f32) + summed(parts)
    middle[...] = total
    normed[...] = (total * inverse_rms(total) * gain[...]).astype(bf16)


def middle_rows(x, gain, parts):
    shape = x.shape
    return call(
        middle_kernel,
        [shaped(shape, f32), shaped(shape, bf16)],
        [x, gain[None], *parts],
        "middle_rows",
    )


def lower_norm(value, gain, upper):
    scale = inverse_rms(value)
    scaled = upper * gain
    lower = scale * scaled - value * (scale * scale * scale) * jnp.mean(
        scaled * value, axis=-1, keepdims=True
    )
    return lower, jnp.sum(upper * value * scale, axis=0, keepdims=True)


def middle_back_kernel(middle, gain, cotangent, *refs):
    parts, (total, low, gain_part) = refs[:-3], refs[-3:]
    lower, gain_part[...] = lower_norm(middle[...], gain[...], summed(parts))
    result = cotangent[...].astype(f32) + lower
    total[...] = result
    low[...] = result.astype(bf16)


def middle_back(middle, gain, cotangent, parts):
    shape = middle.shape
    return call(
        middle_back_kernel,
        [shaped(shape, f32), shaped(shape, bf16), shaped((1, shape[1]), f32)],
        [middle, gain[None], cotangent, *parts],
        "middle_back",
    )


def latent_back_kernel(latent, gain, cosine, sine, *refs):
    parts, (packed, gain_part) = refs[:-2], refs[-2:]
    rank = latent.shape[1]
    total = summed(parts)
    lower, gain_part[...] = lower_norm(latent[...], gain[...], total[:, :rank])
    width = (total.shape[1] - rank) // 2
    half = width // 2
    packed[:, :rank] = lower.astype(bf16)
    first, second = rotated(
        total[:, rank : rank + half], total[:, rank + half : rank + width], cosine[...], -sine[...]
    )
    packed[:, rank : rank + half] = first.astype(bf16)
    packed[:, rank + half : rank + width] = second.astype(bf16)
    packed[:, rank + width :] = total[:, rank + width :].astype(bf16)


def latent_back(latent, gain, cosine, sine, parts):
    shape = parts[0].shape
    return call(
        latent_back_kernel,
        [shaped(shape, bf16), shaped((1, latent.shape[1]), f32)],
        [latent, gain[None], cosine, sine, *parts],
        "latent_back",
    )


def leave_kernel(packed, down, key, value, x, gain, upper, result, gain_part):
    rank, width = down.shape[1], key.shape[1]
    total = right_transposed(packed[:, :rank], down[...])
    total = total + right_transposed(packed[:, rank : rank + width], key[...])
    total = total + right_transposed(packed[:, rank + width :], value[...])
    lower, gain_part[...] = lower_norm(x[...].astype(f32), gain[...], total)
    result[...] = upper[...] + lower


def leave(packed, down, key, value, x, gain, upper):
    return call(
        leave_kernel,
        [shaped(x.shape, f32), shaped((1, x.shape[1]), f32)],
        [packed, down, key, value, x, gain[None], upper],
        "leave",
    )


def shared_kernel(count, table, normed, grads, *outs):
    rows = outs[0].shape[0]
    for r in range(count):
        there = pl.ds(pl.multiple_of(table[r] * rows, rows), rows)
        outs[r][...] = left_transposed(normed[:, there], grads[...]).astype(bf16)


def shared_shares(table, normed, grads):
    count = table.shape[0]
    rows = normed.shape[1] // count
    columns = grads.shape[1]
    return list(
        pl.pallas_call(
            functools.partial(shared_kernel, count),
            out_shape=[jax.ShapeDtypeStruct((rows, columns), bf16)] * count,
            in_specs=[smem(), vmem(), vmem()],
            out_specs=[vmem()] * count,
            compiler_params=pltpu.CompilerParams(vmem_limit_bytes=36 << 20),
            cost_estimate=brief(),
            name="shared_shares",
        )(table, normed, grads)
    )


def unpack_kernel(count, parts, packed, table, *refs):
    pieces = refs[:count]
    outs = refs[count : count + len(parts)]
    buffers = refs[count + len(parts) : -1]
    sems = refs[-1]
    rows = buffers[0].shape[1]
    tall = rows * 3 // 4
    columns = parts[-1][1]
    third = columns // 3
    flying = []
    for r in range(count):
        slot = r % 2
        if r >= 2:
            for copy in flying[r - 2]:
                copy.wait()
        there = pl.ds(pl.multiple_of(table[r] * rows, rows), rows)
        copies = []
        for k, (low, high) in enumerate(parts):
            if packed:
                buffers[k][slot, :tall, :] = pieces[r][:, low:high].astype(f32)
                for j in range(3):
                    first, last = max(low, j * third), min(high, (j + 1) * third)
                    if first < last:
                        start = columns - j * third
                        buffers[k][slot, tall:, first - low : last - low] = pieces[r][
                            j * (rows - tall) : (j + 1) * (rows - tall),
                            start + first : start + last,
                        ].astype(f32)
            else:
                buffers[k][slot] = pieces[r][:, low:high].astype(f32)
            copy = pltpu.make_async_copy(
                buffers[k].at[slot], outs[k].at[there, :], sems.at[k, slot]
            )
            copy.start()
            copies.append(copy)
        flying.append(copies)
    for copies in flying[-2:]:
        for copy in copies:
            copy.wait()


def unpack(table, pieces, parts, packed):
    count = len(pieces)
    rows = pieces[0].shape[0]
    if packed:
        rows = rows * 4 // 3
    return pl.pallas_call(
        functools.partial(unpack_kernel, count, parts, packed),
        out_shape=[jax.ShapeDtypeStruct((count * rows, high - low), f32) for low, high in parts],
        in_specs=[smem()] + [vmem()] * count,
        out_specs=[any_space()] * len(parts),
        scratch_shapes=[pltpu.VMEM((2, rows, high - low), f32) for low, high in parts]
        + [pltpu.SemaphoreType.DMA((len(parts), 2))],
        compiler_params=pltpu.CompilerParams(vmem_limit_bytes=36 << 20),
        cost_estimate=brief(),
        name="unpack",
    )(table, *pieces)


def body(
    packs,
    group,
    block_input,
    segment_ids,
    positions,
    attention_gain,
    query_down,
    query_gain,
    query_up,
    key_proj,
    value_proj,
    out_proj,
    feed_gain,
    gate_weight,
    up_weight,
    down_weight,
    out_grad,
):
    plane = Plane(group)
    line = Line(packs)
    rows = block_input.shape[1]
    segments = segment_ids[0]
    places = positions[0]
    width = key_proj.shape[1]
    rank = query_down.shape[1]
    heads = query_up.shape[1] // width
    scale = 1.0 / math.sqrt(width)
    first_row = plane.me * rows

    gate_rows, up_rows = gate_weight.T, up_weight.T
    clock = Clock()
    belt = Belt(line, clock)
    fast = plane.fast
    move = plane.move
    hop_a, hop_b, hop_c = (plane.hop_a, plane.hop_b, plane.hop_c) if fast else (None,) * 3
    cotangent_rows = out_grad[0]

    x = block_input[0]
    dim = x.shape[1]
    always = (segments[0] & 1) <= 1

    def stage(run):
        def inside():
            inner = Clock()
            inner.last = clock.last
            return tuple(run(inner))

        if not fast:
            return inside()
        shapes = jax.eval_shape(inside)
        result = lax.cond(
            always, inside, lambda: tuple(jnp.zeros(one.shape, one.dtype) for one in shapes)
        )
        return clock.all(*result)

    def hops(values, ways, filler=None, apart=False):
        def run(clock):
            held = clock.all(*values)
            came = [move(value, way) for value, way in zip(held, ways)]
            more = list(filler(clock, *came)) if filler else []
            return [*clock.all(*came), *more]

        result = stage(run) if apart else run(clock)
        return list(result[: len(values)]), list(result[len(values) :])

    def gather(rows, first=None, second=None, apart=False, between=None, last=False):
        def beside(clock, a, b, s_o):
            return first(clock, [rows, clock(s_o)]) if first else []

        (a, b, s_o), more = hops([rows, rows, rows], [hop_a, hop_b, hop_c], beside, apart)
        if between:
            between()

        def beside(clock, c, a_o, b_o):
            if not second:
                return []
            a_o, b_o = clock(a_o, b_o)
            return second(clock, [a, a_o, b, b_o], more)

        (c, a_o, b_o), later = hops([a, a, b], [hop_b, hop_c, hop_c], beside, apart)
        (c_o,), _ = hops([c], [hop_c], None, apart or last)
        return [rows, s_o, a, a_o, b, b_o, c, c_o], more, later

    def scatter(share, filler=None, apart=False, between=None):
        c, c_send = clock(*share(clock, 6, 8))
        (c_came,), near = hops(
            [c_send], [hop_c], lambda clock, came: clock(*share(clock, 2, 6)), apart
        )
        a, a_send, b, b_send = near
        c = clock(add_rows(c, c_came))
        (c_in, a_came, b_came), (own, own_send) = hops(
            [c, a_send, b_send],
            [hop_b, hop_c, hop_c],
            lambda clock, *came: clock(*share(clock, 0, 2)),
            apart,
        )
        a, b = clock(add_rows(a, a_came, c_in), add_rows(b, b_came))
        if between:
            between()
        (a_in, b_in, own_came), more = hops(
            [a, b, own_send],
            [hop_a, hop_b, hop_c],
            (lambda clock, *came: filler(clock)) if filler else None,
            apart,
        )
        return [own, own_came, b_in, a_in], more

    own_places = lax.dynamic_slice_in_dim(places, first_row, rows, 0)
    own_cosine, own_sine = rotation(own_places, width)

    def enter_rows():
        return enter(
            x, attention_gain, query_down, query_gain, key_proj, value_proj, own_cosine, own_sine
        )

    def attend(pieces, cosine, sine):
        return attend_forward(
            plane.table, pieces, query_up, cosine, sine, segments, heads, width, scale
        )

    def attend_back(outer):
        return attend_backward(
            plane.table, outer, queries, keys, values, cosine, sine, segments, heads, scale
        )

    def leave_rows(packed_grad):
        return leave(
            packed_grad, query_down, key_proj, value_proj, x, attention_gain, middle_grad
        )

    def sum_gains(parts, total):
        return total(jnp.concatenate(parts, axis=1))

    units = gate_rows.shape[0]
    size = heads * width
    columns = ((0, rank), (rank, rank + width), (rank + width, rank + 2 * width))
    add = lambda left, right: left + right

    if not fast:
        normed_rows, latent, packed = enter_rows()
        cosine, sine = rotation(places, width)
        pieces = plane.gather(packed)
        latents, queries, keys, values, mixed_there = attend(pieces, cosine, sine)
        share = shares([mixed_there], [out_proj], group)
        parts = [plane.scatter(share(clock, 0, group))]
        middle, normed_mid_rows = middle_rows(x, feed_gain, parts)
        cot_pieces = plane.gather(cotangent_rows)
        hidden_grad = rows_product(cot_pieces, down_weight, f32)
        mid_pieces = plane.gather(normed_mid_rows)
        hidden, gate_grad, upward_grad = feed(
            mid_pieces, 0, group, hidden_grad, gate_rows, up_rows, group, None
        )
        cotangent, normed_mid = join(cot_pieces), join(mid_pieces)
        share = shares([gate_grad, upward_grad], [gate_rows, up_rows], group)
        parts = [plane.scatter(share(clock, 0, group))]
        middle_grad, attention_grad, feed_gain_part = middle_back(
            middle, feed_gain, cotangent_rows, parts
        )
        grad_pieces = plane.gather(attention_grad)
        outer = [rows_product(grad_pieces, out_proj, bf16)]
        query_pre_grad, pair_grads = attend_back(outer)
        share = latent_shares(plane.table, query_pre_grad, pair_grads, query_up)
        parts = [plane.scatter(share(clock, 0, group))]
        packed_grad, query_gain_part = latent_back(latent, query_gain, own_cosine, own_sine, parts)
        shared_pieces = shared_shares(plane.table, normed_rows, packed_grad)
        shared = line.total(plane.scatter(list(shared_pieces)).astype(bf16))
        query_down_gradient, key_proj_gradient, value_proj_gradient = unpack(
            plane.table, plane.gather(shared), columns, False
        )
        input_gradient, attention_gain_part = leave_rows(packed_grad)
        share = shares([hidden], [down_weight], group)
        block_output = add_rows(middle, plane.scatter(share(clock, 0, group)))
        gains = sum_gains([attention_gain_part, query_gain_part, feed_gain_part], plane.total)
        gains = line.total(gains, add)[0]
        down_gradient, gate_gradient, up_gradient, proj_gradient, query_up_gradient = (
            line.total(weight_product(left, right, [left.shape[1]])[0]).astype(f32)
            for left, right in (
                (hidden, cotangent),
                (gate_grad, normed_mid),
                (upward_grad, normed_mid),
                (mixed_there, join(grad_pieces)),
                (latents, query_pre_grad),
            )
        )
    else:
        half = units // 2
        cot_a = move(cotangent_rows, hop_a)
        normed_rows, latent, packed = enter_rows()
        packed = clock(packed)

        def angles(clock, own):
            return clock(*rotation(clock(places), width))

        pieces, (cosine, sine), _ = gather(packed, angles, apart=True)
        cot_now, cot_a = clock(cotangent_rows, cot_a)
        cot_b, cot_c = move(cot_now, hop_b), move(cot_a, hop_b)
        cot_o, cot_ao = move(cot_now, hop_c), move(cot_a, hop_c)
        pieces[0] = clock(packed)

        latents, queries, keys, values, mixed_there = clock(*attend(pieces, cosine, sine))
        share = shares([mixed_there], [out_proj], group)
        c, c_send = clock(*share(clock, 6, 8))
        a, a_send, b, b_send = clock(*share(clock, 2, 6))
        own, own_send = clock(*share(clock, 0, 2))
        cot_b, cot_c, cot_o, cot_ao = clock(cot_b, cot_c, cot_o, cot_ao)
        (c_came,), _ = hops([c_send], [hop_c])
        c = clock(add_rows(c, c_came))
        (c_in, a_came, b_came), _ = hops([c, a_send, b_send], [hop_b, hop_c, hop_c])
        a, b = clock(add_rows(a, a_came, c_in), add_rows(b, b_came))

        def beside_last(clock, a_in, b_in, own_came, cot_bo, cot_co):
            cot_bo, cot_co = clock(cot_bo, cot_co)
            cot_pieces = [cotangent_rows, cot_o, cot_a, cot_ao, cot_b, cot_bo, cot_c, cot_co]
            hidden_grad = clock(rows_product(cot_pieces, down_weight, f32))
            return [hidden_grad]

        (a_in, b_in, own_came, cot_bo, cot_co), (hidden_grad,) = hops(
            [a, b, own_send, cot_b, cot_c], [hop_a, hop_b, hop_c, hop_c, hop_c], beside_last
        )
        cot_pieces = [cotangent_rows, cot_o, cot_a, cot_ao, cot_b, cot_bo, cot_c, cot_co]
        middle, normed_mid_rows = clock(*middle_rows(x, feed_gain, [own, own_came, b_in, a_in]))

        def feed_group(clock, pieces, low, high, past):
            pieces = [None] * low + [clock(pieces[0]), *pieces[1:]]
            return clock(
                *feed(pieces, low, high, hidden_grad, gate_rows, up_rows, group, past)
            )

        def near_feed(clock, near):
            cotangent = clock(join([clock(cot_pieces[0]), *cot_pieces[1:]]))
            return [cotangent, *feed_group(clock, near, 0, 2, None)]

        def next_feed(clock, near, more):
            return feed_group(clock, near, 2, 6, more[1:])

        mid_pieces, (cotangent, *_), past = gather(normed_mid_rows, near_feed, next_feed)
        hidden, gate_grad, upward_grad = feed_group(clock, mid_pieces[6:], 6, 8, past)
        chunk = units * 3 // 4
        tall = dim * 3 // (4 * group)
        beside = chunk - tall
        one, tail = clock(*weight_product(clock(hidden), cotangent, [chunk, units - chunk]))
        one = belt.begin(one)
        two = []

        def middle_filler(clock):
            normed_mid = clock(join([clock(mid_pieces[0]), *mid_pieces[1:]]))
            part, rest = clock(*weight_product(gate_grad, normed_mid, [chunk, units - half], tail))
            two.append(belt.begin(part))
            return [normed_mid, rest]

        share = shares([gate_grad, upward_grad], [gate_rows, up_rows], group)
        parts, (normed_mid, tail) = scatter(share, middle_filler)
        two = two[0]
        belt.cross(one)
        middle_grad, attention_grad, feed_gain_part = clock(
            *middle_back(middle, feed_gain, cotangent_rows, parts)
        )

        def near_grad(clock, near):
            outer = clock(rows_product([clock(near[0]), near[1]], out_proj, bf16))
            pair = clock(*weight_product(clock(upward_grad), normed_mid, [chunk, chunk], tail))
            return [outer, *pair]

        def next_grad(clock, near, more):
            return [clock(rows_product([clock(near[0]), *near[1:]], out_proj, bf16))]

        grad_pieces, (outer_near, three, four), (outer_next,) = gather(
            attention_grad, near_grad, next_grad, last=True
        )
        outer_last = clock(rows_product([clock(grad_pieces[6]), grad_pieces[7]], out_proj, bf16))
        three = belt.back(one, three)
        belt.cross(two)

        query_pre_grad, pair_grads = clock(*attend_back([outer_near, outer_next, clock(outer_last)]))

        def latent_filler(clock):
            whole = clock(join([clock(grad_pieces[0]), *grad_pieces[1:]]))
            return clock(*weight_product(mixed_there, whole, [beside, size - beside]))

        share = latent_shares(plane.table, query_pre_grad, pair_grads, query_up)
        parts, (five, six) = scatter(share, latent_filler)
        packed_grad, query_gain_part = clock(
            *latent_back(latent, query_gain, own_cosine, own_sine, parts)
        )
        belt.cross(three)
        four = belt.back(two, four)

        shared_pieces = clock(*shared_shares(plane.table, normed_rows, packed_grad))

        def shared_filler(clock):
            leaving = clock(*leave_rows(clock(packed_grad)))
            product = clock(weight_product(clock(latents), query_pre_grad, [rank])[0])
            belt.land(one)
            return [*leaving, product, clock(belt.end(one, units))]

        parts, (input_gradient, attention_gain_part, query_sum, down_gradient) = scatter(
            lambda clock, low, high: shared_pieces[low:high], shared_filler
        )
        five = clock(pack(parts, five))
        belt.cross(four)
        five = belt.back(three, five)
        fill = -(2 * dim + rank) % (16 * dim)

        def gain_rows(clock):
            gains = sum_gains(
                [clock(attention_gain_part), query_gain_part, feed_gain_part], plane.total
            )
            gains = jnp.concatenate([gains[0], jnp.zeros((fill,), f32)]).reshape(-1, dim)
            return [pack_last(six, query_sum, gains.astype(bf16))]

        (six,) = stage(gain_rows)

        settled = []

        def turn():
            belt.back(four)
            belt.cross(five)
            begun = belt.begin(six)
            belt.land(two)
            down = clock(belt.end(two, units, chunk, down_gradient, 0, units - chunk))
            gate = clock(belt.end(two, units, 0, None, units - chunk))
            belt.land(three)
            gate = clock(belt.end(three, units, half, gate, 0, half))
            up = clock(belt.end(three, units, 0, None, half))
            belt.land(four)
            belt.back(five)
            belt.cross(begun)
            settled.extend([begun, down, gate, up])

        share = shares([hidden], [down_weight], group)
        parts, _ = scatter(share, None, True, turn)
        block_output = clock(add_rows(middle, *parts))
        six, down_gradient, gate_gradient, up_gradient = settled
        up_gradient = clock(belt.end(four, units, chunk - half, up_gradient))
        belt.land(five)
        shared_rows = clock(pick(belt.inner, five["own"], five["came"], tall))

        def between():
            belt.back(six)

        shared_all, _, _ = gather(shared_rows, apart=True, between=between)
        query_down_gradient, key_proj_gradient, value_proj_gradient = clock(
            *unpack(plane.table, shared_all, columns, True)
        )
        proj_gradient = clock(belt.end(five, size, 0, None, tall))
        belt.land(six)
        proj_gradient = clock(
            belt.end(six, size, beside, proj_gradient, 0, size - beside)
        )
        query_up_gradient, gains = settle_last(
            belt.inner, six["own"], six["came"], size - beside, rank, size
        )
        gains = gains.reshape(-1)
    return (
        block_output[None],
        input_gradient[None],
        gains[:dim],
        query_down_gradient,
        gains[dim : dim + rank],
        query_up_gradient,
        key_proj_gradient,
        value_proj_gradient,
        proj_gradient,
        gains[dim + rank : dim + rank + dim],
        gate_gradient.T,
        up_gradient.T,
        down_gradient,
    )


def solution(mesh):
    in_specs = (
        P("tok", "head", None),
        P("tok", None),
        P("tok", None),
        P(),
        P(),
        P(),
        P(None, "head"),
        P(),
        P(),
        P("head", None),
        P(),
        P(None, "head"),
        P(None, "head"),
        P("head", None),
        P("tok", "head", None),
    )
    out_specs = (
        P("tok", "head", None),
        P("tok", "head", None),
        P(),
        P(),
        P(),
        P(None, "head"),
        P(),
        P(),
        P("head", None),
        P(),
        P(None, "head"),
        P(None, "head"),
        P("head", None),
    )
    sizes = dict(mesh.shape)
    return jax.shard_map(
        functools.partial(body, sizes["tok"], sizes["head"]),
        mesh=mesh,
        in_specs=in_specs,
        out_specs=out_specs,
        check_vma=False,
    )
```

```python
import functools
import math

import jax
import jax.numpy as jnp
from jax import lax
from jax.experimental import pallas as pl
from jax.experimental.pallas import tpu as pltpu
from jax.sharding import PartitionSpec as P

norm_epsilon = 1e-05
rope_base = 10000.0
first_document = 1024
bf16 = jnp.bfloat16
f32 = jnp.float32


def inverse_rms(value):
    return lax.rsqrt(jnp.mean(value * value, axis=-1, keepdims=True) + norm_epsilon)


def norm_backward(value, gain, upper):
    scale = inverse_rms(value)
    scaled = upper * gain
    lower = scale * scaled - value * (scale * scale * scale) * jnp.mean(
        scaled * value, axis=-1, keepdims=True
    )
    return (lower, jnp.sum(upper * value * scale, axis=0))


def rotation(places, head_width):
    half = head_width // 2
    steps = jnp.arange(half).astype(f32) * (2.0 / head_width)
    inverse = jnp.exp(steps * -math.log(rope_base))
    angles = places.astype(f32)[:, None] * inverse[None, :]
    return (jnp.cos(angles), jnp.sin(angles))


def rotate(value, cosine, sine):
    half = value.shape[-1] // 2
    first = value[..., :half]
    second = value[..., half:]
    return jnp.concatenate(
        [first * cosine - second * sine, second * cosine + first * sine], axis=-1
    )


def dot(left, right):
    return jnp.dot(left, right, preferred_element_type=f32)


def right_transposed(left, right):
    return lax.dot_general(left, right, (((1,), (1,)), ((), ())), preferred_element_type=f32)


def left_transposed(left, right):
    return lax.dot_general(left, right, (((0,), (0,)), ((), ())), preferred_element_type=f32)


def add_low(left, right):
    return (left.astype(f32) + right.astype(f32)).astype(bf16)


class Clock:
    def __init__(self):
        self.last = ()

    def all(self, *values):
        held = lax.optimization_barrier(values + self.last)
        self.last = (held[0],)
        return held[: len(values)]

    def __call__(self, *values):
        held = self.all(*values)
        return held[0] if len(values) == 1 else held


class Plane:
    def __init__(self, size):
        self.size = size
        self.fast = size == 8 and lax.axis_size("tok") == 4
        self.me = lax.axis_index("head")
        if self.fast:
            even = [index % 2 == 0 for index in range(size)]
            self.hop_a = [(i, i ^ (2 if even[i] else 4)) for i in range(size)]
            self.hop_b = [(i, i ^ (4 if even[i] else 2)) for i in range(size)]
            self.hop_c = [(i, i ^ 1) for i in range(size)]
            mask_a = jnp.where(self.me % 2 == 0, 2, 4)
            other = self.me ^ 1
            order = [
                self.me,
                other,
                self.me ^ mask_a,
                other ^ (6 - mask_a),
                self.me ^ (6 - mask_a),
                other ^ mask_a,
                self.me ^ 6,
                other ^ 6,
            ]
            self.table = jnp.stack(order).astype(jnp.int32)
            self.groups = [(0, 2), (2, 6), (6, 8)]
        else:
            self.table = jnp.arange(size, dtype=jnp.int32)
            self.groups = [(0, size)]

    def move(self, value, hop):
        return lax.ppermute(value, "head", hop)

    def gather(self, rows):
        whole = lax.all_gather(rows, "head", axis=0, tiled=True)
        return list(jnp.split(whole, self.size, axis=0))

    def scatter(self, pieces):
        whole = jnp.concatenate(pieces, axis=0)
        return lax.psum_scatter(whole, "head", scatter_dimension=0, tiled=True).astype(f32)

    def total(self, value):
        if not self.fast:
            return lax.psum(value, "head")
        for bit in (1, 2, 4):
            value = value + self.move(value, [(i, i ^ bit) for i in range(8)])
        return value


class Line:
    def __init__(self, size):
        self.size = size
        self.me = lax.axis_index("tok")
        half = size // 2
        self.stages = [([(k, k + 1), (size - 1 - k, size - 2 - k)], None) for k in range(half - 1)]
        self.stages.append(([(half - 1, half), (half, half - 1)], None))
        for k in reversed(range(half - 1)):
            self.stages.append(([(k + 1, k), (size - 2 - k, size - 1 - k)], k))

    def start(self, stage, value):
        return lax.ppermute(value, "tok", self.stages[stage][0])

    def finish(self, stage, value, came, plus=add_low):
        outward = self.stages[stage][1]
        if outward is None:
            return plus(value, came)
        mine = (self.me == outward) | (self.me == self.size - 1 - outward)
        return jnp.where(mine, came, value)

    def total(self, value, plus=add_low):
        for stage in range(len(self.stages)):
            value = self.finish(stage, value, self.start(stage, value), plus)
        return value


class Belt:
    inward = [(0, 1), (3, 2)]
    middle = [(1, 2), (2, 1)]
    outward = [(1, 0), (2, 3)]

    def __init__(self, line, clock):
        self.clock = clock
        self.inner = jnp.where((line.me == 1) | (line.me == 2), 1, 0).astype(jnp.int32).reshape(1)

    def move(self, value, pairs):
        return lax.ppermute(value, "tok", pairs)

    def begin(self, value):
        value = self.clock(value)
        return {"own": value, "came": self.move(value, self.inward)}

    def cross(self, item):
        item["came"] = self.clock(item["came"])
        item["own"] = self.clock(add_rows(item["own"], item["came"]))
        item["came"] = self.move(item["own"], self.middle)

    def meet(self, item):
        item["came"] = self.clock(item["came"])
        item["own"] = self.clock(add_rows(item["own"], item["came"]))

    def send(self, item):
        item["own"] = self.clock(item["own"])
        item["came"] = self.move(item["own"], self.outward)

    def back(self, item, value=None):
        if value is None:
            self.meet(item)
            self.send(item)
            return None
        item["came"] = self.clock(item["came"])
        both = self.clock(add_or_begin(self.inner, item["own"], item["came"], value))
        came = self.move(both, self.inward + self.outward)
        item["own"], item["came"] = both, came
        return {"own": value, "came": came}

    def land(self, item):
        item["came"] = self.clock(item["came"])

    def end(self, item, size, at=0, past=None, low=0, high=None):
        return settle(self.inner, item["own"], item["came"], size, at, past, low, high)


def query_blocks(length):
    first = min(length, max(first_document, length // 2))
    block = 256
    return [
        (start, min(block, length - start), 0 if start < first else first)
        for start in range(0, length, block)
    ]


def allowed(seg_column, seg_row, start, rows, low, high):
    query_order = start + lax.broadcasted_iota(jnp.int32, (rows, high - low), 0)
    key_order = low + lax.broadcasted_iota(jnp.int32, (rows, high - low), 1)
    same = seg_column[start : start + rows, :] == seg_row[:, low:high]
    return (key_order <= query_order) & same


def weights_of(stacked, keys, permit, heads, scale):
    scores = right_transposed(stacked, keys) * scale
    scores = jnp.where(jnp.concatenate([permit] * heads, axis=0), scores, -1e30)
    top = jnp.max(scores, axis=-1, keepdims=True)
    weights = jnp.exp(scores - top)
    return weights, jnp.sum(weights, axis=-1, keepdims=True)


def stack_heads(ref, start, rows, heads, width):
    return jnp.concatenate(
        [ref[start : start + rows, h * width : (h + 1) * width] for h in range(heads)], axis=0
    )


def attend_forward_kernel(count, heads, width, rank, scale, *refs):
    table = refs[0]
    pieces = refs[1 : 1 + count]
    weight, cosine, sine, seg_column, seg_row = refs[1 + count : 6 + count]
    latents, queries, keys, values, mixed_there, mixed = refs[6 + count :]
    length = queries.shape[0]
    rows = length // count
    half = width // 2
    for r in range(count):
        there = pl.ds(pl.multiple_of(table[r] * rows, rows), rows)
        latents[there, :] = pieces[r][:, :rank]
        keys[there, :] = pieces[r][:, rank : rank + width]
        values[there, :] = pieces[r][:, rank + width :]
        flat = dot(pieces[r][:, :rank], weight[...])
        cos = cosine[there, :]
        sin = sine[there, :]
        for h in range(heads):
            first = flat[:, h * width : h * width + half]
            second = flat[:, h * width + half : (h + 1) * width]
            queries[there, h * width : h * width + half] = (first * cos - second * sin).astype(bf16)
            queries[there, h * width + half : (h + 1) * width] = (
                second * cos + first * sin
            ).astype(bf16)
    for start, size, low in query_blocks(length):
        high = start + size
        stacked = stack_heads(queries, start, size, heads, width)
        permit = allowed(seg_column, seg_row, start, size, low, high)
        weights, total = weights_of(stacked, keys[low:high, :], permit, heads, scale)
        probs = (weights / total).astype(bf16)
        result = dot(probs, values[low:high, :]).astype(bf16)
        for h in range(heads):
            mixed[start:high, h * width : (h + 1) * width] = result[h * size : (h + 1) * size]
    for r in range(count):
        there = pl.ds(pl.multiple_of(table[r] * rows, rows), rows)
        mixed_there[r * rows : (r + 1) * rows, :] = mixed[there, :]


def brief():
    return pl.CostEstimate(flops=1024, bytes_accessed=1024, transcendentals=0)


def vmem():
    return pl.BlockSpec(memory_space=pltpu.VMEM)


def smem():
    return pl.BlockSpec(memory_space=pltpu.SMEM)


def attend_forward(table, pieces, weight, cosine, sine, segments, heads, width, scale):
    count = len(pieces)
    length = cosine.shape[0]
    rank = weight.shape[0]
    shapes = [
        jax.ShapeDtypeStruct((length, rank), bf16),
        jax.ShapeDtypeStruct((length, heads * width), bf16),
        jax.ShapeDtypeStruct((length, width), bf16),
        jax.ShapeDtypeStruct((length, width), bf16),
        jax.ShapeDtypeStruct((length, heads * width), bf16),
    ]
    return pl.pallas_call(
        functools.partial(attend_forward_kernel, count, heads, width, rank, scale),
        out_shape=shapes,
        in_specs=[smem()] + [vmem()] * (count + 5),
        out_specs=[vmem()] * 5,
        scratch_shapes=[pltpu.VMEM((length, heads * width), bf16)],
        compiler_params=pltpu.CompilerParams(vmem_limit_bytes=48 << 20),
        cost_estimate=brief(),
        name="attend_forward",
    )(table, *pieces, weight, cosine, sine, segments[:, None], segments[None, :])


def attend_backward_kernel(parts, heads, width, scale, *refs):
    table = refs[0]
    grads_in = refs[1 : 1 + parts]
    queries, keys, values, cosine, sine, seg_column, seg_row = refs[1 + parts : 8 + parts]
    query_out, pair_out, outer, key_total, value_total = refs[8 + parts :]
    length = queries.shape[0]
    count = table.shape[0]
    rows = length // count
    half = width // 2

    def there(r):
        return pl.ds(pl.multiple_of(table[r] * rows, rows), rows)

    r = 0
    for part in grads_in:
        for k in range(part.shape[0] // rows):
            outer[there(r), :] = part[k * rows : (k + 1) * rows, :]
            r += 1
    key_total[...] = jnp.zeros_like(key_total)
    value_total[...] = jnp.zeros_like(value_total)
    for start, size, low in query_blocks(length):
        high = start + size
        stacked = stack_heads(queries, start, size, heads, width)
        grads = stack_heads(outer, start, size, heads, width)
        permit = allowed(seg_column, seg_row, start, size, low, high)
        weights, total = weights_of(stacked, keys[low:high, :], permit, heads, scale)
        probs = weights / total
        prob_grad = right_transposed(grads, values[low:high, :])
        centre = jnp.sum(probs * prob_grad, axis=-1, keepdims=True)
        score_grad = (probs * (prob_grad - centre)).astype(bf16)
        query_grad = dot(score_grad, keys[low:high, :]) * scale
        key_total[low:high, :] += left_transposed(score_grad, stacked) * scale
        value_total[low:high, :] += left_transposed(probs.astype(bf16), grads)
        cos = cosine[start:high, :]
        sin = sine[start:high, :]
        for h in range(heads):
            first = query_grad[h * size : (h + 1) * size, :half]
            second = query_grad[h * size : (h + 1) * size, half:]
            query_out[start:high, h * width : h * width + half] = (
                first * cos + second * sin
            ).astype(bf16)
            query_out[start:high, h * width + half : (h + 1) * width] = (
                second * cos - first * sin
            ).astype(bf16)
    pair_out[:, :width] = key_total[...].astype(bf16)
    pair_out[:, width:] = value_total[...].astype(bf16)


def attend_backward(table, grads, queries, keys, values, cosine, sine, segments, heads, scale):
    parts = len(grads)
    length, width = keys.shape
    shapes = [
        jax.ShapeDtypeStruct((length, heads * width), bf16),
        jax.ShapeDtypeStruct((length, 2 * width), bf16),
    ]
    return pl.pallas_call(
        functools.partial(attend_backward_kernel, parts, heads, width, scale),
        out_shape=shapes,
        in_specs=[smem()] + [vmem()] * (parts + 7),
        out_specs=[vmem()] * 2,
        scratch_shapes=[
            pltpu.VMEM((length, heads * width), bf16),
            pltpu.VMEM((length, width), f32),
            pltpu.VMEM((length, width), f32),
        ],
        compiler_params=pltpu.CompilerParams(vmem_limit_bytes=44 << 20),
        cost_estimate=brief(),
        name="attend_backward",
    )(
        table,
        *grads,
        queries,
        keys,
        values,
        cosine,
        sine,
        segments[:, None],
        segments[None, :],
    )


def rows_product_kernel(*refs):
    pieces, weight, out = refs[:-2], refs[-2], refs[-1]
    rows = pieces[0].shape[0]
    for p in range(0, len(pieces), 2):
        here = jnp.concatenate([pieces[p][...], pieces[p + 1][...]], axis=0)
        out[p * rows : (p + 2) * rows, :] = right_transposed(here, weight[...]).astype(out.dtype)


def rows_product(pieces, weight, kind):
    return pl.pallas_call(
        rows_product_kernel,
        out_shape=jax.ShapeDtypeStruct(
            (len(pieces) * pieces[0].shape[0], weight.shape[0]), kind
        ),
        in_specs=[vmem()] * (len(pieces) + 1),
        out_specs=vmem(),
        compiler_params=pltpu.CompilerParams(vmem_limit_bytes=36 << 20),
        cost_estimate=brief(),
        name="rows_product",
    )(*pieces, weight)


def latent_share_kernel(low, size, table, query_grads, pairs, weight, *refs):
    outs = refs[:-3]
    held, beside, sems = refs[-3:]
    rows = outs[0].shape[0]
    rank = weight.shape[0]
    copies = []
    for k in range(size // rows):
        there = pl.ds(pl.multiple_of(table[low + k] * rows, rows), rows)
        here = pl.ds(k * rows, rows)
        copies += [
            pltpu.make_async_copy(query_grads.at[there, :], held.at[here, :], sems.at[0, k]),
            pltpu.make_async_copy(pairs.at[there, :], beside.at[here, :], sems.at[1, k]),
        ]
    for copy in copies:
        copy.start()
    for copy in copies:
        copy.wait()
    for p in range(0, size // rows, 2):
        total = right_transposed(held[p * rows : (p + 2) * rows, :], weight[...])
        for k in range(2):
            outs[p + k][:, :rank] = total[k * rows : (k + 1) * rows].astype(bf16)
            outs[p + k][:, rank:] = beside[(p + k) * rows : (p + k + 1) * rows, :]


def latent_shares(table, query_grads, pairs, weight):
    count = table.shape[0]
    rows = query_grads.shape[0] // count
    rank, inner = weight.shape
    extra = pairs.shape[1]

    def share(clock, low, high):
        size = (high - low) * rows
        return pl.pallas_call(
            functools.partial(latent_share_kernel, low, size),
            out_shape=[jax.ShapeDtypeStruct((rows, rank + extra), bf16)] * (high - low),
            in_specs=[smem(), any_space(), any_space(), vmem()],
            out_specs=[vmem()] * (high - low),
            scratch_shapes=[
                pltpu.VMEM((size, inner), bf16),
                pltpu.VMEM((size, extra), bf16),
                pltpu.SemaphoreType.DMA((2, high - low)),
            ],
            compiler_params=pltpu.CompilerParams(vmem_limit_bytes=36 << 20),
            cost_estimate=brief(),
            name="latent_share",
        )(table, *clock(query_grads, pairs), weight)

    return share


def join_kernel(count, *refs):
    pieces, whole = refs[:count], refs[count]
    rows = pieces[0].shape[0]
    for r in range(count):
        whole[r * rows : (r + 1) * rows, :] = pieces[r][...]


def join(pieces):
    count = len(pieces)
    rows, columns = pieces[0].shape
    step = min(columns, 512)
    return pl.pallas_call(
        functools.partial(join_kernel, count),
        grid=(columns // step,),
        out_shape=jax.ShapeDtypeStruct((count * rows, columns), bf16),
        in_specs=[pl.BlockSpec((rows, step), lambda j: (0, j))] * count,
        out_specs=pl.BlockSpec((count * rows, step), lambda j: (0, j)),
        compiler_params=pltpu.CompilerParams(vmem_limit_bytes=17 << 20),
        cost_estimate=brief(),
        name="join",
    )(*pieces)


def any_space():
    return pl.BlockSpec(memory_space=pl.ANY)


def share_kernel(low, size, terms, *refs):
    lefts = refs[:terms]
    weights = refs[terms : 2 * terms]
    outs = refs[2 * terms : -terms - 1]
    held, sems = refs[-terms - 1 : -1], refs[-1]
    rows = outs[0].shape[0]
    copies = []
    for t in range(terms):
        copy = pltpu.make_async_copy(lefts[t].at[pl.ds(low * rows, size), :], held[t], sems.at[t])
        copy.start()
        copies.append(copy)
    for copy in copies:
        copy.wait()
    for p in range(size // (2 * rows)):
        here = pl.ds(2 * p * rows, 2 * rows)
        total = dot(held[0][here, :], weights[0][...])
        for t in range(1, terms):
            total = total + dot(held[t][here, :], weights[t][...])
        outs[2 * p][...] = total[:rows].astype(bf16)
        outs[2 * p + 1][...] = total[rows:].astype(bf16)


def shares(lefts, weights, count):
    rows = lefts[0].shape[0] // count
    inner = lefts[0].shape[1]
    columns = weights[0].shape[1]
    terms = len(lefts)

    def share(clock, low, high):
        size = (high - low) * rows
        return pl.pallas_call(
            functools.partial(share_kernel, low, size, terms),
            out_shape=[jax.ShapeDtypeStruct((rows, columns), bf16)] * (high - low),
            in_specs=[any_space()] * terms + [vmem()] * terms,
            out_specs=[vmem()] * (high - low),
            scratch_shapes=[pltpu.VMEM((size, inner), bf16)] * terms
            + [pltpu.SemaphoreType.DMA((terms,))],
            compiler_params=pltpu.CompilerParams(vmem_limit_bytes=36 << 20),
            cost_estimate=brief(),
            name="share",
        )(*clock.all(*lefts), *weights)

    return share


def feed_kernel(pairs, first, *refs):
    pieces = refs[: 2 * pairs]
    upper, gate_weight, up_weight = refs[2 * pairs : 2 * pairs + 3]
    rest = refs[2 * pairs + 3 :]
    outs, held, buffers, sems = rest[-8:-5], rest[-5], rest[-4:-1], rest[-1]
    rows = pieces[0].shape[0]

    def rows_of(p):
        return pl.ds((first + p) * 2 * rows, 2 * rows)

    loads = []
    for p in range(pairs):
        load = pltpu.make_async_copy(upper.at[rows_of(p), :], held.at[p], sems.at[3, p])
        load.start()
        loads.append(load)
    copies = []
    for p in range(pairs):
        here = jnp.concatenate([pieces[2 * p][...], pieces[2 * p + 1][...]], axis=0)
        gate = right_transposed(here, gate_weight[...])
        upward = right_transposed(here, up_weight[...])
        loads[p].wait()
        hidden_grad = held[p]
        sigmoid = jax.nn.sigmoid(gate)
        swish = gate * sigmoid
        results = (
            swish * upward,
            hidden_grad * upward * sigmoid * (1.0 + gate * (1.0 - sigmoid)),
            hidden_grad * swish,
        )
        for k, result in enumerate(results):
            buffers[k][p] = result.astype(bf16)
            copy = pltpu.make_async_copy(buffers[k].at[p], outs[k].at[rows_of(p), :], sems.at[k, p])
            copy.start()
            copies.append(copy)
    for copy in copies:
        copy.wait()


def feed(pieces, low, high, upper, gate_weight, up_weight, count, past):
    rows, dim = pieces[low].shape
    units = gate_weight.shape[0]
    pairs = (high - low) // 2
    operands = list(pieces[low:high]) + [upper, gate_weight, up_weight]
    specs = [vmem()] * (high - low) + [any_space()] + [vmem()] * 2
    aliases = {}
    if past is not None:
        aliases = {len(operands) + k: k for k in range(3)}
        operands += list(past)
        specs += [any_space()] * 3
    size = (high - low) * rows
    return pl.pallas_call(
        functools.partial(feed_kernel, pairs, low // 2),
        out_shape=[jax.ShapeDtypeStruct((count * rows, units), bf16)] * 3,
        in_specs=specs,
        out_specs=[any_space()] * 3,
        scratch_shapes=[pltpu.VMEM((pairs, 2 * rows, units), f32)]
        + [pltpu.VMEM((pairs, 2 * rows, units), bf16)] * 3
        + [pltpu.SemaphoreType.DMA((4, pairs))],
        input_output_aliases=aliases,
        compiler_params=pltpu.CompilerParams(vmem_limit_bytes=28 << 20),
        cost_estimate=brief(),
        name="feed",
    )(*operands)


def sum_kernel(*refs):
    total = refs[0][...].astype(f32)
    for ref in refs[1:-1]:
        total = total + ref[...].astype(f32)
    refs[-1][...] = total.astype(bf16)


def call(kernel, shapes, operands, name, scalars=0, limit=24, scratch=()):
    single = not isinstance(shapes, list)
    return pl.pallas_call(
        kernel,
        out_shape=shapes,
        in_specs=[smem()] * scalars + [vmem()] * (len(operands) - scalars),
        out_specs=vmem() if single else [vmem()] * len(shapes),
        scratch_shapes=list(scratch),
        compiler_params=pltpu.CompilerParams(vmem_limit_bytes=limit << 20),
        cost_estimate=brief(),
        name=name,
    )(*operands)


def shaped(shape, kind):
    return jax.ShapeDtypeStruct(shape, kind)


def add_rows(*values):
    return call(sum_kernel, shaped(values[0].shape, bf16), values, "add_rows")


def add_or_begin_kernel(inner, own, came, value, out):
    @pl.when(inner[0] == 1)
    def _():
        out[...] = (own[...].astype(f32) + came[...].astype(f32)).astype(bf16)

    @pl.when(inner[0] == 0)
    def _():
        out[...] = value[...]


def add_or_begin(inner, own, came, value):
    return call(
        add_or_begin_kernel,
        shaped(own.shape, bf16),
        [inner, own, came, value],
        "add_or_begin",
        scalars=1,
    )


def settle_kernel(low, at, *refs):
    inner, own, came = refs[:3]
    out, buffer, sem = refs[-3:]
    rows = buffer.shape[0]

    @pl.when(inner[0] == 1)
    def _():
        buffer[...] = own[low : low + rows, :].astype(f32)

    @pl.when(inner[0] == 0)
    def _():
        buffer[...] = came[low : low + rows, :].astype(f32)

    copy = pltpu.make_async_copy(buffer, out.at[pl.ds(at, rows), :], sem)
    copy.start()
    copy.wait()


def settle(inner, own, came, size, at=0, past=None, low=0, high=None):
    columns = own.shape[1]
    rows = (high or own.shape[0]) - low
    operands = [inner, own, came]
    specs = [smem(), vmem(), vmem()]
    aliases = {}
    if past is not None:
        aliases = {3: 0}
        operands.append(past)
        specs.append(any_space())
    return pl.pallas_call(
        functools.partial(settle_kernel, low, at),
        out_shape=shaped((size, columns), f32),
        in_specs=specs,
        out_specs=any_space(),
        scratch_shapes=[pltpu.VMEM((rows, columns), f32), pltpu.SemaphoreType.DMA],
        input_output_aliases=aliases,
        compiler_params=pltpu.CompilerParams(vmem_limit_bytes=16 << 20),
        cost_estimate=brief(),
        name="settle",
    )(*operands)


def product_kernel(count, first, step, left, *refs):
    pieces = refs[:count]
    outs, held, sems = refs[count + first : -2], refs[-2], refs[-1]
    rows = pieces[0].shape[0]
    here = pl.program_id(0)
    steps = pl.num_programs(0)

    def copies(j, slot):
        there = pl.ds(pl.multiple_of(j * step, step), step)
        return [
            pltpu.make_async_copy(
                pieces[r].at[:, there], held.at[slot, pl.ds(r * rows, rows), :], sems.at[slot, r]
            )
            for r in range(count)
        ]

    slot = lax.rem(here, 2)

    @pl.when(here == 0)
    def _():
        for copy in copies(0, 0):
            copy.start()

    @pl.when(here + 1 < steps)
    def _():
        for copy in copies(here + 1, 1 - slot):
            copy.start()

    for copy in copies(here, slot):
        copy.wait()
    total = left_transposed(left[...], held[slot]).astype(bf16)
    if first:
        total = jnp.concatenate([refs[count][...], total], axis=0)
    low = 0
    for out in outs:
        size = out.shape[0]
        out[...] = total[low : low + size]
        low += size


def weight_product(left, right, rows, above=None, step=512):
    right = list(right) if isinstance(right, (list, tuple)) else [right]
    count = len(right)
    tokens, units = left.shape
    columns = right[0].shape[1]
    step = min(step, columns)
    operands = [left, *right]
    specs = [pl.BlockSpec((tokens, units), lambda j: (0, 0))] + [any_space()] * count
    if above is not None:
        operands.append(above)
        specs.append(pl.BlockSpec((above.shape[0], step), lambda j: (0, j)))
    return pl.pallas_call(
        functools.partial(product_kernel, count, len(operands) - 1 - count, step),
        grid=(columns // step,),
        out_shape=[shaped((one, columns), bf16) for one in rows],
        in_specs=specs,
        out_specs=[pl.BlockSpec((one, step), lambda j: (0, j)) for one in rows],
        scratch_shapes=[
            pltpu.VMEM((2, tokens, step), bf16),
            pltpu.SemaphoreType.DMA((2, count)),
        ],
        compiler_params=pltpu.CompilerParams(vmem_limit_bytes=30 << 20),
        cost_estimate=brief(),
        name="weight_product",
    )(*operands)


def pack_last_kernel(above, wide, below, out):
    top = above.shape[0]
    rows, columns = wide.shape
    parts = out.shape[1] // columns
    step = rows // parts
    out[:top, :] = above[...]
    for j in range(parts):
        out[top : top + step, j * columns : (j + 1) * columns] = wide[j * step : (j + 1) * step, :]
    out[top + step :, :] = below[...]


def pack_last(above, wide, below):
    columns = above.shape[1]
    rows = above.shape[0] + wide.size // columns + below.shape[0]
    return call(
        pack_last_kernel, shaped((rows, columns), bf16), [above, wide, below], "pack_last"
    )


def settle_last_kernel(top, at, inner, own, came, past, wide, below, whole, buffer, sem):
    rows, columns = wide.shape
    parts = own.shape[1] // columns
    step = rows // parts

    def write(source):
        buffer[...] = source[:top, :].astype(f32)
        copy = pltpu.make_async_copy(buffer, whole.at[pl.ds(at, top), :], sem)
        copy.start()
        for j in range(parts):
            wide[j * step : (j + 1) * step, :] = source[
                top : top + step, j * columns : (j + 1) * columns
            ].astype(f32)
        below[...] = source[top + step :, :].astype(f32)
        copy.wait()

    @pl.when(inner[0] == 1)
    def _():
        write(own)

    @pl.when(inner[0] == 0)
    def _():
        write(came)


def settle_last(inner, own, came, top, rows, columns, past, at):
    total, dim = own.shape
    left = total - top - rows * columns // dim
    return pl.pallas_call(
        functools.partial(settle_last_kernel, top, at),
        out_shape=[
            shaped((rows, columns), f32),
            shaped((left, dim), f32),
            shaped(past.shape, f32),
        ],
        in_specs=[smem(), vmem(), vmem(), any_space()],
        out_specs=[vmem(), vmem(), any_space()],
        scratch_shapes=[pltpu.VMEM((top, dim), f32), pltpu.SemaphoreType.DMA],
        input_output_aliases={3: 2},
        compiler_params=pltpu.CompilerParams(vmem_limit_bytes=24 << 20),
        cost_estimate=brief(),
        name="settle_last",
    )(inner, own, came, past)


def pack_kernel(count, *refs):
    total = summed(refs[:count]).astype(bf16)
    beside, out = refs[count:]
    rows, columns = total.shape
    tall = rows * 3 // 4
    out[:tall, :columns] = total[:tall]
    third = columns // 3
    for j in range(3):
        low = j * (rows - tall)
        out[low : low + rows - tall, columns:] = total[tall:, j * third : (j + 1) * third]
    out[tall:, :] = beside[...]


def pack(parts, beside):
    rows, columns = parts[0].shape
    tall = rows * 3 // 4
    return call(
        functools.partial(pack_kernel, len(parts)),
        shaped((tall + beside.shape[0], beside.shape[1]), bf16),
        [*parts, beside],
        "pack",
    )


def pick_kernel(inner, own, came, out):
    rows = out.shape[0]

    @pl.when(inner[0] == 1)
    def _():
        out[...] = own[:rows, :]

    @pl.when(inner[0] == 0)
    def _():
        out[...] = came[:rows, :]


def pick(inner, own, came, rows):
    return call(
        pick_kernel,
        shaped((rows, own.shape[1]), bf16),
        [inner, own, came],
        "pick",
        scalars=1,
    )


def widen_kernel(*refs):
    out = refs[-1]
    low = 0
    for x in refs[:-1]:
        rows = x.shape[0]
        out[low : low + rows, :] = x[...].astype(f32)
        low += rows


def widen(parts, step=512):
    rows = sum(part.shape[0] for part in parts)
    columns = parts[0].shape[1]
    return pl.pallas_call(
        widen_kernel,
        grid=(columns // step,),
        out_shape=shaped((rows, columns), f32),
        in_specs=[pl.BlockSpec((part.shape[0], step), lambda j: (0, j)) for part in parts],
        out_specs=pl.BlockSpec((rows, step), lambda j: (0, j)),
        compiler_params=pltpu.CompilerParams(vmem_limit_bytes=16 << 20),
        cost_estimate=brief(),
        name="widen",
    )(*parts)


def settle_two_kernel(inner, own, came, above, below):
    rows = above.shape[0]

    @pl.when(inner[0] == 1)
    def _():
        above[...] = own[:rows, :].astype(f32)
        below[...] = own[rows:, :].astype(f32)

    @pl.when(inner[0] == 0)
    def _():
        above[...] = came[:rows, :].astype(f32)
        below[...] = came[rows:, :].astype(f32)


def settle_two(inner, own, came, rows):
    total, columns = own.shape
    return call(
        settle_two_kernel,
        [shaped((rows, columns), f32), shaped((total - rows, columns), f32)],
        [inner, own, came],
        "settle_two",
        scalars=1,
    )


def rotated(first, second, cosine, sine):
    return first * cosine - second * sine, second * cosine + first * sine


def enter_kernel(rank, width, x, gain, down, latent_gain, key, value, cosine, sine, *outs):
    normed, latent, packed = outs
    half = width // 2
    rows = x[...].astype(f32)
    low = (rows * inverse_rms(rows) * gain[...]).astype(bf16)
    normed[...] = low
    inner = dot(low, down[...])
    latent[...] = inner
    packed[:, :rank] = (inner * inverse_rms(inner) * latent_gain[...]).astype(bf16)
    keys = dot(low, key[...])
    first, second = rotated(keys[:, :half], keys[:, half:], cosine[...], sine[...])
    packed[:, rank : rank + half] = first.astype(bf16)
    packed[:, rank + half : rank + width] = second.astype(bf16)
    packed[:, rank + width :] = dot(low, value[...]).astype(bf16)


def enter(x, gain, down, latent_gain, key, value, cosine, sine):
    rows, dim = x.shape
    rank, width = down.shape[1], key.shape[1]
    return call(
        functools.partial(enter_kernel, rank, width),
        [shaped((rows, dim), bf16), shaped((rows, rank), f32), shaped((rows, rank + 2 * width), bf16)],
        [x, gain[None], down, latent_gain[None], key, value, cosine, sine],
        "enter",
        limit=60,
    )


def summed(parts):
    total = parts[0][...].astype(f32)
    for part in parts[1:]:
        total = total + part[...].astype(f32)
    return total


def middle_kernel(x, gain, *refs):
    parts, (middle, normed) = refs[:-2], refs[-2:]
    total = x[...].astype(f32) + summed(parts)
    middle[...] = total
    normed[...] = (total * inverse_rms(total) * gain[...]).astype(bf16)


def middle_rows(x, gain, parts):
    shape = x.shape
    return call(
        middle_kernel,
        [shaped(shape, f32), shaped(shape, bf16)],
        [x, gain[None], *parts],
        "middle_rows",
    )


def lower_norm(value, gain, upper):
    scale = inverse_rms(value)
    scaled = upper * gain
    lower = scale * scaled - value * (scale * scale * scale) * jnp.mean(
        scaled * value, axis=-1, keepdims=True
    )
    return lower, jnp.sum(upper * value * scale, axis=0, keepdims=True)


def middle_back_kernel(middle, gain, cotangent, *refs):
    parts, (total, low, gain_part) = refs[:-3], refs[-3:]
    lower, gain_part[...] = lower_norm(middle[...], gain[...], summed(parts))
    result = cotangent[...].astype(f32) + lower
    total[...] = result
    low[...] = result.astype(bf16)


def middle_back(middle, gain, cotangent, parts):
    shape = middle.shape
    return call(
        middle_back_kernel,
        [shaped(shape, f32), shaped(shape, bf16), shaped((1, shape[1]), f32)],
        [middle, gain[None], cotangent, *parts],
        "middle_back",
    )


def latent_back_kernel(latent, gain, cosine, sine, *refs):
    parts, (packed, gain_part) = refs[:-2], refs[-2:]
    rank = latent.shape[1]
    total = summed(parts)
    lower, gain_part[...] = lower_norm(latent[...], gain[...], total[:, :rank])
    width = (total.shape[1] - rank) // 2
    half = width // 2
    packed[:, :rank] = lower.astype(bf16)
    first, second = rotated(
        total[:, rank : rank + half], total[:, rank + half : rank + width], cosine[...], -sine[...]
    )
    packed[:, rank : rank + half] = first.astype(bf16)
    packed[:, rank + half : rank + width] = second.astype(bf16)
    packed[:, rank + width :] = total[:, rank + width :].astype(bf16)


def latent_back(latent, gain, cosine, sine, parts):
    shape = parts[0].shape
    return call(
        latent_back_kernel,
        [shaped(shape, bf16), shaped((1, latent.shape[1]), f32)],
        [latent, gain[None], cosine, sine, *parts],
        "latent_back",
    )


def leave_kernel(packed, down, key, value, x, gain, upper, result, gain_part):
    rank, width = down.shape[1], key.shape[1]
    total = right_transposed(packed[:, :rank], down[...])
    total = total + right_transposed(packed[:, rank : rank + width], key[...])
    total = total + right_transposed(packed[:, rank + width :], value[...])
    lower, gain_part[...] = lower_norm(x[...].astype(f32), gain[...], total)
    result[...] = upper[...] + lower


def leave(packed, down, key, value, x, gain, upper):
    return call(
        leave_kernel,
        [shaped(x.shape, f32), shaped((1, x.shape[1]), f32)],
        [packed, down, key, value, x, gain[None], upper],
        "leave",
    )


def shared_kernel(count, table, normed, grads, *outs):
    rows = outs[0].shape[0]
    for r in range(count):
        there = pl.ds(pl.multiple_of(table[r] * rows, rows), rows)
        outs[r][...] = left_transposed(normed[:, there], grads[...]).astype(bf16)


def shared_shares(table, normed, grads):
    count = table.shape[0]
    rows = normed.shape[1] // count
    columns = grads.shape[1]
    return list(
        pl.pallas_call(
            functools.partial(shared_kernel, count),
            out_shape=[jax.ShapeDtypeStruct((rows, columns), bf16)] * count,
            in_specs=[smem(), vmem(), vmem()],
            out_specs=[vmem()] * count,
            compiler_params=pltpu.CompilerParams(vmem_limit_bytes=36 << 20),
            cost_estimate=brief(),
            name="shared_shares",
        )(table, normed, grads)
    )


def unpack_kernel(base, count, parts, packed, table, *refs):
    pieces = refs[:count]
    outs, buffers = refs[-1 - 2 * len(parts) : -1 - len(parts)], refs[-1 - len(parts) : -1]
    sems = refs[-1]
    rows = buffers[0].shape[1]
    tall = rows * 3 // 4
    columns = parts[-1][1]
    third = columns // 3
    flying = []
    for r in range(count):
        slot = r % 2
        if r >= 2:
            for copy in flying[r - 2]:
                copy.wait()
        there = pl.ds(pl.multiple_of(table[base + r] * rows, rows), rows)
        copies = []
        for k, (low, high) in enumerate(parts):
            if packed:
                buffers[k][slot, :tall, :] = pieces[r][:, low:high].astype(f32)
                for j in range(3):
                    first, last = max(low, j * third), min(high, (j + 1) * third)
                    if first < last:
                        start = columns - j * third
                        buffers[k][slot, tall:, first - low : last - low] = pieces[r][
                            j * (rows - tall) : (j + 1) * (rows - tall),
                            start + first : start + last,
                        ].astype(f32)
            else:
                buffers[k][slot] = pieces[r][:, low:high].astype(f32)
            copy = pltpu.make_async_copy(
                buffers[k].at[slot], outs[k].at[there, :], sems.at[k, slot]
            )
            copy.start()
            copies.append(copy)
        flying.append(copies)
    for copies in flying[-2:]:
        for copy in copies:
            copy.wait()


def unpack(table, pieces, parts, packed, first=0, past=None):
    count = len(pieces)
    rows = pieces[0].shape[0]
    if packed:
        rows = rows * 4 // 3
    past = [] if past is None else list(past)
    return pl.pallas_call(
        functools.partial(unpack_kernel, first, count, parts, packed),
        out_shape=[
            jax.ShapeDtypeStruct((table.shape[0] * rows, high - low), f32) for low, high in parts
        ],
        in_specs=[smem()] + [vmem()] * count + [any_space()] * len(past),
        out_specs=[any_space()] * len(parts),
        scratch_shapes=[pltpu.VMEM((2, rows, high - low), f32) for low, high in parts]
        + [pltpu.SemaphoreType.DMA((len(parts), 2))],
        input_output_aliases={1 + count + k: k for k in range(len(past))},
        compiler_params=pltpu.CompilerParams(vmem_limit_bytes=24 << 20),
        cost_estimate=brief(),
        name="unpack",
    )(table, *pieces, *past)


def body(
    packs,
    group,
    block_input,
    segment_ids,
    positions,
    attention_gain,
    query_down,
    query_gain,
    query_up,
    key_proj,
    value_proj,
    out_proj,
    feed_gain,
    gate_weight,
    up_weight,
    down_weight,
    out_grad,
):
    plane = Plane(group)
    line = Line(packs)
    rows = block_input.shape[1]
    segments = segment_ids[0]
    places = positions[0]
    width = key_proj.shape[1]
    rank = query_down.shape[1]
    heads = query_up.shape[1] // width
    scale = 1.0 / math.sqrt(width)
    first_row = plane.me * rows

    gate_rows, up_rows = gate_weight.T, up_weight.T
    clock = Clock()
    belt = Belt(line, clock)
    fast = plane.fast
    move = plane.move
    hop_a, hop_b, hop_c = (plane.hop_a, plane.hop_b, plane.hop_c) if fast else (None,) * 3
    cotangent_rows = out_grad[0]

    x = block_input[0]
    dim = x.shape[1]
    always = (segments[0] & 1) <= 1

    def stage(run):
        def inside():
            inner = Clock()
            inner.last = clock.last
            return tuple(run(inner))

        if not fast:
            return inside()
        shapes = jax.eval_shape(inside)
        result = lax.cond(
            always, inside, lambda: tuple(jnp.zeros(one.shape, one.dtype) for one in shapes)
        )
        return clock.all(*result)

    def hops(values, ways, filler=None, apart=False):
        def run(clock):
            held = clock.all(*values)
            came = [move(value, way) for value, way in zip(held, ways)]
            more = list(filler(clock, *came)) if filler else []
            return [*clock.all(*came), *more]

        result = stage(run) if apart else run(clock)
        return list(result[: len(values)]), list(result[len(values) :])

    def gather(rows, first=None, second=None, apart=False, between=None, last=False):
        def beside(clock, a, b, s_o):
            return first(clock, [rows, clock(s_o)]) if first else []

        (a, b, s_o), more = hops([rows, rows, rows], [hop_a, hop_b, hop_c], beside, apart)
        if between:
            between()

        def beside(clock, c, a_o, b_o):
            if not second:
                return []
            a_o, b_o = clock(a_o, b_o)
            return second(clock, [a, a_o, b, b_o], more)

        (c, a_o, b_o), later = hops([a, a, b], [hop_b, hop_c, hop_c], beside, apart)
        (c_o,), _ = hops([c], [hop_c], None, apart or last)
        return [rows, s_o, a, a_o, b, b_o, c, c_o], more, later

    def scatter(share, filler=None, apart=False, between=None):
        c, c_send = clock(*share(clock, 6, 8))
        (c_came,), near = hops(
            [c_send], [hop_c], lambda clock, came: clock(*share(clock, 2, 6)), apart
        )
        a, a_send, b, b_send = near
        c = clock(add_rows(c, c_came))
        (c_in, a_came, b_came), (own, own_send) = hops(
            [c, a_send, b_send],
            [hop_b, hop_c, hop_c],
            lambda clock, *came: clock(*share(clock, 0, 2)),
            apart,
        )
        a, b = clock(add_rows(a, a_came, c_in), add_rows(b, b_came))
        if between:
            between()
        (a_in, b_in, own_came), more = hops(
            [a, b, own_send],
            [hop_a, hop_b, hop_c],
            (lambda clock, *came: filler(clock)) if filler else None,
            apart,
        )
        return [own, own_came, b_in, a_in], more

    own_places = lax.dynamic_slice_in_dim(places, first_row, rows, 0)
    own_cosine, own_sine = rotation(own_places, width)

    def enter_rows():
        return enter(
            x, attention_gain, query_down, query_gain, key_proj, value_proj, own_cosine, own_sine
        )

    def attend(pieces, cosine, sine):
        return attend_forward(
            plane.table, pieces, query_up, cosine, sine, segments, heads, width, scale
        )

    def attend_back(outer):
        return attend_backward(
            plane.table, outer, queries, keys, values, cosine, sine, segments, heads, scale
        )

    def leave_rows(packed_grad):
        return leave(
            packed_grad, query_down, key_proj, value_proj, x, attention_gain, middle_grad
        )

    def sum_gains(parts, total):
        return total(jnp.concatenate(parts, axis=1))

    units = gate_rows.shape[0]
    size = heads * width
    columns = ((0, rank), (rank, rank + width), (rank + width, rank + 2 * width))
    add = lambda left, right: left + right

    if not fast:
        normed_rows, latent, packed = enter_rows()
        cosine, sine = rotation(places, width)
        pieces = plane.gather(packed)
        latents, queries, keys, values, mixed_there = attend(pieces, cosine, sine)
        share = shares([mixed_there], [out_proj], group)
        parts = [plane.scatter(share(clock, 0, group))]
        middle, normed_mid_rows = middle_rows(x, feed_gain, parts)
        cot_pieces = plane.gather(cotangent_rows)
        hidden_grad = rows_product(cot_pieces, down_weight, f32)
        mid_pieces = plane.gather(normed_mid_rows)
        hidden, gate_grad, upward_grad = feed(
            mid_pieces, 0, group, hidden_grad, gate_rows, up_rows, group, None
        )
        cotangent, normed_mid = join(cot_pieces), join(mid_pieces)
        share = shares([gate_grad, upward_grad], [gate_rows, up_rows], group)
        parts = [plane.scatter(share(clock, 0, group))]
        middle_grad, attention_grad, feed_gain_part = middle_back(
            middle, feed_gain, cotangent_rows, parts
        )
        grad_pieces = plane.gather(attention_grad)
        outer = [rows_product(grad_pieces, out_proj, bf16)]
        query_pre_grad, pair_grads = attend_back(outer)
        share = latent_shares(plane.table, query_pre_grad, pair_grads, query_up)
        parts = [plane.scatter(share(clock, 0, group))]
        packed_grad, query_gain_part = latent_back(latent, query_gain, own_cosine, own_sine, parts)
        shared_pieces = shared_shares(plane.table, normed_rows, packed_grad)
        shared = line.total(plane.scatter(list(shared_pieces)).astype(bf16))
        query_down_gradient, key_proj_gradient, value_proj_gradient = unpack(
            plane.table, plane.gather(shared), columns, False
        )
        input_gradient, attention_gain_part = leave_rows(packed_grad)
        share = shares([hidden], [down_weight], group)
        block_output = add_rows(middle, plane.scatter(share(clock, 0, group)))
        gains = sum_gains([attention_gain_part, query_gain_part, feed_gain_part], plane.total)
        gains = line.total(gains, add)[0]
        down_gradient, gate_gradient, up_gradient, proj_gradient, query_up_gradient = (
            line.total(weight_product(left, right, [left.shape[1]])[0]).astype(f32)
            for left, right in (
                (hidden, cotangent),
                (gate_grad, normed_mid),
                (upward_grad, normed_mid),
                (mixed_there, join(grad_pieces)),
                (latents, query_pre_grad),
            )
        )
    else:
        half = units // 2
        cot_a = move(cotangent_rows, hop_a)
        normed_rows, latent, packed = enter_rows()
        packed = clock(packed)

        def angles(clock, own):
            return clock(*rotation(clock(places), width))

        pieces, (cosine, sine), _ = gather(packed, angles, apart=True)
        cot_now, cot_a = clock(cotangent_rows, cot_a)
        cot_b, cot_c = move(cot_now, hop_b), move(cot_a, hop_b)
        cot_o, cot_ao = move(cot_now, hop_c), move(cot_a, hop_c)
        pieces[0] = clock(packed)

        latents, queries, keys, values, mixed_there = clock(*attend(pieces, cosine, sine))
        share = shares([mixed_there], [out_proj], group)
        c, c_send = clock(*share(clock, 6, 8))
        a, a_send, b, b_send = clock(*share(clock, 2, 6))
        own, own_send = clock(*share(clock, 0, 2))
        cot_b, cot_c, cot_o, cot_ao = clock(cot_b, cot_c, cot_o, cot_ao)
        (c_came,), _ = hops([c_send], [hop_c])
        c = clock(add_rows(c, c_came))
        (c_in, a_came, b_came), _ = hops([c, a_send, b_send], [hop_b, hop_c, hop_c])
        a, b = clock(add_rows(a, a_came, c_in), add_rows(b, b_came))

        def beside_last(clock, a_in, b_in, own_came, cot_bo, cot_co):
            cot_bo, cot_co = clock(cot_bo, cot_co)
            cot_pieces = [cotangent_rows, cot_o, cot_a, cot_ao, cot_b, cot_bo, cot_c, cot_co]
            hidden_grad = clock(rows_product(cot_pieces, down_weight, f32))
            return [hidden_grad]

        (a_in, b_in, own_came, cot_bo, cot_co), (hidden_grad,) = hops(
            [a, b, own_send, cot_b, cot_c], [hop_a, hop_b, hop_c, hop_c, hop_c], beside_last
        )
        cot_pieces = [cotangent_rows, cot_o, cot_a, cot_ao, cot_b, cot_bo, cot_c, cot_co]
        middle, normed_mid_rows = clock(*middle_rows(x, feed_gain, [own, own_came, b_in, a_in]))

        def feed_group(clock, pieces, low, high, past):
            pieces = [None] * low + [clock(pieces[0]), *pieces[1:]]
            return clock(
                *feed(pieces, low, high, hidden_grad, gate_rows, up_rows, group, past)
            )

        def near_feed(clock, near):
            return feed_group(clock, near, 0, 2, None)

        (a, b, s_o), past = hops(
            [normed_mid_rows] * 3,
            [hop_a, hop_b, hop_c],
            lambda clock, a, b, s_o: near_feed(clock, [normed_mid_rows, clock(s_o)]),
        )

        def next_feed(clock, c, a_o, b_o):
            a_o, b_o = clock(a_o, b_o)
            return [a_o, b_o, *feed_group(clock, [a, a_o], 2, 4, past)]

        (c, a_o, b_o), past = hops([a, a, b], [hop_b, hop_c, hop_c], next_feed)
        a_o, b_o, *past = past
        (c_o,), past = hops(
            [c], [hop_c], lambda clock, c_o: feed_group(clock, [b, b_o], 4, 6, past)
        )
        hidden, gate_grad, upward_grad = feed_group(clock, [c, c_o], 6, 8, past)
        mid_pieces = [normed_mid_rows, s_o, a, a_o, b, b_o, c, c_o]
        chunk = units * 3 // 4
        tall = dim * 3 // (4 * group)
        beside = chunk - tall
        one, tail = clock(*weight_product(clock(hidden), cot_pieces, [chunk, units - chunk]))
        one = belt.begin(one)
        two = []

        def middle_filler(clock):
            part, rest = clock(
                *weight_product(clock(gate_grad), mid_pieces, [chunk, units - half], tail)
            )
            two.append(belt.begin(part))
            return [rest]

        share = shares([gate_grad, upward_grad], [gate_rows, up_rows], group)
        parts, (tail,) = scatter(share, middle_filler)
        two = two[0]
        belt.cross(one)
        middle_grad, attention_grad, feed_gain_part = clock(
            *middle_back(middle, feed_gain, cotangent_rows, parts)
        )

        def near_grad(clock, near):
            outer = clock(rows_product([clock(near[0]), near[1]], out_proj, bf16))
            pair = clock(*weight_product(clock(upward_grad), mid_pieces, [chunk, chunk], tail))
            return [outer, *pair]

        def next_grad(clock, near, more):
            return [clock(rows_product([clock(near[0]), *near[1:]], out_proj, bf16))]

        grad_pieces, (outer_near, three, four), (outer_next,) = gather(
            attention_grad, near_grad, next_grad, last=True
        )
        outer_last = clock(rows_product([clock(grad_pieces[6]), grad_pieces[7]], out_proj, bf16))
        three = belt.back(one, three)
        belt.cross(two)

        query_pre_grad, pair_grads = clock(*attend_back([outer_near, outer_next, clock(outer_last)]))

        def latent_filler(clock):
            return clock(
                *weight_product(clock(mixed_there), grad_pieces, [beside, size - beside])
            )

        share = latent_shares(plane.table, query_pre_grad, pair_grads, query_up)
        parts, (five, six) = scatter(share, latent_filler)
        packed_grad, query_gain_part = clock(
            *latent_back(latent, query_gain, own_cosine, own_sine, parts)
        )
        belt.cross(three)
        four = belt.back(two, four)

        shared_pieces = clock(*shared_shares(plane.table, normed_rows, packed_grad))

        def shared_filler(clock):
            leaving = clock(*leave_rows(clock(packed_grad)))
            product = clock(weight_product(clock(latents), query_pre_grad, [rank])[0])
            belt.land(one)
            return [*leaving, product, clock(belt.end(one, units))]

        parts, (input_gradient, attention_gain_part, query_sum, down_gradient) = scatter(
            lambda clock, low, high: shared_pieces[low:high], shared_filler
        )
        five = clock(pack(parts, five))
        five = belt.back(three, five)
        belt.cross(four)
        fill = -(2 * dim + rank) % (16 * dim)

        def gain_rows(clock):
            gains = sum_gains(
                [clock(attention_gain_part), query_gain_part, feed_gain_part], plane.total
            )
            gains = jnp.concatenate([gains[0], jnp.zeros((fill,), f32)]).reshape(-1, dim)
            return [pack_last(six, query_sum, gains.astype(bf16))]

        (six,) = stage(gain_rows)

        settled = []

        def turn():
            belt.cross(five)
            belt.back(four)
            begun = belt.begin(six)
            belt.land(two)
            down = clock(belt.end(two, units, chunk, down_gradient, 0, units - chunk))
            gate = clock(belt.end(two, units, 0, None, units - chunk))
            belt.land(three)
            gate = clock(belt.end(three, units, half, gate, 0, half))
            up = clock(belt.end(three, units, 0, None, half))
            belt.land(four)
            belt.back(five)
            belt.cross(begun)
            settled.extend([begun, down, gate, up])

        share = shares([hidden], [down_weight], group)
        parts, _ = scatter(share, None, True, turn)
        block_output = clock(add_rows(middle, *parts))
        six, down_gradient, gate_gradient, up_gradient = settled
        up_gradient = clock(belt.end(four, units, chunk - half, up_gradient))
        belt.meet(six)
        belt.land(five)
        belt.send(six)
        shared_rows = clock(pick(belt.inner, five["own"], five["came"], tall))

        def five_end(clock, own):
            held = dict(five, came=clock(five["came"]))
            return [clock(belt.end(held, size, 0, None, tall))]

        def near_unpack(clock, near, more):
            pieces = [shared_rows, s_one, *near]
            return clock(*unpack(plane.table, pieces, columns, True))

        (a, b, s_one), (proj_gradient,) = hops(
            [shared_rows] * 3, [hop_a, hop_b, hop_c], lambda clock, *came: five_end(clock, None), True
        )

        def beside_next(clock, c, a_o, b_o):
            a_o, b_o = clock(a_o, b_o)
            return near_unpack(clock, [a, a_o, b, b_o], None)

        (c, a_o, b_o), past = hops([a, a, b], [hop_b, hop_c, hop_c], beside_next, True)
        (c_o,), _ = hops([c], [hop_c], None, True)
        query_down_gradient, key_proj_gradient, value_proj_gradient = clock(
            *unpack(plane.table, [c, c_o], columns, True, 6, past)
        )
        belt.land(six)
        query_up_gradient, gains, proj_gradient = settle_last(
            belt.inner, six["own"], six["came"], size - beside, rank, size, proj_gradient, beside
        )
        gains = gains.reshape(-1)
    return (
        block_output[None],
        input_gradient[None],
        gains[:dim],
        query_down_gradient,
        gains[dim : dim + rank],
        query_up_gradient,
        key_proj_gradient,
        value_proj_gradient,
        proj_gradient,
        gains[dim + rank : dim + rank + dim],
        gate_gradient.T,
        up_gradient.T,
        down_gradient,
    )


def solution(mesh):
    in_specs = (
        P("tok", "head", None),
        P("tok", None),
        P("tok", None),
        P(),
        P(),
        P(),
        P(None, "head"),
        P(),
        P(),
        P("head", None),
        P(),
        P(None, "head"),
        P(None, "head"),
        P("head", None),
        P("tok", "head", None),
    )
    out_specs = (
        P("tok", "head", None),
        P("tok", "head", None),
        P(),
        P(),
        P(),
        P(None, "head"),
        P(),
        P(),
        P("head", None),
        P(),
        P(None, "head"),
        P(None, "head"),
        P("head", None),
    )
    sizes = dict(mesh.shape)
    return jax.shard_map(
        functools.partial(body, sizes["tok"], sizes["head"]),
        mesh=mesh,
        in_specs=in_specs,
        out_specs=out_specs,
        check_vma=False,
    )
```

```python
import functools
import math

import jax
import jax.numpy as jnp
from jax import lax
from jax.experimental import pallas as pl
from jax.experimental.pallas import tpu as pltpu
from jax.sharding import PartitionSpec as P

norm_epsilon = 1e-05
rope_base = 10000.0
first_document = 1024
bf16 = jnp.bfloat16
f32 = jnp.float32


def inverse_rms(value):
    return lax.rsqrt(jnp.mean(value * value, axis=-1, keepdims=True) + norm_epsilon)


def norm_backward(value, gain, upper):
    scale = inverse_rms(value)
    scaled = upper * gain
    lower = scale * scaled - value * (scale * scale * scale) * jnp.mean(
        scaled * value, axis=-1, keepdims=True
    )
    return (lower, jnp.sum(upper * value * scale, axis=0))


def rotation(places, head_width):
    half = head_width // 2
    steps = jnp.arange(half).astype(f32) * (2.0 / head_width)
    inverse = jnp.exp(steps * -math.log(rope_base))
    angles = places.astype(f32)[:, None] * inverse[None, :]
    return (jnp.cos(angles), jnp.sin(angles))


def rotate(value, cosine, sine):
    half = value.shape[-1] // 2
    first = value[..., :half]
    second = value[..., half:]
    return jnp.concatenate(
        [first * cosine - second * sine, second * cosine + first * sine], axis=-1
    )


def dot(left, right):
    return jnp.dot(left, right, preferred_element_type=f32)


def right_transposed(left, right):
    return lax.dot_general(left, right, (((1,), (1,)), ((), ())), preferred_element_type=f32)


def left_transposed(left, right):
    return lax.dot_general(left, right, (((0,), (0,)), ((), ())), preferred_element_type=f32)


def add_low(left, right):
    return (left.astype(f32) + right.astype(f32)).astype(bf16)


class Clock:
    def __init__(self):
        self.last = ()

    def all(self, *values):
        held = lax.optimization_barrier(values + self.last)
        self.last = (held[0],)
        return held[: len(values)]

    def __call__(self, *values):
        held = self.all(*values)
        return held[0] if len(values) == 1 else held


class Plane:
    def __init__(self, size):
        self.size = size
        self.fast = size == 8 and lax.axis_size("tok") == 4
        self.me = lax.axis_index("head")
        if self.fast:
            even = [index % 2 == 0 for index in range(size)]
            self.hop_a = [(i, i ^ (2 if even[i] else 4)) for i in range(size)]
            self.hop_b = [(i, i ^ (4 if even[i] else 2)) for i in range(size)]
            self.hop_c = [(i, i ^ 1) for i in range(size)]
            mask_a = jnp.where(self.me % 2 == 0, 2, 4)
            other = self.me ^ 1
            order = [
                self.me,
                other,
                self.me ^ mask_a,
                other ^ (6 - mask_a),
                self.me ^ (6 - mask_a),
                other ^ mask_a,
                self.me ^ 6,
                other ^ 6,
            ]
            self.table = jnp.stack(order).astype(jnp.int32)
            self.groups = [(0, 2), (2, 6), (6, 8)]
        else:
            self.table = jnp.arange(size, dtype=jnp.int32)
            self.groups = [(0, size)]

    def move(self, value, hop):
        return lax.ppermute(value, "head", hop)

    def gather(self, rows):
        whole = lax.all_gather(rows, "head", axis=0, tiled=True)
        return list(jnp.split(whole, self.size, axis=0))

    def scatter(self, pieces):
        whole = jnp.concatenate(pieces, axis=0)
        return lax.psum_scatter(whole, "head", scatter_dimension=0, tiled=True).astype(f32)

    def total(self, value):
        if not self.fast:
            return lax.psum(value, "head")
        for bit in (1, 2, 4):
            value = value + self.move(value, [(i, i ^ bit) for i in range(8)])
        return value


class Line:
    def __init__(self, size):
        self.size = size
        self.me = lax.axis_index("tok")
        half = size // 2
        self.stages = [([(k, k + 1), (size - 1 - k, size - 2 - k)], None) for k in range(half - 1)]
        self.stages.append(([(half - 1, half), (half, half - 1)], None))
        for k in reversed(range(half - 1)):
            self.stages.append(([(k + 1, k), (size - 2 - k, size - 1 - k)], k))

    def start(self, stage, value):
        return lax.ppermute(value, "tok", self.stages[stage][0])

    def finish(self, stage, value, came, plus=add_low):
        outward = self.stages[stage][1]
        if outward is None:
            return plus(value, came)
        mine = (self.me == outward) | (self.me == self.size - 1 - outward)
        return jnp.where(mine, came, value)

    def total(self, value, plus=add_low):
        for stage in range(len(self.stages)):
            value = self.finish(stage, value, self.start(stage, value), plus)
        return value


class Belt:
    inward = [(0, 1), (3, 2)]
    middle = [(1, 2), (2, 1)]
    outward = [(1, 0), (2, 3)]

    def __init__(self, line, clock):
        self.clock = clock
        self.inner = jnp.where((line.me == 1) | (line.me == 2), 1, 0).astype(jnp.int32).reshape(1)

    def move(self, value, pairs):
        return lax.ppermute(value, "tok", pairs)

    def begin(self, value):
        value = self.clock(value)
        return {"own": value, "came": self.move(value, self.inward)}

    def cross(self, item):
        item["came"] = self.clock(item["came"])
        item["own"] = self.clock(add_rows(item["own"], item["came"]))
        item["came"] = self.move(item["own"], self.middle)

    def meet(self, item):
        item["came"] = self.clock(item["came"])
        item["own"] = self.clock(add_rows(item["own"], item["came"]))

    def send(self, item):
        item["own"] = self.clock(item["own"])
        item["came"] = self.move(item["own"], self.outward)

    def back(self, item, value=None):
        if value is None:
            self.meet(item)
            self.send(item)
            return None
        item["came"] = self.clock(item["came"])
        both = self.clock(add_or_begin(self.inner, item["own"], item["came"], value))
        came = self.move(both, self.inward + self.outward)
        item["own"], item["came"] = both, came
        return {"own": value, "came": came}

    def land(self, item):
        item["came"] = self.clock(item["came"])

    def end(self, item, size, at=0, past=None, low=0, high=None):
        return settle(self.inner, item["own"], item["came"], size, at, past, low, high)


def query_blocks(length):
    first = min(length, max(first_document, length // 2))
    block = 256
    return [
        (start, min(block, length - start), 0 if start < first else first)
        for start in range(0, length, block)
    ]


def allowed(seg_column, seg_row, start, rows, low, high):
    query_order = start + lax.broadcasted_iota(jnp.int32, (rows, high - low), 0)
    key_order = low + lax.broadcasted_iota(jnp.int32, (rows, high - low), 1)
    same = seg_column[start : start + rows, :] == seg_row[:, low:high]
    return (key_order <= query_order) & same


def weights_of(stacked, keys, permit, heads, scale):
    scores = right_transposed(stacked, keys) * scale
    scores = jnp.where(jnp.concatenate([permit] * heads, axis=0), scores, -1e30)
    top = jnp.max(scores, axis=-1, keepdims=True)
    weights = jnp.exp(scores - top)
    return weights, jnp.sum(weights, axis=-1, keepdims=True)


def stack_heads(ref, start, rows, heads, width):
    return jnp.concatenate(
        [ref[start : start + rows, h * width : (h + 1) * width] for h in range(heads)], axis=0
    )


def attend_forward_kernel(count, heads, width, rank, scale, *refs):
    table = refs[0]
    pieces = refs[1 : 1 + count]
    weight, cosine, sine, seg_column, seg_row = refs[1 + count : 6 + count]
    latents, queries_out, keys_out, values_out, mixed_there = refs[6 + count : 11 + count]
    queries, keys, values, mixed, sems = refs[11 + count :]
    length = queries.shape[0]
    leaving = []

    def leave_now(source, target):
        copy = pltpu.make_async_copy(source, target, sems.at[len(leaving)])
        copy.start()
        leaving.append(copy)

    rows = length // count
    half = width // 2
    for r in range(count):
        there = pl.ds(pl.multiple_of(table[r] * rows, rows), rows)
        leave_now(pieces[r].at[:, :rank], latents.at[there, :])
        keys[there, :] = pieces[r][:, rank : rank + width]
        values[there, :] = pieces[r][:, rank + width :]
        flat = dot(pieces[r][:, :rank], weight[...])
        cos = cosine[there, :]
        sin = sine[there, :]
        for h in range(heads):
            first = flat[:, h * width : h * width + half]
            second = flat[:, h * width + half : (h + 1) * width]
            queries[there, h * width : h * width + half] = (first * cos - second * sin).astype(bf16)
            queries[there, h * width + half : (h + 1) * width] = (
                second * cos + first * sin
            ).astype(bf16)
    leave_now(queries, queries_out)
    leave_now(keys, keys_out)
    leave_now(values, values_out)
    for start, size, low in query_blocks(length):
        high = start + size
        stacked = stack_heads(queries, start, size, heads, width)
        permit = allowed(seg_column, seg_row, start, size, low, high)
        weights, total = weights_of(stacked, keys[low:high, :], permit, heads, scale)
        probs = (weights / total).astype(bf16)
        result = dot(probs, values[low:high, :]).astype(bf16)
        for h in range(heads):
            mixed[start:high, h * width : (h + 1) * width] = result[h * size : (h + 1) * size]
    for r in range(count):
        there = pl.ds(pl.multiple_of(table[r] * rows, rows), rows)
        mixed_there[r * rows : (r + 1) * rows, :] = mixed[there, :]
    for copy in leaving:
        copy.wait()


def brief():
    return pl.CostEstimate(flops=1024, bytes_accessed=1024, transcendentals=0)


def vmem():
    return pl.BlockSpec(memory_space=pltpu.VMEM)


def smem():
    return pl.BlockSpec(memory_space=pltpu.SMEM)


def attend_forward(table, pieces, weight, cosine, sine, segments, heads, width, scale):
    count = len(pieces)
    length = cosine.shape[0]
    rank = weight.shape[0]
    shapes = [
        jax.ShapeDtypeStruct((length, rank), bf16),
        jax.ShapeDtypeStruct((length, heads * width), bf16),
        jax.ShapeDtypeStruct((length, width), bf16),
        jax.ShapeDtypeStruct((length, width), bf16),
        jax.ShapeDtypeStruct((length, heads * width), bf16),
    ]
    return pl.pallas_call(
        functools.partial(attend_forward_kernel, count, heads, width, rank, scale),
        out_shape=shapes,
        in_specs=[smem()] + [vmem()] * (count + 5),
        out_specs=[any_space()] * 4 + [vmem()],
        scratch_shapes=[
            pltpu.VMEM((length, heads * width), bf16),
            pltpu.VMEM((length, width), bf16),
            pltpu.VMEM((length, width), bf16),
            pltpu.VMEM((length, heads * width), bf16),
            pltpu.SemaphoreType.DMA((count + 3,)),
        ],
        compiler_params=pltpu.CompilerParams(vmem_limit_bytes=48 << 20),
        cost_estimate=brief(),
        name="attend_forward",
    )(table, *pieces, weight, cosine, sine, segments[:, None], segments[None, :])


def attend_backward_kernel(parts, heads, width, scale, *refs):
    table = refs[0]
    grads_in = refs[1 : 1 + parts]
    queries, keys, values, cosine, sine, seg_column, seg_row = refs[1 + parts : 8 + parts]
    query_out, pair_out, outer, key_total, value_total = refs[8 + parts :]
    length = queries.shape[0]
    count = table.shape[0]
    rows = length // count
    half = width // 2

    def there(r):
        return pl.ds(pl.multiple_of(table[r] * rows, rows), rows)

    r = 0
    for part in grads_in:
        for k in range(part.shape[0] // rows):
            outer[there(r), :] = part[k * rows : (k + 1) * rows, :]
            r += 1
    key_total[...] = jnp.zeros_like(key_total)
    value_total[...] = jnp.zeros_like(value_total)
    for start, size, low in query_blocks(length):
        high = start + size
        stacked = stack_heads(queries, start, size, heads, width)
        grads = stack_heads(outer, start, size, heads, width)
        permit = allowed(seg_column, seg_row, start, size, low, high)
        weights, total = weights_of(stacked, keys[low:high, :], permit, heads, scale)
        probs = weights / total
        prob_grad = right_transposed(grads, values[low:high, :])
        centre = jnp.sum(probs * prob_grad, axis=-1, keepdims=True)
        score_grad = (probs * (prob_grad - centre)).astype(bf16)
        query_grad = dot(score_grad, keys[low:high, :]) * scale
        key_total[low:high, :] += left_transposed(score_grad, stacked) * scale
        value_total[low:high, :] += left_transposed(probs.astype(bf16), grads)
        cos = cosine[start:high, :]
        sin = sine[start:high, :]
        for h in range(heads):
            first = query_grad[h * size : (h + 1) * size, :half]
            second = query_grad[h * size : (h + 1) * size, half:]
            query_out[start:high, h * width : h * width + half] = (
                first * cos + second * sin
            ).astype(bf16)
            query_out[start:high, h * width + half : (h + 1) * width] = (
                second * cos - first * sin
            ).astype(bf16)
    pair_out[:, :width] = key_total[...].astype(bf16)
    pair_out[:, width:] = value_total[...].astype(bf16)


def attend_backward(table, grads, queries, keys, values, cosine, sine, segments, heads, scale):
    parts = len(grads)
    length, width = keys.shape
    shapes = [
        jax.ShapeDtypeStruct((length, heads * width), bf16),
        jax.ShapeDtypeStruct((length, 2 * width), bf16),
    ]
    return pl.pallas_call(
        functools.partial(attend_backward_kernel, parts, heads, width, scale),
        out_shape=shapes,
        in_specs=[smem()] + [vmem()] * (parts + 7),
        out_specs=[vmem()] * 2,
        scratch_shapes=[
            pltpu.VMEM((length, heads * width), bf16),
            pltpu.VMEM((length, width), f32),
            pltpu.VMEM((length, width), f32),
        ],
        compiler_params=pltpu.CompilerParams(vmem_limit_bytes=44 << 20),
        cost_estimate=brief(),
        name="attend_backward",
    )(
        table,
        *grads,
        queries,
        keys,
        values,
        cosine,
        sine,
        segments[:, None],
        segments[None, :],
    )


def rows_product_kernel(*refs):
    pieces, weight, out = refs[:-2], refs[-2], refs[-1]
    rows = pieces[0].shape[0]
    for p in range(0, len(pieces), 2):
        here = jnp.concatenate([pieces[p][...], pieces[p + 1][...]], axis=0)
        out[p * rows : (p + 2) * rows, :] = right_transposed(here, weight[...]).astype(out.dtype)


def rows_product(pieces, weight, kind):
    return pl.pallas_call(
        rows_product_kernel,
        out_shape=jax.ShapeDtypeStruct(
            (len(pieces) * pieces[0].shape[0], weight.shape[0]), kind
        ),
        in_specs=[vmem()] * (len(pieces) + 1),
        out_specs=vmem(),
        compiler_params=pltpu.CompilerParams(vmem_limit_bytes=36 << 20),
        cost_estimate=brief(),
        name="rows_product",
    )(*pieces, weight)


def latent_share_kernel(low, size, table, query_grads, pairs, weight, *refs):
    outs = refs[:-3]
    held, beside, sems = refs[-3:]
    rows = outs[0].shape[0]
    rank = weight.shape[0]
    copies = []
    for k in range(size // rows):
        there = pl.ds(pl.multiple_of(table[low + k] * rows, rows), rows)
        here = pl.ds(k * rows, rows)
        copies += [
            pltpu.make_async_copy(query_grads.at[there, :], held.at[here, :], sems.at[0, k]),
            pltpu.make_async_copy(pairs.at[there, :], beside.at[here, :], sems.at[1, k]),
        ]
    for copy in copies:
        copy.start()
    for copy in copies:
        copy.wait()
    for p in range(0, size // rows, 2):
        total = right_transposed(held[p * rows : (p + 2) * rows, :], weight[...])
        for k in range(2):
            outs[p + k][:, :rank] = total[k * rows : (k + 1) * rows].astype(bf16)
            outs[p + k][:, rank:] = beside[(p + k) * rows : (p + k + 1) * rows, :]


def latent_shares(table, query_grads, pairs, weight):
    count = table.shape[0]
    rows = query_grads.shape[0] // count
    rank, inner = weight.shape
    extra = pairs.shape[1]

    def share(clock, low, high):
        size = (high - low) * rows
        return pl.pallas_call(
            functools.partial(latent_share_kernel, low, size),
            out_shape=[jax.ShapeDtypeStruct((rows, rank + extra), bf16)] * (high - low),
            in_specs=[smem(), any_space(), any_space(), vmem()],
            out_specs=[vmem()] * (high - low),
            scratch_shapes=[
                pltpu.VMEM((size, inner), bf16),
                pltpu.VMEM((size, extra), bf16),
                pltpu.SemaphoreType.DMA((2, high - low)),
            ],
            compiler_params=pltpu.CompilerParams(vmem_limit_bytes=36 << 20),
            cost_estimate=brief(),
            name="latent_share",
        )(table, *clock(query_grads, pairs), weight)

    return share


def join_kernel(count, *refs):
    pieces, whole = refs[:count], refs[count]
    rows = pieces[0].shape[0]
    for r in range(count):
        whole[r * rows : (r + 1) * rows, :] = pieces[r][...]


def join(pieces):
    count = len(pieces)
    rows, columns = pieces[0].shape
    step = min(columns, 512)
    return pl.pallas_call(
        functools.partial(join_kernel, count),
        grid=(columns // step,),
        out_shape=jax.ShapeDtypeStruct((count * rows, columns), bf16),
        in_specs=[pl.BlockSpec((rows, step), lambda j: (0, j))] * count,
        out_specs=pl.BlockSpec((count * rows, step), lambda j: (0, j)),
        compiler_params=pltpu.CompilerParams(vmem_limit_bytes=17 << 20),
        cost_estimate=brief(),
        name="join",
    )(*pieces)


def any_space():
    return pl.BlockSpec(memory_space=pl.ANY)


def share_kernel(low, size, terms, *refs):
    lefts = refs[:terms]
    weights = refs[terms : 2 * terms]
    outs = refs[2 * terms : -terms - 1]
    held, sems = refs[-terms - 1 : -1], refs[-1]
    rows = outs[0].shape[0]
    copies = []
    for t in range(terms):
        copy = pltpu.make_async_copy(lefts[t].at[pl.ds(low * rows, size), :], held[t], sems.at[t])
        copy.start()
        copies.append(copy)
    for copy in copies:
        copy.wait()
    for p in range(size // (2 * rows)):
        here = pl.ds(2 * p * rows, 2 * rows)
        total = dot(held[0][here, :], weights[0][...])
        for t in range(1, terms):
            total = total + dot(held[t][here, :], weights[t][...])
        outs[2 * p][...] = total[:rows].astype(bf16)
        outs[2 * p + 1][...] = total[rows:].astype(bf16)


def shares(lefts, weights, count):
    rows = lefts[0].shape[0] // count
    inner = lefts[0].shape[1]
    columns = weights[0].shape[1]
    terms = len(lefts)

    def share(clock, low, high):
        size = (high - low) * rows
        return pl.pallas_call(
            functools.partial(share_kernel, low, size, terms),
            out_shape=[jax.ShapeDtypeStruct((rows, columns), bf16)] * (high - low),
            in_specs=[any_space()] * terms + [vmem()] * terms,
            out_specs=[vmem()] * (high - low),
            scratch_shapes=[pltpu.VMEM((size, inner), bf16)] * terms
            + [pltpu.SemaphoreType.DMA((terms,))],
            compiler_params=pltpu.CompilerParams(vmem_limit_bytes=36 << 20),
            cost_estimate=brief(),
            name="share",
        )(*clock.all(*lefts), *weights)

    return share


def feed_kernel(pairs, first, *refs):
    pieces = refs[: 2 * pairs]
    upper, gate_weight, up_weight = refs[2 * pairs : 2 * pairs + 3]
    rest = refs[2 * pairs + 3 :]
    outs, held, buffers, sems = rest[-8:-5], rest[-5], rest[-4:-1], rest[-1]
    rows = pieces[0].shape[0]

    def rows_of(p):
        return pl.ds((first + p) * 2 * rows, 2 * rows)

    loads = []
    for p in range(pairs):
        load = pltpu.make_async_copy(upper.at[rows_of(p), :], held.at[p], sems.at[3, p])
        load.start()
        loads.append(load)
    copies = []
    for p in range(pairs):
        here = jnp.concatenate([pieces[2 * p][...], pieces[2 * p + 1][...]], axis=0)
        gate = right_transposed(here, gate_weight[...])
        upward = right_transposed(here, up_weight[...])
        loads[p].wait()
        hidden_grad = held[p]
        sigmoid = jax.nn.sigmoid(gate)
        swish = gate * sigmoid
        results = (
            swish * upward,
            hidden_grad * upward * sigmoid * (1.0 + gate * (1.0 - sigmoid)),
            hidden_grad * swish,
        )
        for k, result in enumerate(results):
            buffers[k][p] = result.astype(bf16)
            copy = pltpu.make_async_copy(buffers[k].at[p], outs[k].at[rows_of(p), :], sems.at[k, p])
            copy.start()
            copies.append(copy)
    for copy in copies:
        copy.wait()


def feed(pieces, low, high, upper, gate_weight, up_weight, count, past):
    rows, dim = pieces[low].shape
    units = gate_weight.shape[0]
    pairs = (high - low) // 2
    operands = list(pieces[low:high]) + [upper, gate_weight, up_weight]
    specs = [vmem()] * (high - low) + [any_space()] + [vmem()] * 2
    aliases = {}
    if past is not None:
        aliases = {len(operands) + k: k for k in range(3)}
        operands += list(past)
        specs += [any_space()] * 3
    size = (high - low) * rows
    return pl.pallas_call(
        functools.partial(feed_kernel, pairs, low // 2),
        out_shape=[jax.ShapeDtypeStruct((count * rows, units), bf16)] * 3,
        in_specs=specs,
        out_specs=[any_space()] * 3,
        scratch_shapes=[pltpu.VMEM((pairs, 2 * rows, units), f32)]
        + [pltpu.VMEM((pairs, 2 * rows, units), bf16)] * 3
        + [pltpu.SemaphoreType.DMA((4, pairs))],
        input_output_aliases=aliases,
        compiler_params=pltpu.CompilerParams(vmem_limit_bytes=28 << 20),
        cost_estimate=brief(),
        name="feed",
    )(*operands)


def sum_kernel(*refs):
    total = refs[0][...].astype(f32)
    for ref in refs[1:-1]:
        total = total + ref[...].astype(f32)
    refs[-1][...] = total.astype(bf16)


def call(kernel, shapes, operands, name, scalars=0, limit=24, scratch=()):
    single = not isinstance(shapes, list)
    return pl.pallas_call(
        kernel,
        out_shape=shapes,
        in_specs=[smem()] * scalars + [vmem()] * (len(operands) - scalars),
        out_specs=vmem() if single else [vmem()] * len(shapes),
        scratch_shapes=list(scratch),
        compiler_params=pltpu.CompilerParams(vmem_limit_bytes=limit << 20),
        cost_estimate=brief(),
        name=name,
    )(*operands)


def shaped(shape, kind):
    return jax.ShapeDtypeStruct(shape, kind)


def add_rows(*values):
    return call(sum_kernel, shaped(values[0].shape, bf16), values, "add_rows")


def add_or_begin_kernel(inner, own, came, value, out):
    @pl.when(inner[0] == 1)
    def _():
        out[...] = (own[...].astype(f32) + came[...].astype(f32)).astype(bf16)

    @pl.when(inner[0] == 0)
    def _():
        out[...] = value[...]


def add_or_begin(inner, own, came, value):
    return call(
        add_or_begin_kernel,
        shaped(own.shape, bf16),
        [inner, own, came, value],
        "add_or_begin",
        scalars=1,
    )


def settle_kernel(low, at, *refs):
    inner, own, came = refs[:3]
    out, buffer, sem = refs[-3:]
    rows = buffer.shape[0]

    @pl.when(inner[0] == 1)
    def _():
        buffer[...] = own[low : low + rows, :].astype(f32)

    @pl.when(inner[0] == 0)
    def _():
        buffer[...] = came[low : low + rows, :].astype(f32)

    copy = pltpu.make_async_copy(buffer, out.at[pl.ds(at, rows), :], sem)
    copy.start()
    copy.wait()


def settle(inner, own, came, size, at=0, past=None, low=0, high=None):
    columns = own.shape[1]
    rows = (high or own.shape[0]) - low
    operands = [inner, own, came]
    specs = [smem(), vmem(), vmem()]
    aliases = {}
    if past is not None:
        aliases = {3: 0}
        operands.append(past)
        specs.append(any_space())
    return pl.pallas_call(
        functools.partial(settle_kernel, low, at),
        out_shape=shaped((size, columns), f32),
        in_specs=specs,
        out_specs=any_space(),
        scratch_shapes=[pltpu.VMEM((rows, columns), f32), pltpu.SemaphoreType.DMA],
        input_output_aliases=aliases,
        compiler_params=pltpu.CompilerParams(vmem_limit_bytes=16 << 20),
        cost_estimate=brief(),
        name="settle",
    )(*operands)


def product_kernel(count, first, step, left, *refs):
    pieces = refs[:count]
    outs, held, sems = refs[count + first : -2], refs[-2], refs[-1]
    rows = pieces[0].shape[0]
    here = pl.program_id(0)
    steps = pl.num_programs(0)

    def copies(j, slot):
        there = pl.ds(pl.multiple_of(j * step, step), step)
        return [
            pltpu.make_async_copy(
                pieces[r].at[:, there], held.at[slot, pl.ds(r * rows, rows), :], sems.at[slot, r]
            )
            for r in range(count)
        ]

    slot = lax.rem(here, 2)

    @pl.when(here == 0)
    def _():
        for copy in copies(0, 0):
            copy.start()

    @pl.when(here + 1 < steps)
    def _():
        for copy in copies(here + 1, 1 - slot):
            copy.start()

    for copy in copies(here, slot):
        copy.wait()
    total = left_transposed(left[...], held[slot]).astype(bf16)
    if first:
        total = jnp.concatenate([refs[count][...], total], axis=0)
    low = 0
    for out in outs:
        size = out.shape[0]
        out[...] = total[low : low + size]
        low += size


def weight_product(left, right, rows, above=None, step=1024):
    right = list(right) if isinstance(right, (list, tuple)) else [right]
    count = len(right)
    tokens, units = left.shape
    columns = right[0].shape[1]
    step = min(step, columns)
    operands = [left, *right]
    specs = [pl.BlockSpec((tokens, units), lambda j: (0, 0))] + [any_space()] * count
    if above is not None:
        operands.append(above)
        specs.append(pl.BlockSpec((above.shape[0], step), lambda j: (0, j)))
    return pl.pallas_call(
        functools.partial(product_kernel, count, len(operands) - 1 - count, step),
        grid=(columns // step,),
        out_shape=[shaped((one, columns), bf16) for one in rows],
        in_specs=specs,
        out_specs=[pl.BlockSpec((one, step), lambda j: (0, j)) for one in rows],
        scratch_shapes=[
            pltpu.VMEM((2, tokens, step), bf16),
            pltpu.SemaphoreType.DMA((2, count)),
        ],
        compiler_params=pltpu.CompilerParams(vmem_limit_bytes=30 << 20),
        cost_estimate=brief(),
        name="weight_product",
    )(*operands)


def pack_last_kernel(above, wide, below, out):
    top = above.shape[0]
    rows, columns = wide.shape
    parts = out.shape[1] // columns
    step = rows // parts
    out[:top, :] = above[...]
    for j in range(parts):
        out[top : top + step, j * columns : (j + 1) * columns] = wide[j * step : (j + 1) * step, :]
    out[top + step :, :] = below[...]


def pack_last(above, wide, below):
    columns = above.shape[1]
    rows = above.shape[0] + wide.size // columns + below.shape[0]
    return call(
        pack_last_kernel, shaped((rows, columns), bf16), [above, wide, below], "pack_last"
    )


def settle_last_kernel(top, at, inner, own, came, past, wide, below, whole, buffer, sem):
    rows, columns = wide.shape
    parts = own.shape[1] // columns
    step = rows // parts

    def write(source):
        buffer[...] = source[:top, :].astype(f32)
        copy = pltpu.make_async_copy(buffer, whole.at[pl.ds(at, top), :], sem)
        copy.start()
        for j in range(parts):
            wide[j * step : (j + 1) * step, :] = source[
                top : top + step, j * columns : (j + 1) * columns
            ].astype(f32)
        below[...] = source[top + step :, :].astype(f32)
        copy.wait()

    @pl.when(inner[0] == 1)
    def _():
        write(own)

    @pl.when(inner[0] == 0)
    def _():
        write(came)


def settle_last(inner, own, came, top, rows, columns, past, at):
    total, dim = own.shape
    left = total - top - rows * columns // dim
    return pl.pallas_call(
        functools.partial(settle_last_kernel, top, at),
        out_shape=[
            shaped((rows, columns), f32),
            shaped((left, dim), f32),
            shaped(past.shape, f32),
        ],
        in_specs=[smem(), vmem(), vmem(), any_space()],
        out_specs=[vmem(), vmem(), any_space()],
        scratch_shapes=[pltpu.VMEM((top, dim), f32), pltpu.SemaphoreType.DMA],
        input_output_aliases={3: 2},
        compiler_params=pltpu.CompilerParams(vmem_limit_bytes=24 << 20),
        cost_estimate=brief(),
        name="settle_last",
    )(inner, own, came, past)


def pack_kernel(count, *refs):
    total = summed(refs[:count]).astype(bf16)
    beside, out = refs[count:]
    rows, columns = total.shape
    tall = rows * 3 // 4
    out[:tall, :columns] = total[:tall]
    third = columns // 3
    for j in range(3):
        low = j * (rows - tall)
        out[low : low + rows - tall, columns:] = total[tall:, j * third : (j + 1) * third]
    out[tall:, :] = beside[...]


def pack(parts, beside):
    rows, columns = parts[0].shape
    tall = rows * 3 // 4
    return call(
        functools.partial(pack_kernel, len(parts)),
        shaped((tall + beside.shape[0], beside.shape[1]), bf16),
        [*parts, beside],
        "pack",
    )


def pick_kernel(inner, own, came, out):
    rows = out.shape[0]

    @pl.when(inner[0] == 1)
    def _():
        out[...] = own[:rows, :]

    @pl.when(inner[0] == 0)
    def _():
        out[...] = came[:rows, :]


def pick(inner, own, came, rows):
    return call(
        pick_kernel,
        shaped((rows, own.shape[1]), bf16),
        [inner, own, came],
        "pick",
        scalars=1,
    )


def widen_kernel(*refs):
    out = refs[-1]
    low = 0
    for x in refs[:-1]:
        rows = x.shape[0]
        out[low : low + rows, :] = x[...].astype(f32)
        low += rows


def widen(parts, step=512):
    rows = sum(part.shape[0] for part in parts)
    columns = parts[0].shape[1]
    return pl.pallas_call(
        widen_kernel,
        grid=(columns // step,),
        out_shape=shaped((rows, columns), f32),
        in_specs=[pl.BlockSpec((part.shape[0], step), lambda j: (0, j)) for part in parts],
        out_specs=pl.BlockSpec((rows, step), lambda j: (0, j)),
        compiler_params=pltpu.CompilerParams(vmem_limit_bytes=16 << 20),
        cost_estimate=brief(),
        name="widen",
    )(*parts)


def settle_two_kernel(inner, own, came, above, below):
    rows = above.shape[0]

    @pl.when(inner[0] == 1)
    def _():
        above[...] = own[:rows, :].astype(f32)
        below[...] = own[rows:, :].astype(f32)

    @pl.when(inner[0] == 0)
    def _():
        above[...] = came[:rows, :].astype(f32)
        below[...] = came[rows:, :].astype(f32)


def settle_two(inner, own, came, rows):
    total, columns = own.shape
    return call(
        settle_two_kernel,
        [shaped((rows, columns), f32), shaped((total - rows, columns), f32)],
        [inner, own, came],
        "settle_two",
        scalars=1,
    )


def rotated(first, second, cosine, sine):
    return first * cosine - second * sine, second * cosine + first * sine


def enter_kernel(rank, width, x, gain, down, latent_gain, key, value, cosine, sine, *outs):
    normed, latent, packed = outs
    half = width // 2
    rows = x[...].astype(f32)
    low = (rows * inverse_rms(rows) * gain[...]).astype(bf16)
    normed[...] = low
    inner = dot(low, down[...])
    latent[...] = inner
    packed[:, :rank] = (inner * inverse_rms(inner) * latent_gain[...]).astype(bf16)
    keys = dot(low, key[...])
    first, second = rotated(keys[:, :half], keys[:, half:], cosine[...], sine[...])
    packed[:, rank : rank + half] = first.astype(bf16)
    packed[:, rank + half : rank + width] = second.astype(bf16)
    packed[:, rank + width :] = dot(low, value[...]).astype(bf16)


def enter(x, gain, down, latent_gain, key, value, cosine, sine):
    rows, dim = x.shape
    rank, width = down.shape[1], key.shape[1]
    return call(
        functools.partial(enter_kernel, rank, width),
        [shaped((rows, dim), bf16), shaped((rows, rank), f32), shaped((rows, rank + 2 * width), bf16)],
        [x, gain[None], down, latent_gain[None], key, value, cosine, sine],
        "enter",
        limit=60,
    )


def summed(parts):
    total = parts[0][...].astype(f32)
    for part in parts[1:]:
        total = total + part[...].astype(f32)
    return total


def middle_kernel(x, gain, *refs):
    parts, (middle, normed) = refs[:-2], refs[-2:]
    total = x[...].astype(f32) + summed(parts)
    middle[...] = total
    normed[...] = (total * inverse_rms(total) * gain[...]).astype(bf16)


def middle_rows(x, gain, parts):
    shape = x.shape
    return call(
        middle_kernel,
        [shaped(shape, f32), shaped(shape, bf16)],
        [x, gain[None], *parts],
        "middle_rows",
    )


def lower_norm(value, gain, upper):
    scale = inverse_rms(value)
    scaled = upper * gain
    lower = scale * scaled - value * (scale * scale * scale) * jnp.mean(
        scaled * value, axis=-1, keepdims=True
    )
    return lower, jnp.sum(upper * value * scale, axis=0, keepdims=True)


def middle_back_kernel(middle, gain, cotangent, *refs):
    parts, (total, low, gain_part) = refs[:-3], refs[-3:]
    lower, gain_part[...] = lower_norm(middle[...], gain[...], summed(parts))
    result = cotangent[...].astype(f32) + lower
    total[...] = result
    low[...] = result.astype(bf16)


def middle_back(middle, gain, cotangent, parts):
    shape = middle.shape
    return call(
        middle_back_kernel,
        [shaped(shape, f32), shaped(shape, bf16), shaped((1, shape[1]), f32)],
        [middle, gain[None], cotangent, *parts],
        "middle_back",
    )


def latent_back_kernel(latent, gain, cosine, sine, *refs):
    parts, (packed, gain_part) = refs[:-2], refs[-2:]
    rank = latent.shape[1]
    total = summed(parts)
    lower, gain_part[...] = lower_norm(latent[...], gain[...], total[:, :rank])
    width = (total.shape[1] - rank) // 2
    half = width // 2
    packed[:, :rank] = lower.astype(bf16)
    first, second = rotated(
        total[:, rank : rank + half], total[:, rank + half : rank + width], cosine[...], -sine[...]
    )
    packed[:, rank : rank + half] = first.astype(bf16)
    packed[:, rank + half : rank + width] = second.astype(bf16)
    packed[:, rank + width :] = total[:, rank + width :].astype(bf16)


def latent_back(latent, gain, cosine, sine, parts):
    shape = parts[0].shape
    return call(
        latent_back_kernel,
        [shaped(shape, bf16), shaped((1, latent.shape[1]), f32)],
        [latent, gain[None], cosine, sine, *parts],
        "latent_back",
    )


def leave_kernel(packed, down, key, value, x, gain, upper, result, gain_part):
    rank, width = down.shape[1], key.shape[1]
    total = right_transposed(packed[:, :rank], down[...])
    total = total + right_transposed(packed[:, rank : rank + width], key[...])
    total = total + right_transposed(packed[:, rank + width :], value[...])
    lower, gain_part[...] = lower_norm(x[...].astype(f32), gain[...], total)
    result[...] = upper[...] + lower


def leave(packed, down, key, value, x, gain, upper):
    return call(
        leave_kernel,
        [shaped(x.shape, f32), shaped((1, x.shape[1]), f32)],
        [packed, down, key, value, x, gain[None], upper],
        "leave",
    )


def shared_kernel(count, table, normed, grads, *outs):
    rows = outs[0].shape[0]
    for r in range(count):
        there = pl.ds(pl.multiple_of(table[r] * rows, rows), rows)
        outs[r][...] = left_transposed(normed[:, there], grads[...]).astype(bf16)


def shared_shares(table, normed, grads):
    count = table.shape[0]
    rows = normed.shape[1] // count
    columns = grads.shape[1]
    return list(
        pl.pallas_call(
            functools.partial(shared_kernel, count),
            out_shape=[jax.ShapeDtypeStruct((rows, columns), bf16)] * count,
            in_specs=[smem(), vmem(), vmem()],
            out_specs=[vmem()] * count,
            compiler_params=pltpu.CompilerParams(vmem_limit_bytes=36 << 20),
            cost_estimate=brief(),
            name="shared_shares",
        )(table, normed, grads)
    )


def unpack_kernel(base, count, parts, packed, table, *refs):
    pieces = refs[:count]
    outs, buffers = refs[-1 - 2 * len(parts) : -1 - len(parts)], refs[-1 - len(parts) : -1]
    sems = refs[-1]
    rows = buffers[0].shape[1]
    tall = rows * 3 // 4
    columns = parts[-1][1]
    third = columns // 3
    flying = []
    for r in range(count):
        slot = r % 2
        if r >= 2:
            for copy in flying[r - 2]:
                copy.wait()
        there = pl.ds(pl.multiple_of(table[base + r] * rows, rows), rows)
        copies = []
        for k, (low, high) in enumerate(parts):
            if packed:
                buffers[k][slot, :tall, :] = pieces[r][:, low:high].astype(f32)
                for j in range(3):
                    first, last = max(low, j * third), min(high, (j + 1) * third)
                    if first < last:
                        start = columns - j * third
                        buffers[k][slot, tall:, first - low : last - low] = pieces[r][
                            j * (rows - tall) : (j + 1) * (rows - tall),
                            start + first : start + last,
                        ].astype(f32)
            else:
                buffers[k][slot] = pieces[r][:, low:high].astype(f32)
            copy = pltpu.make_async_copy(
                buffers[k].at[slot], outs[k].at[there, :], sems.at[k, slot]
            )
            copy.start()
            copies.append(copy)
        flying.append(copies)
    for copies in flying[-2:]:
        for copy in copies:
            copy.wait()


def unpack(table, pieces, parts, packed, first=0, past=None):
    count = len(pieces)
    rows = pieces[0].shape[0]
    if packed:
        rows = rows * 4 // 3
    past = [] if past is None else list(past)
    return pl.pallas_call(
        functools.partial(unpack_kernel, first, count, parts, packed),
        out_shape=[
            jax.ShapeDtypeStruct((table.shape[0] * rows, high - low), f32) for low, high in parts
        ],
        in_specs=[smem()] + [vmem()] * count + [any_space()] * len(past),
        out_specs=[any_space()] * len(parts),
        scratch_shapes=[pltpu.VMEM((2, rows, high - low), f32) for low, high in parts]
        + [pltpu.SemaphoreType.DMA((len(parts), 2))],
        input_output_aliases={1 + count + k: k for k in range(len(past))},
        compiler_params=pltpu.CompilerParams(vmem_limit_bytes=24 << 20),
        cost_estimate=brief(),
        name="unpack",
    )(table, *pieces, *past)


def body(
    packs,
    group,
    block_input,
    segment_ids,
    positions,
    attention_gain,
    query_down,
    query_gain,
    query_up,
    key_proj,
    value_proj,
    out_proj,
    feed_gain,
    gate_weight,
    up_weight,
    down_weight,
    out_grad,
):
    plane = Plane(group)
    line = Line(packs)
    rows = block_input.shape[1]
    segments = segment_ids[0]
    places = positions[0]
    width = key_proj.shape[1]
    rank = query_down.shape[1]
    heads = query_up.shape[1] // width
    scale = 1.0 / math.sqrt(width)
    first_row = plane.me * rows

    gate_rows, up_rows = gate_weight.T, up_weight.T
    clock = Clock()
    belt = Belt(line, clock)
    fast = plane.fast
    move = plane.move
    hop_a, hop_b, hop_c = (plane.hop_a, plane.hop_b, plane.hop_c) if fast else (None,) * 3
    cotangent_rows = out_grad[0]

    x = block_input[0]
    dim = x.shape[1]
    always = (segments[0] & 1) <= 1

    def stage(run):
        def inside():
            inner = Clock()
            inner.last = clock.last
            return tuple(run(inner))

        if not fast:
            return inside()
        shapes = jax.eval_shape(inside)
        result = lax.cond(
            always, inside, lambda: tuple(jnp.zeros(one.shape, one.dtype) for one in shapes)
        )
        return clock.all(*result)

    def hops(values, ways, filler=None, apart=False):
        def run(clock):
            held = clock.all(*values)
            came = [move(value, way) for value, way in zip(held, ways)]
            more = list(filler(clock, *came)) if filler else []
            return [*clock.all(*came), *more]

        result = stage(run) if apart else run(clock)
        return list(result[: len(values)]), list(result[len(values) :])

    def gather(rows, first=None, second=None, apart=False, between=None, last=False):
        def beside(clock, a, b, s_o):
            return first(clock, [rows, clock(s_o)]) if first else []

        (a, b, s_o), more = hops([rows, rows, rows], [hop_a, hop_b, hop_c], beside, apart)
        if between:
            between()

        def beside(clock, c, a_o, b_o):
            if not second:
                return []
            a_o, b_o = clock(a_o, b_o)
            return second(clock, [a, a_o, b, b_o], more)

        (c, a_o, b_o), later = hops([a, a, b], [hop_b, hop_c, hop_c], beside, apart)
        (c_o,), _ = hops([c], [hop_c], None, apart or last)
        return [rows, s_o, a, a_o, b, b_o, c, c_o], more, later

    def scatter(share, filler=None, apart=False, between=None, head=False):
        c, c_send = clock(*share(clock, 6, 8))
        (c_came,), near = hops(
            [c_send], [hop_c], lambda clock, came: clock(*share(clock, 2, 6)), apart or head
        )
        a, a_send, b, b_send = near
        c = clock(add_rows(c, c_came))
        (c_in, a_came, b_came), (own, own_send) = hops(
            [c, a_send, b_send],
            [hop_b, hop_c, hop_c],
            lambda clock, *came: clock(*share(clock, 0, 2)),
            apart,
        )
        a, b = clock(add_rows(a, a_came, c_in), add_rows(b, b_came))
        if between:
            between()
        (a_in, b_in, own_came), more = hops(
            [a, b, own_send],
            [hop_a, hop_b, hop_c],
            (lambda clock, *came: filler(clock)) if filler else None,
            apart,
        )
        return [own, own_came, b_in, a_in], more

    own_places = lax.dynamic_slice_in_dim(places, first_row, rows, 0)
    own_cosine, own_sine = rotation(own_places, width)

    def enter_rows():
        return enter(
            x, attention_gain, query_down, query_gain, key_proj, value_proj, own_cosine, own_sine
        )

    def attend(pieces, cosine, sine):
        return attend_forward(
            plane.table, pieces, query_up, cosine, sine, segments, heads, width, scale
        )

    def attend_back(outer):
        return attend_backward(
            plane.table, outer, queries, keys, values, cosine, sine, segments, heads, scale
        )

    def leave_rows(packed_grad):
        return leave(
            packed_grad, query_down, key_proj, value_proj, x, attention_gain, middle_grad
        )

    def sum_gains(parts, total):
        return total(jnp.concatenate(parts, axis=1))

    units = gate_rows.shape[0]
    size = heads * width
    columns = ((0, rank), (rank, rank + width), (rank + width, rank + 2 * width))
    add = lambda left, right: left + right

    if not fast:
        normed_rows, latent, packed = enter_rows()
        cosine, sine = rotation(places, width)
        pieces = plane.gather(packed)
        latents, queries, keys, values, mixed_there = attend(pieces, cosine, sine)
        share = shares([mixed_there], [out_proj], group)
        parts = [plane.scatter(share(clock, 0, group))]
        middle, normed_mid_rows = middle_rows(x, feed_gain, parts)
        cot_pieces = plane.gather(cotangent_rows)
        hidden_grad = rows_product(cot_pieces, down_weight, f32)
        mid_pieces = plane.gather(normed_mid_rows)
        hidden, gate_grad, upward_grad = feed(
            mid_pieces, 0, group, hidden_grad, gate_rows, up_rows, group, None
        )
        cotangent, normed_mid = join(cot_pieces), join(mid_pieces)
        share = shares([gate_grad, upward_grad], [gate_rows, up_rows], group)
        parts = [plane.scatter(share(clock, 0, group))]
        middle_grad, attention_grad, feed_gain_part = middle_back(
            middle, feed_gain, cotangent_rows, parts
        )
        grad_pieces = plane.gather(attention_grad)
        outer = [rows_product(grad_pieces, out_proj, bf16)]
        query_pre_grad, pair_grads = attend_back(outer)
        share = latent_shares(plane.table, query_pre_grad, pair_grads, query_up)
        parts = [plane.scatter(share(clock, 0, group))]
        packed_grad, query_gain_part = latent_back(latent, query_gain, own_cosine, own_sine, parts)
        shared_pieces = shared_shares(plane.table, normed_rows, packed_grad)
        shared = line.total(plane.scatter(list(shared_pieces)).astype(bf16))
        query_down_gradient, key_proj_gradient, value_proj_gradient = unpack(
            plane.table, plane.gather(shared), columns, False
        )
        input_gradient, attention_gain_part = leave_rows(packed_grad)
        share = shares([hidden], [down_weight], group)
        block_output = add_rows(middle, plane.scatter(share(clock, 0, group)))
        gains = sum_gains([attention_gain_part, query_gain_part, feed_gain_part], plane.total)
        gains = line.total(gains, add)[0]
        down_gradient, gate_gradient, up_gradient, proj_gradient, query_up_gradient = (
            line.total(weight_product(left, right, [left.shape[1]])[0]).astype(f32)
            for left, right in (
                (hidden, cotangent),
                (gate_grad, normed_mid),
                (upward_grad, normed_mid),
                (mixed_there, join(grad_pieces)),
                (latents, query_pre_grad),
            )
        )
    else:
        half = units // 2
        cot_a = move(cotangent_rows, hop_a)
        normed_rows, latent, packed = enter_rows()
        packed = clock(packed)

        def angles(clock, own):
            return clock(*rotation(clock(places), width))

        pieces, (cosine, sine), _ = gather(packed, angles, apart=True)
        cot_now, cot_a = clock(cotangent_rows, cot_a)
        cot_b, cot_c = move(cot_now, hop_b), move(cot_a, hop_b)
        cot_o, cot_ao = move(cot_now, hop_c), move(cot_a, hop_c)
        pieces[0] = clock(packed)

        latents, queries, keys, values, mixed_there = clock(*attend(pieces, cosine, sine))
        share = shares([mixed_there], [out_proj], group)
        c, c_send = clock(*share(clock, 6, 8))
        a, a_send, b, b_send = clock(*share(clock, 2, 6))
        own, own_send = clock(*share(clock, 0, 2))
        cot_b, cot_c, cot_o, cot_ao = clock(cot_b, cot_c, cot_o, cot_ao)
        (c_came,), _ = hops([c_send], [hop_c])
        c = clock(add_rows(c, c_came))
        (c_in, a_came, b_came), _ = hops([c, a_send, b_send], [hop_b, hop_c, hop_c])
        a, b = clock(add_rows(a, a_came, c_in), add_rows(b, b_came))

        def beside_last(clock, a_in, b_in, own_came, cot_bo, cot_co):
            cot_bo, cot_co = clock(cot_bo, cot_co)
            cot_pieces = [cotangent_rows, cot_o, cot_a, cot_ao, cot_b, cot_bo, cot_c, cot_co]
            hidden_grad = clock(rows_product(cot_pieces, down_weight, f32))
            return [hidden_grad]

        (a_in, b_in, own_came, cot_bo, cot_co), (hidden_grad,) = hops(
            [a, b, own_send, cot_b, cot_c], [hop_a, hop_b, hop_c, hop_c, hop_c], beside_last
        )
        cot_pieces = [cotangent_rows, cot_o, cot_a, cot_ao, cot_b, cot_bo, cot_c, cot_co]
        middle, normed_mid_rows = clock(*middle_rows(x, feed_gain, [own, own_came, b_in, a_in]))

        def feed_group(clock, pieces, low, high, past):
            pieces = [None] * low + [clock(pieces[0]), *pieces[1:]]
            return clock(
                *feed(pieces, low, high, hidden_grad, gate_rows, up_rows, group, past)
            )

        def near_feed(clock, near):
            return feed_group(clock, near, 0, 2, None)

        (a, b, s_o), past = hops(
            [normed_mid_rows] * 3,
            [hop_a, hop_b, hop_c],
            lambda clock, a, b, s_o: near_feed(clock, [normed_mid_rows, clock(s_o)]),
        )

        def next_feed(clock, c, a_o, b_o):
            a_o, b_o = clock(a_o, b_o)
            more = feed_group(clock, [a, a_o], 2, 4, past)
            return [a_o, b_o, *feed_group(clock, [b, b_o], 4, 6, more)]

        (c, a_o, b_o), past = hops([a, a, b], [hop_b, hop_c, hop_c], next_feed)
        a_o, b_o, *past = past
        (c_o,), _ = hops([c], [hop_c])
        hidden, gate_grad, upward_grad = feed_group(clock, [c, c_o], 6, 8, past)
        mid_pieces = [normed_mid_rows, s_o, a, a_o, b, b_o, c, c_o]
        chunk = units * 3 // 4
        tall = dim * 3 // (4 * group)
        beside = chunk - tall
        one, tail = clock(*weight_product(clock(hidden), cot_pieces, [chunk, units - chunk]))
        one = belt.begin(one)
        two = []

        def middle_filler(clock):
            part, rest = clock(
                *weight_product(clock(gate_grad), mid_pieces, [chunk, units - half], tail)
            )
            two.append(belt.begin(part))
            belt.cross(one)
            return [rest]

        share = shares([gate_grad, upward_grad], [gate_rows, up_rows], group)
        parts, (tail,) = scatter(share, middle_filler, head=True)
        two = two[0]
        middle_grad, attention_grad, feed_gain_part = clock(
            *middle_back(middle, feed_gain, cotangent_rows, parts)
        )

        def near_grad(clock, near):
            outer = clock(rows_product([clock(near[0]), near[1]], out_proj, bf16))
            pair = clock(*weight_product(clock(upward_grad), mid_pieces, [chunk, chunk], tail))
            return [outer, *pair]

        def next_grad(clock, near, more):
            return [clock(rows_product([clock(near[0]), *near[1:]], out_proj, bf16))]

        grad_pieces, (outer_near, three, four), (outer_next,) = gather(
            attention_grad, near_grad, next_grad, last=True
        )
        outer_last = clock(rows_product([clock(grad_pieces[6]), grad_pieces[7]], out_proj, bf16))
        three = belt.back(one, three)
        belt.cross(two)

        query_pre_grad, pair_grads = clock(*attend_back([outer_near, outer_next, clock(outer_last)]))

        def latent_filler(clock):
            return clock(
                *weight_product(clock(mixed_there), grad_pieces, [beside, size - beside])
            )

        share = latent_shares(plane.table, query_pre_grad, pair_grads, query_up)
        parts, (five, six) = scatter(share, latent_filler)
        packed_grad, query_gain_part = clock(
            *latent_back(latent, query_gain, own_cosine, own_sine, parts)
        )
        belt.cross(three)
        four = belt.back(two, four)

        shared_pieces = clock(*shared_shares(plane.table, normed_rows, packed_grad))

        def shared_filler(clock):
            leaving = clock(*leave_rows(clock(packed_grad)))
            product = clock(weight_product(clock(latents), query_pre_grad, [rank])[0])
            belt.land(one)
            return [*leaving, product, clock(belt.end(one, units))]

        parts, (input_gradient, attention_gain_part, query_sum, down_gradient) = scatter(
            lambda clock, low, high: shared_pieces[low:high], shared_filler
        )
        five = clock(pack(parts, five))
        five = belt.back(three, five)
        belt.cross(four)
        fill = -(2 * dim + rank) % (16 * dim)

        def gain_rows(clock):
            gains = sum_gains(
                [clock(attention_gain_part), query_gain_part, feed_gain_part], plane.total
            )
            gains = jnp.concatenate([gains[0], jnp.zeros((fill,), f32)]).reshape(-1, dim)
            return [pack_last(six, query_sum, gains.astype(bf16))]

        (six,) = stage(gain_rows)

        settled = []

        def turn():
            belt.cross(five)
            belt.back(four)
            begun = belt.begin(six)
            belt.land(two)
            down = clock(belt.end(two, units, chunk, down_gradient, 0, units - chunk))
            gate = clock(belt.end(two, units, 0, None, units - chunk))
            belt.land(three)
            gate = clock(belt.end(three, units, half, gate, 0, half))
            up = clock(belt.end(three, units, 0, None, half))
            belt.land(four)
            belt.back(five)
            belt.cross(begun)
            settled.extend([begun, down, gate, up])

        share = shares([hidden], [down_weight], group)
        parts, _ = scatter(share, None, True, turn)
        block_output = clock(add_rows(middle, *parts))
        six, down_gradient, gate_gradient, up_gradient = settled
        up_gradient = clock(belt.end(four, units, chunk - half, up_gradient))
        belt.meet(six)
        belt.land(five)
        belt.send(six)
        shared_rows = clock(pick(belt.inner, five["own"], five["came"], tall))

        def five_end(clock, own):
            held = dict(five, came=clock(five["came"]))
            return [clock(belt.end(held, size, 0, None, tall))]

        def near_unpack(clock, near, more):
            pieces = [shared_rows, s_one, *near]
            return clock(*unpack(plane.table, pieces, columns, True))

        (a, b, s_one), (proj_gradient,) = hops(
            [shared_rows] * 3, [hop_a, hop_b, hop_c], lambda clock, *came: five_end(clock, None), True
        )

        def beside_next(clock, c, a_o, b_o):
            a_o, b_o = clock(a_o, b_o)
            return near_unpack(clock, [a, a_o, b, b_o], None)

        (c, a_o, b_o), past = hops([a, a, b], [hop_b, hop_c, hop_c], beside_next, True)
        (c_o,), _ = hops([c], [hop_c], None, True)
        query_down_gradient, key_proj_gradient, value_proj_gradient = clock(
            *unpack(plane.table, [c, c_o], columns, True, 6, past)
        )
        belt.land(six)
        query_up_gradient, gains, proj_gradient = settle_last(
            belt.inner, six["own"], six["came"], size - beside, rank, size, proj_gradient, beside
        )
        gains = gains.reshape(-1)
    return (
        block_output[None],
        input_gradient[None],
        gains[:dim],
        query_down_gradient,
        gains[dim : dim + rank],
        query_up_gradient,
        key_proj_gradient,
        value_proj_gradient,
        proj_gradient,
        gains[dim + rank : dim + rank + dim],
        gate_gradient.T,
        up_gradient.T,
        down_gradient,
    )


def solution(mesh):
    in_specs = (
        P("tok", "head", None),
        P("tok", None),
        P("tok", None),
        P(),
        P(),
        P(),
        P(None, "head"),
        P(),
        P(),
        P("head", None),
        P(),
        P(None, "head"),
        P(None, "head"),
        P("head", None),
        P("tok", "head", None),
    )
    out_specs = (
        P("tok", "head", None),
        P("tok", "head", None),
        P(),
        P(),
        P(),
        P(None, "head"),
        P(),
        P(),
        P("head", None),
        P(),
        P(None, "head"),
        P(None, "head"),
        P("head", None),
    )
    sizes = dict(mesh.shape)
    return jax.shard_map(
        functools.partial(body, sizes["tok"], sizes["head"]),
        mesh=mesh,
        in_specs=in_specs,
        out_specs=out_specs,
        check_vma=False,
    )
```

```python
import functools
import math

import jax
import jax.numpy as jnp
from jax import lax
from jax.experimental import pallas as pl
from jax.experimental.pallas import tpu as pltpu
from jax.sharding import PartitionSpec as P

norm_epsilon = 1e-05
rope_base = 10000.0
first_document = 1024
bf16 = jnp.bfloat16
f32 = jnp.float32


def inverse_rms(value):
    return lax.rsqrt(jnp.mean(value * value, axis=-1, keepdims=True) + norm_epsilon)


def norm_backward(value, gain, upper):
    scale = inverse_rms(value)
    scaled = upper * gain
    lower = scale * scaled - value * (scale * scale * scale) * jnp.mean(
        scaled * value, axis=-1, keepdims=True
    )
    return (lower, jnp.sum(upper * value * scale, axis=0))


def rotation(places, head_width):
    half = head_width // 2
    steps = jnp.arange(half).astype(f32) * (2.0 / head_width)
    inverse = jnp.exp(steps * -math.log(rope_base))
    angles = places.astype(f32)[:, None] * inverse[None, :]
    return (jnp.cos(angles), jnp.sin(angles))


def rotate(value, cosine, sine):
    half = value.shape[-1] // 2
    first = value[..., :half]
    second = value[..., half:]
    return jnp.concatenate(
        [first * cosine - second * sine, second * cosine + first * sine], axis=-1
    )


def dot(left, right):
    return jnp.dot(left, right, preferred_element_type=f32)


def right_transposed(left, right):
    return lax.dot_general(left, right, (((1,), (1,)), ((), ())), preferred_element_type=f32)


def left_transposed(left, right):
    return lax.dot_general(left, right, (((0,), (0,)), ((), ())), preferred_element_type=f32)


def add_low(left, right):
    return (left.astype(f32) + right.astype(f32)).astype(bf16)


class Clock:
    def __init__(self):
        self.last = ()

    def all(self, *values):
        held = lax.optimization_barrier(values + self.last)
        self.last = (held[0],)
        return held[: len(values)]

    def __call__(self, *values):
        held = self.all(*values)
        return held[0] if len(values) == 1 else held


class Plane:
    def __init__(self, size):
        self.size = size
        self.fast = size == 8 and lax.axis_size("tok") == 4
        self.me = lax.axis_index("head")
        if self.fast:
            even = [index % 2 == 0 for index in range(size)]
            self.hop_a = [(i, i ^ (2 if even[i] else 4)) for i in range(size)]
            self.hop_b = [(i, i ^ (4 if even[i] else 2)) for i in range(size)]
            self.hop_c = [(i, i ^ 1) for i in range(size)]
            mask_a = jnp.where(self.me % 2 == 0, 2, 4)
            other = self.me ^ 1
            order = [
                self.me,
                other,
                self.me ^ mask_a,
                other ^ (6 - mask_a),
                self.me ^ (6 - mask_a),
                other ^ mask_a,
                self.me ^ 6,
                other ^ 6,
            ]
            self.table = jnp.stack(order).astype(jnp.int32)
            self.groups = [(0, 2), (2, 6), (6, 8)]
        else:
            self.table = jnp.arange(size, dtype=jnp.int32)
            self.groups = [(0, size)]

    def move(self, value, hop):
        return lax.ppermute(value, "head", hop)

    def gather(self, rows):
        whole = lax.all_gather(rows, "head", axis=0, tiled=True)
        return list(jnp.split(whole, self.size, axis=0))

    def scatter(self, pieces):
        whole = jnp.concatenate(pieces, axis=0)
        return lax.psum_scatter(whole, "head", scatter_dimension=0, tiled=True).astype(f32)

    def total(self, value):
        if not self.fast:
            return lax.psum(value, "head")
        for bit in (1, 2, 4):
            value = value + self.move(value, [(i, i ^ bit) for i in range(8)])
        return value


class Line:
    def __init__(self, size):
        self.size = size
        self.me = lax.axis_index("tok")
        half = size // 2
        self.stages = [([(k, k + 1), (size - 1 - k, size - 2 - k)], None) for k in range(half - 1)]
        self.stages.append(([(half - 1, half), (half, half - 1)], None))
        for k in reversed(range(half - 1)):
            self.stages.append(([(k + 1, k), (size - 2 - k, size - 1 - k)], k))

    def start(self, stage, value):
        return lax.ppermute(value, "tok", self.stages[stage][0])

    def finish(self, stage, value, came, plus=add_low):
        outward = self.stages[stage][1]
        if outward is None:
            return plus(value, came)
        mine = (self.me == outward) | (self.me == self.size - 1 - outward)
        return jnp.where(mine, came, value)

    def total(self, value, plus=add_low):
        for stage in range(len(self.stages)):
            value = self.finish(stage, value, self.start(stage, value), plus)
        return value


class Belt:
    inward = [(0, 1), (3, 2)]
    middle = [(1, 2), (2, 1)]
    outward = [(1, 0), (2, 3)]

    def __init__(self, line, clock):
        self.clock = clock
        self.inner = jnp.where((line.me == 1) | (line.me == 2), 1, 0).astype(jnp.int32).reshape(1)

    def move(self, value, pairs):
        return lax.ppermute(value, "tok", pairs)

    def begin(self, value):
        value = self.clock(value)
        return {"own": value, "came": self.move(value, self.inward)}

    def cross(self, item):
        item["came"] = self.clock(item["came"])
        item["own"] = self.clock(add_rows(item["own"], item["came"]))
        item["came"] = self.move(item["own"], self.middle)

    def meet(self, item):
        item["came"] = self.clock(item["came"])
        item["own"] = self.clock(add_rows(item["own"], item["came"]))

    def send(self, item):
        item["own"] = self.clock(item["own"])
        item["came"] = self.move(item["own"], self.outward)

    def back(self, item, value=None):
        if value is None:
            self.meet(item)
            self.send(item)
            return None
        item["came"] = self.clock(item["came"])
        both = self.clock(add_or_begin(self.inner, item["own"], item["came"], value))
        came = self.move(both, self.inward + self.outward)
        item["own"], item["came"] = both, came
        return {"own": value, "came": came}

    def land(self, item):
        item["came"] = self.clock(item["came"])

    def end(self, item, size, at=0, past=None, low=0, high=None):
        return settle(self.inner, item["own"], item["came"], size, at, past, low, high)


def query_blocks(length):
    first = min(length, max(first_document, length // 2))
    block = 256
    return [
        (start, min(block, length - start), 0 if start < first else first)
        for start in range(0, length, block)
    ]


def allowed(seg_column, seg_row, start, rows, low, high):
    query_order = start + lax.broadcasted_iota(jnp.int32, (rows, high - low), 0)
    key_order = low + lax.broadcasted_iota(jnp.int32, (rows, high - low), 1)
    same = seg_column[start : start + rows, :] == seg_row[:, low:high]
    return (key_order <= query_order) & same


def weights_of(stacked, keys, permit, heads, scale):
    scores = right_transposed(stacked, keys) * scale
    scores = jnp.where(jnp.concatenate([permit] * heads, axis=0), scores, -1e30)
    top = jnp.max(scores, axis=-1, keepdims=True)
    weights = jnp.exp(scores - top)
    return weights, jnp.sum(weights, axis=-1, keepdims=True)


def stack_heads(ref, start, rows, heads, width):
    return jnp.concatenate(
        [ref[start : start + rows, h * width : (h + 1) * width] for h in range(heads)], axis=0
    )


def attend_forward_kernel(count, heads, width, rank, scale, *refs):
    table = refs[0]
    pieces = refs[1 : 1 + count]
    weight, cosine, sine, seg_column, seg_row = refs[1 + count : 6 + count]
    latents, queries_out, keys_out, values_out, mixed_there = refs[6 + count : 11 + count]
    queries, keys, values, mixed, sems = refs[11 + count :]
    length = queries.shape[0]
    leaving = []

    def leave_now(source, target):
        copy = pltpu.make_async_copy(source, target, sems.at[len(leaving)])
        copy.start()
        leaving.append(copy)

    rows = length // count
    half = width // 2
    for r in range(count):
        there = pl.ds(pl.multiple_of(table[r] * rows, rows), rows)
        leave_now(pieces[r].at[:, :rank], latents.at[there, :])
        keys[there, :] = pieces[r][:, rank : rank + width]
        values[there, :] = pieces[r][:, rank + width :]
        flat = dot(pieces[r][:, :rank], weight[...])
        cos = cosine[there, :]
        sin = sine[there, :]
        for h in range(heads):
            first = flat[:, h * width : h * width + half]
            second = flat[:, h * width + half : (h + 1) * width]
            queries[there, h * width : h * width + half] = (first * cos - second * sin).astype(bf16)
            queries[there, h * width + half : (h + 1) * width] = (
                second * cos + first * sin
            ).astype(bf16)
    leave_now(queries, queries_out)
    leave_now(keys, keys_out)
    leave_now(values, values_out)
    for start, size, low in query_blocks(length):
        high = start + size
        stacked = stack_heads(queries, start, size, heads, width)
        permit = allowed(seg_column, seg_row, start, size, low, high)
        weights, total = weights_of(stacked, keys[low:high, :], permit, heads, scale)
        probs = (weights / total).astype(bf16)
        result = dot(probs, values[low:high, :]).astype(bf16)
        for h in range(heads):
            mixed[start:high, h * width : (h + 1) * width] = result[h * size : (h + 1) * size]
    for r in range(count):
        there = pl.ds(pl.multiple_of(table[r] * rows, rows), rows)
        mixed_there[r * rows : (r + 1) * rows, :] = mixed[there, :]
    for copy in leaving:
        copy.wait()


def brief():
    return pl.CostEstimate(flops=1024, bytes_accessed=1024, transcendentals=0)


def vmem():
    return pl.BlockSpec(memory_space=pltpu.VMEM)


def smem():
    return pl.BlockSpec(memory_space=pltpu.SMEM)


def attend_forward(table, pieces, weight, cosine, sine, segments, heads, width, scale):
    count = len(pieces)
    length = cosine.shape[0]
    rank = weight.shape[0]
    shapes = [
        jax.ShapeDtypeStruct((length, rank), bf16),
        jax.ShapeDtypeStruct((length, heads * width), bf16),
        jax.ShapeDtypeStruct((length, width), bf16),
        jax.ShapeDtypeStruct((length, width), bf16),
        jax.ShapeDtypeStruct((length, heads * width), bf16),
    ]
    return pl.pallas_call(
        functools.partial(attend_forward_kernel, count, heads, width, rank, scale),
        out_shape=shapes,
        in_specs=[smem()] + [vmem()] * (count + 5),
        out_specs=[any_space()] * 4 + [vmem()],
        scratch_shapes=[
            pltpu.VMEM((length, heads * width), bf16),
            pltpu.VMEM((length, width), bf16),
            pltpu.VMEM((length, width), bf16),
            pltpu.VMEM((length, heads * width), bf16),
            pltpu.SemaphoreType.DMA((count + 3,)),
        ],
        compiler_params=pltpu.CompilerParams(vmem_limit_bytes=48 << 20),
        cost_estimate=brief(),
        name="attend_forward",
    )(table, *pieces, weight, cosine, sine, segments[:, None], segments[None, :])


def attend_backward_kernel(parts, heads, width, scale, *refs):
    table = refs[0]
    grads_in = refs[1 : 1 + parts]
    queries, keys, values, cosine, sine, seg_column, seg_row = refs[1 + parts : 8 + parts]
    query_out, pair_out, outer, key_total, value_total = refs[8 + parts :]
    length = queries.shape[0]
    count = table.shape[0]
    rows = length // count
    half = width // 2

    def there(r):
        return pl.ds(pl.multiple_of(table[r] * rows, rows), rows)

    r = 0
    for part in grads_in:
        for k in range(part.shape[0] // rows):
            outer[there(r), :] = part[k * rows : (k + 1) * rows, :]
            r += 1
    key_total[...] = jnp.zeros_like(key_total)
    value_total[...] = jnp.zeros_like(value_total)
    for start, size, low in query_blocks(length):
        high = start + size
        stacked = stack_heads(queries, start, size, heads, width)
        grads = stack_heads(outer, start, size, heads, width)
        permit = allowed(seg_column, seg_row, start, size, low, high)
        weights, total = weights_of(stacked, keys[low:high, :], permit, heads, scale)
        probs = weights / total
        prob_grad = right_transposed(grads, values[low:high, :])
        centre = jnp.sum(probs * prob_grad, axis=-1, keepdims=True)
        score_grad = (probs * (prob_grad - centre)).astype(bf16)
        query_grad = dot(score_grad, keys[low:high, :]) * scale
        key_total[low:high, :] += left_transposed(score_grad, stacked) * scale
        value_total[low:high, :] += left_transposed(probs.astype(bf16), grads)
        cos = cosine[start:high, :]
        sin = sine[start:high, :]
        for h in range(heads):
            first = query_grad[h * size : (h + 1) * size, :half]
            second = query_grad[h * size : (h + 1) * size, half:]
            query_out[start:high, h * width : h * width + half] = (
                first * cos + second * sin
            ).astype(bf16)
            query_out[start:high, h * width + half : (h + 1) * width] = (
                second * cos - first * sin
            ).astype(bf16)
    pair_out[:, :width] = key_total[...].astype(bf16)
    pair_out[:, width:] = value_total[...].astype(bf16)


def attend_backward(table, grads, queries, keys, values, cosine, sine, segments, heads, scale):
    parts = len(grads)
    length, width = keys.shape
    shapes = [
        jax.ShapeDtypeStruct((length, heads * width), bf16),
        jax.ShapeDtypeStruct((length, 2 * width), bf16),
    ]
    return pl.pallas_call(
        functools.partial(attend_backward_kernel, parts, heads, width, scale),
        out_shape=shapes,
        in_specs=[smem()] + [vmem()] * (parts + 7),
        out_specs=[vmem()] * 2,
        scratch_shapes=[
            pltpu.VMEM((length, heads * width), bf16),
            pltpu.VMEM((length, width), f32),
            pltpu.VMEM((length, width), f32),
        ],
        compiler_params=pltpu.CompilerParams(vmem_limit_bytes=44 << 20),
        cost_estimate=brief(),
        name="attend_backward",
    )(
        table,
        *grads,
        queries,
        keys,
        values,
        cosine,
        sine,
        segments[:, None],
        segments[None, :],
    )


def rows_product_kernel(*refs):
    pieces, weight, out = refs[:-2], refs[-2], refs[-1]
    rows = pieces[0].shape[0]
    for p in range(0, len(pieces), 2):
        here = jnp.concatenate([pieces[p][...], pieces[p + 1][...]], axis=0)
        out[p * rows : (p + 2) * rows, :] = right_transposed(here, weight[...]).astype(out.dtype)


def rows_product(pieces, weight, kind):
    return pl.pallas_call(
        rows_product_kernel,
        out_shape=jax.ShapeDtypeStruct(
            (len(pieces) * pieces[0].shape[0], weight.shape[0]), kind
        ),
        in_specs=[vmem()] * (len(pieces) + 1),
        out_specs=vmem(),
        compiler_params=pltpu.CompilerParams(vmem_limit_bytes=36 << 20),
        cost_estimate=brief(),
        name="rows_product",
    )(*pieces, weight)


def latent_share_kernel(low, size, table, query_grads, pairs, weight, *refs):
    outs = refs[:-3]
    held, beside, sems = refs[-3:]
    rows = outs[0].shape[0]
    rank = weight.shape[0]
    copies = []
    for k in range(size // rows):
        there = pl.ds(pl.multiple_of(table[low + k] * rows, rows), rows)
        here = pl.ds(k * rows, rows)
        copies += [
            pltpu.make_async_copy(query_grads.at[there, :], held.at[here, :], sems.at[0, k]),
            pltpu.make_async_copy(pairs.at[there, :], beside.at[here, :], sems.at[1, k]),
        ]
    for copy in copies:
        copy.start()
    for copy in copies:
        copy.wait()
    for p in range(0, size // rows, 2):
        total = right_transposed(held[p * rows : (p + 2) * rows, :], weight[...])
        for k in range(2):
            outs[p + k][:, :rank] = total[k * rows : (k + 1) * rows].astype(bf16)
            outs[p + k][:, rank:] = beside[(p + k) * rows : (p + k + 1) * rows, :]


def latent_shares(table, query_grads, pairs, weight):
    count = table.shape[0]
    rows = query_grads.shape[0] // count
    rank, inner = weight.shape
    extra = pairs.shape[1]

    def share(clock, low, high):
        size = (high - low) * rows
        return pl.pallas_call(
            functools.partial(latent_share_kernel, low, size),
            out_shape=[jax.ShapeDtypeStruct((rows, rank + extra), bf16)] * (high - low),
            in_specs=[smem(), any_space(), any_space(), vmem()],
            out_specs=[vmem()] * (high - low),
            scratch_shapes=[
                pltpu.VMEM((size, inner), bf16),
                pltpu.VMEM((size, extra), bf16),
                pltpu.SemaphoreType.DMA((2, high - low)),
            ],
            compiler_params=pltpu.CompilerParams(vmem_limit_bytes=36 << 20),
            cost_estimate=brief(),
            name="latent_share",
        )(table, *clock(query_grads, pairs), weight)

    return share


def join_kernel(count, *refs):
    pieces, whole = refs[:count], refs[count]
    rows = pieces[0].shape[0]
    for r in range(count):
        whole[r * rows : (r + 1) * rows, :] = pieces[r][...]


def join(pieces):
    count = len(pieces)
    rows, columns = pieces[0].shape
    step = min(columns, 512)
    return pl.pallas_call(
        functools.partial(join_kernel, count),
        grid=(columns // step,),
        out_shape=jax.ShapeDtypeStruct((count * rows, columns), bf16),
        in_specs=[pl.BlockSpec((rows, step), lambda j: (0, j))] * count,
        out_specs=pl.BlockSpec((count * rows, step), lambda j: (0, j)),
        compiler_params=pltpu.CompilerParams(vmem_limit_bytes=17 << 20),
        cost_estimate=brief(),
        name="join",
    )(*pieces)


def any_space():
    return pl.BlockSpec(memory_space=pl.ANY)


def share_kernel(low, size, terms, *refs):
    lefts = refs[:terms]
    weights = refs[terms : 2 * terms]
    outs = refs[2 * terms : -terms - 1]
    held, sems = refs[-terms - 1 : -1], refs[-1]
    rows = outs[0].shape[0]
    copies = []
    for t in range(terms):
        copy = pltpu.make_async_copy(lefts[t].at[pl.ds(low * rows, size), :], held[t], sems.at[t])
        copy.start()
        copies.append(copy)
    for copy in copies:
        copy.wait()
    for p in range(size // (2 * rows)):
        here = pl.ds(2 * p * rows, 2 * rows)
        total = dot(held[0][here, :], weights[0][...])
        for t in range(1, terms):
            total = total + dot(held[t][here, :], weights[t][...])
        outs[2 * p][...] = total[:rows].astype(bf16)
        outs[2 * p + 1][...] = total[rows:].astype(bf16)


def shares(lefts, weights, count):
    rows = lefts[0].shape[0] // count
    inner = lefts[0].shape[1]
    columns = weights[0].shape[1]
    terms = len(lefts)

    def share(clock, low, high):
        size = (high - low) * rows
        return pl.pallas_call(
            functools.partial(share_kernel, low, size, terms),
            out_shape=[jax.ShapeDtypeStruct((rows, columns), bf16)] * (high - low),
            in_specs=[any_space()] * terms + [vmem()] * terms,
            out_specs=[vmem()] * (high - low),
            scratch_shapes=[pltpu.VMEM((size, inner), bf16)] * terms
            + [pltpu.SemaphoreType.DMA((terms,))],
            compiler_params=pltpu.CompilerParams(vmem_limit_bytes=36 << 20),
            cost_estimate=brief(),
            name="share",
        )(*clock.all(*lefts), *weights)

    return share


def feed_kernel(pairs, first, *refs):
    pieces = refs[: 2 * pairs]
    upper, gate_weight, up_weight = refs[2 * pairs : 2 * pairs + 3]
    rest = refs[2 * pairs + 3 :]
    outs, held, buffers, sems = rest[-8:-5], rest[-5], rest[-4:-1], rest[-1]
    rows = pieces[0].shape[0]

    def rows_of(p):
        return pl.ds((first + p) * 2 * rows, 2 * rows)

    loads = []
    for p in range(pairs):
        load = pltpu.make_async_copy(upper.at[rows_of(p), :], held.at[p], sems.at[3, p])
        load.start()
        loads.append(load)
    copies = []
    for p in range(pairs):
        here = jnp.concatenate([pieces[2 * p][...], pieces[2 * p + 1][...]], axis=0)
        gate = right_transposed(here, gate_weight[...])
        upward = right_transposed(here, up_weight[...])
        loads[p].wait()
        hidden_grad = held[p]
        sigmoid = jax.nn.sigmoid(gate)
        swish = gate * sigmoid
        results = (
            swish * upward,
            hidden_grad * upward * sigmoid * (1.0 + gate * (1.0 - sigmoid)),
            hidden_grad * swish,
        )
        for k, result in enumerate(results):
            buffers[k][p] = result.astype(bf16)
            copy = pltpu.make_async_copy(buffers[k].at[p], outs[k].at[rows_of(p), :], sems.at[k, p])
            copy.start()
            copies.append(copy)
    for copy in copies:
        copy.wait()


def feed(pieces, low, high, upper, gate_weight, up_weight, count, past):
    rows, dim = pieces[low].shape
    units = gate_weight.shape[0]
    pairs = (high - low) // 2
    operands = list(pieces[low:high]) + [upper, gate_weight, up_weight]
    specs = [vmem()] * (high - low) + [any_space()] + [vmem()] * 2
    aliases = {}
    if past is not None:
        aliases = {len(operands) + k: k for k in range(3)}
        operands += list(past)
        specs += [any_space()] * 3
    size = (high - low) * rows
    return pl.pallas_call(
        functools.partial(feed_kernel, pairs, low // 2),
        out_shape=[jax.ShapeDtypeStruct((count * rows, units), bf16)] * 3,
        in_specs=specs,
        out_specs=[any_space()] * 3,
        scratch_shapes=[pltpu.VMEM((pairs, 2 * rows, units), f32)]
        + [pltpu.VMEM((pairs, 2 * rows, units), bf16)] * 3
        + [pltpu.SemaphoreType.DMA((4, pairs))],
        input_output_aliases=aliases,
        compiler_params=pltpu.CompilerParams(vmem_limit_bytes=28 << 20),
        cost_estimate=brief(),
        name="feed",
    )(*operands)


def sum_kernel(*refs):
    total = refs[0][...].astype(f32)
    for ref in refs[1:-1]:
        total = total + ref[...].astype(f32)
    refs[-1][...] = total.astype(bf16)


def call(kernel, shapes, operands, name, scalars=0, limit=24, scratch=()):
    single = not isinstance(shapes, list)
    return pl.pallas_call(
        kernel,
        out_shape=shapes,
        in_specs=[smem()] * scalars + [vmem()] * (len(operands) - scalars),
        out_specs=vmem() if single else [vmem()] * len(shapes),
        scratch_shapes=list(scratch),
        compiler_params=pltpu.CompilerParams(vmem_limit_bytes=limit << 20),
        cost_estimate=brief(),
        name=name,
    )(*operands)


def shaped(shape, kind):
    return jax.ShapeDtypeStruct(shape, kind)


def add_rows(*values):
    return call(sum_kernel, shaped(values[0].shape, bf16), values, "add_rows")


def add_or_begin_kernel(inner, own, came, value, out):
    @pl.when(inner[0] == 1)
    def _():
        out[...] = (own[...].astype(f32) + came[...].astype(f32)).astype(bf16)

    @pl.when(inner[0] == 0)
    def _():
        out[...] = value[...]


def add_or_begin(inner, own, came, value):
    return call(
        add_or_begin_kernel,
        shaped(own.shape, bf16),
        [inner, own, came, value],
        "add_or_begin",
        scalars=1,
    )


def settle_kernel(low, at, *refs):
    inner, own, came = refs[:3]
    out, buffer, sem = refs[-3:]
    rows = buffer.shape[0]

    @pl.when(inner[0] == 1)
    def _():
        buffer[...] = own[low : low + rows, :].astype(f32)

    @pl.when(inner[0] == 0)
    def _():
        buffer[...] = came[low : low + rows, :].astype(f32)

    copy = pltpu.make_async_copy(buffer, out.at[pl.ds(at, rows), :], sem)
    copy.start()
    copy.wait()


def settle(inner, own, came, size, at=0, past=None, low=0, high=None):
    columns = own.shape[1]
    rows = (high or own.shape[0]) - low
    operands = [inner, own, came]
    specs = [smem(), vmem(), vmem()]
    aliases = {}
    if past is not None:
        aliases = {3: 0}
        operands.append(past)
        specs.append(any_space())
    return pl.pallas_call(
        functools.partial(settle_kernel, low, at),
        out_shape=shaped((size, columns), f32),
        in_specs=specs,
        out_specs=any_space(),
        scratch_shapes=[pltpu.VMEM((rows, columns), f32), pltpu.SemaphoreType.DMA],
        input_output_aliases=aliases,
        compiler_params=pltpu.CompilerParams(vmem_limit_bytes=16 << 20),
        cost_estimate=brief(),
        name="settle",
    )(*operands)


def product_kernel(count, first, step, left, *refs):
    pieces = refs[:count]
    outs, held, sems = refs[count + first : -2], refs[-2], refs[-1]
    rows = pieces[0].shape[0]
    here = pl.program_id(0)
    steps = pl.num_programs(0)

    def copies(j, slot):
        there = pl.ds(pl.multiple_of(j * step, step), step)
        return [
            pltpu.make_async_copy(
                pieces[r].at[:, there], held.at[slot, pl.ds(r * rows, rows), :], sems.at[slot, r]
            )
            for r in range(count)
        ]

    slot = lax.rem(here, 2)

    @pl.when(here == 0)
    def _():
        for copy in copies(0, 0):
            copy.start()

    @pl.when(here + 1 < steps)
    def _():
        for copy in copies(here + 1, 1 - slot):
            copy.start()

    for copy in copies(here, slot):
        copy.wait()
    total = left_transposed(left[...], held[slot]).astype(bf16)
    if first:
        total = jnp.concatenate([refs[count][...], total], axis=0)
    low = 0
    for out in outs:
        size = out.shape[0]
        out[...] = total[low : low + size]
        low += size


def weight_product(left, right, rows, above=None, step=1024):
    right = list(right) if isinstance(right, (list, tuple)) else [right]
    count = len(right)
    tokens, units = left.shape
    columns = right[0].shape[1]
    step = min(step, columns)
    operands = [left, *right]
    specs = [pl.BlockSpec((tokens, units), lambda j: (0, 0))] + [any_space()] * count
    if above is not None:
        operands.append(above)
        specs.append(pl.BlockSpec((above.shape[0], step), lambda j: (0, j)))
    return pl.pallas_call(
        functools.partial(product_kernel, count, len(operands) - 1 - count, step),
        grid=(columns // step,),
        out_shape=[shaped((one, columns), bf16) for one in rows],
        in_specs=specs,
        out_specs=[pl.BlockSpec((one, step), lambda j: (0, j)) for one in rows],
        scratch_shapes=[
            pltpu.VMEM((2, tokens, step), bf16),
            pltpu.SemaphoreType.DMA((2, count)),
        ],
        compiler_params=pltpu.CompilerParams(vmem_limit_bytes=30 << 20),
        cost_estimate=brief(),
        name="weight_product",
    )(*operands)


def pack_last_kernel(above, wide, below, out):
    top = above.shape[0]
    rows, columns = wide.shape
    parts = out.shape[1] // columns
    step = rows // parts
    out[:top, :] = above[...]
    for j in range(parts):
        out[top : top + step, j * columns : (j + 1) * columns] = wide[j * step : (j + 1) * step, :]
    out[top + step :, :] = below[...]


def pack_last(above, wide, below):
    columns = above.shape[1]
    rows = above.shape[0] + wide.size // columns + below.shape[0]
    return call(
        pack_last_kernel, shaped((rows, columns), bf16), [above, wide, below], "pack_last"
    )


def settle_last_kernel(top, at, inner, own, came, past, wide, below, whole, buffer, sem):
    rows, columns = wide.shape
    parts = own.shape[1] // columns
    step = rows // parts

    def write(source):
        buffer[...] = source[:top, :].astype(f32)
        copy = pltpu.make_async_copy(buffer, whole.at[pl.ds(at, top), :], sem)
        copy.start()
        for j in range(parts):
            wide[j * step : (j + 1) * step, :] = source[
                top : top + step, j * columns : (j + 1) * columns
            ].astype(f32)
        below[...] = source[top + step :, :].astype(f32)
        copy.wait()

    @pl.when(inner[0] == 1)
    def _():
        write(own)

    @pl.when(inner[0] == 0)
    def _():
        write(came)


def settle_last(inner, own, came, top, rows, columns, past, at):
    total, dim = own.shape
    left = total - top - rows * columns // dim
    return pl.pallas_call(
        functools.partial(settle_last_kernel, top, at),
        out_shape=[
            shaped((rows, columns), f32),
            shaped((left, dim), f32),
            shaped(past.shape, f32),
        ],
        in_specs=[smem(), vmem(), vmem(), any_space()],
        out_specs=[vmem(), vmem(), any_space()],
        scratch_shapes=[pltpu.VMEM((top, dim), f32), pltpu.SemaphoreType.DMA],
        input_output_aliases={3: 2},
        compiler_params=pltpu.CompilerParams(vmem_limit_bytes=24 << 20),
        cost_estimate=brief(),
        name="settle_last",
    )(inner, own, came, past)


def pack_kernel(count, *refs):
    total = summed(refs[:count]).astype(bf16)
    beside, out = refs[count:]
    rows, columns = total.shape
    tall = rows * 3 // 4
    out[:tall, :columns] = total[:tall]
    third = columns // 3
    for j in range(3):
        low = j * (rows - tall)
        out[low : low + rows - tall, columns:] = total[tall:, j * third : (j + 1) * third]
    out[tall:, :] = beside[...]


def pack(parts, beside):
    rows, columns = parts[0].shape
    tall = rows * 3 // 4
    return call(
        functools.partial(pack_kernel, len(parts)),
        shaped((tall + beside.shape[0], beside.shape[1]), bf16),
        [*parts, beside],
        "pack",
    )


def pick_kernel(inner, own, came, out):
    rows = out.shape[0]

    @pl.when(inner[0] == 1)
    def _():
        out[...] = own[:rows, :]

    @pl.when(inner[0] == 0)
    def _():
        out[...] = came[:rows, :]


def pick(inner, own, came, rows):
    return call(
        pick_kernel,
        shaped((rows, own.shape[1]), bf16),
        [inner, own, came],
        "pick",
        scalars=1,
    )


def widen_kernel(*refs):
    out = refs[-1]
    low = 0
    for x in refs[:-1]:
        rows = x.shape[0]
        out[low : low + rows, :] = x[...].astype(f32)
        low += rows


def widen(parts, step=512):
    rows = sum(part.shape[0] for part in parts)
    columns = parts[0].shape[1]
    return pl.pallas_call(
        widen_kernel,
        grid=(columns // step,),
        out_shape=shaped((rows, columns), f32),
        in_specs=[pl.BlockSpec((part.shape[0], step), lambda j: (0, j)) for part in parts],
        out_specs=pl.BlockSpec((rows, step), lambda j: (0, j)),
        compiler_params=pltpu.CompilerParams(vmem_limit_bytes=16 << 20),
        cost_estimate=brief(),
        name="widen",
    )(*parts)


def settle_two_kernel(inner, own, came, above, below):
    rows = above.shape[0]

    @pl.when(inner[0] == 1)
    def _():
        above[...] = own[:rows, :].astype(f32)
        below[...] = own[rows:, :].astype(f32)

    @pl.when(inner[0] == 0)
    def _():
        above[...] = came[:rows, :].astype(f32)
        below[...] = came[rows:, :].astype(f32)


def settle_two(inner, own, came, rows):
    total, columns = own.shape
    return call(
        settle_two_kernel,
        [shaped((rows, columns), f32), shaped((total - rows, columns), f32)],
        [inner, own, came],
        "settle_two",
        scalars=1,
    )


def rotated(first, second, cosine, sine):
    return first * cosine - second * sine, second * cosine + first * sine


def enter_kernel(rank, width, x, gain, down, latent_gain, key, value, cosine, sine, *outs):
    normed, latent, packed = outs
    half = width // 2
    rows = x[...].astype(f32)
    low = (rows * inverse_rms(rows) * gain[...]).astype(bf16)
    normed[...] = low
    inner = dot(low, down[...])
    latent[...] = inner
    packed[:, :rank] = (inner * inverse_rms(inner) * latent_gain[...]).astype(bf16)
    keys = dot(low, key[...])
    first, second = rotated(keys[:, :half], keys[:, half:], cosine[...], sine[...])
    packed[:, rank : rank + half] = first.astype(bf16)
    packed[:, rank + half : rank + width] = second.astype(bf16)
    packed[:, rank + width :] = dot(low, value[...]).astype(bf16)


def enter(x, gain, down, latent_gain, key, value, cosine, sine):
    rows, dim = x.shape
    rank, width = down.shape[1], key.shape[1]
    return call(
        functools.partial(enter_kernel, rank, width),
        [shaped((rows, dim), bf16), shaped((rows, rank), f32), shaped((rows, rank + 2 * width), bf16)],
        [x, gain[None], down, latent_gain[None], key, value, cosine, sine],
        "enter",
        limit=60,
    )


def summed(parts):
    total = parts[0][...].astype(f32)
    for part in parts[1:]:
        total = total + part[...].astype(f32)
    return total


def middle_kernel(x, gain, *refs):
    parts, (middle, normed) = refs[:-2], refs[-2:]
    total = x[...].astype(f32) + summed(parts)
    middle[...] = total
    normed[...] = (total * inverse_rms(total) * gain[...]).astype(bf16)


def middle_rows(x, gain, parts):
    shape = x.shape
    return call(
        middle_kernel,
        [shaped(shape, f32), shaped(shape, bf16)],
        [x, gain[None], *parts],
        "middle_rows",
    )


def lower_norm(value, gain, upper):
    scale = inverse_rms(value)
    scaled = upper * gain
    lower = scale * scaled - value * (scale * scale * scale) * jnp.mean(
        scaled * value, axis=-1, keepdims=True
    )
    return lower, jnp.sum(upper * value * scale, axis=0, keepdims=True)


def middle_back_kernel(middle, gain, cotangent, *refs):
    parts, (total, low, gain_part) = refs[:-3], refs[-3:]
    lower, gain_part[...] = lower_norm(middle[...], gain[...], summed(parts))
    result = cotangent[...].astype(f32) + lower
    total[...] = result
    low[...] = result.astype(bf16)


def middle_back(middle, gain, cotangent, parts):
    shape = middle.shape
    return call(
        middle_back_kernel,
        [shaped(shape, f32), shaped(shape, bf16), shaped((1, shape[1]), f32)],
        [middle, gain[None], cotangent, *parts],
        "middle_back",
    )


def latent_back_kernel(latent, gain, cosine, sine, *refs):
    parts, (packed, gain_part) = refs[:-2], refs[-2:]
    rank = latent.shape[1]
    total = summed(parts)
    lower, gain_part[...] = lower_norm(latent[...], gain[...], total[:, :rank])
    width = (total.shape[1] - rank) // 2
    half = width // 2
    packed[:, :rank] = lower.astype(bf16)
    first, second = rotated(
        total[:, rank : rank + half], total[:, rank + half : rank + width], cosine[...], -sine[...]
    )
    packed[:, rank : rank + half] = first.astype(bf16)
    packed[:, rank + half : rank + width] = second.astype(bf16)
    packed[:, rank + width :] = total[:, rank + width :].astype(bf16)


def latent_back(latent, gain, cosine, sine, parts):
    shape = parts[0].shape
    return call(
        latent_back_kernel,
        [shaped(shape, bf16), shaped((1, latent.shape[1]), f32)],
        [latent, gain[None], cosine, sine, *parts],
        "latent_back",
    )


def leave_kernel(packed, down, key, value, x, gain, upper, result, gain_part):
    rank, width = down.shape[1], key.shape[1]
    total = right_transposed(packed[:, :rank], down[...])
    total = total + right_transposed(packed[:, rank : rank + width], key[...])
    total = total + right_transposed(packed[:, rank + width :], value[...])
    lower, gain_part[...] = lower_norm(x[...].astype(f32), gain[...], total)
    result[...] = upper[...] + lower


def leave(packed, down, key, value, x, gain, upper):
    return call(
        leave_kernel,
        [shaped(x.shape, f32), shaped((1, x.shape[1]), f32)],
        [packed, down, key, value, x, gain[None], upper],
        "leave",
    )


def shared_kernel(count, table, normed, grads, *outs):
    rows = outs[0].shape[0]
    for r in range(count):
        there = pl.ds(pl.multiple_of(table[r] * rows, rows), rows)
        outs[r][...] = left_transposed(normed[:, there], grads[...]).astype(bf16)


def shared_shares(table, normed, grads):
    count = table.shape[0]
    rows = normed.shape[1] // count
    columns = grads.shape[1]
    return list(
        pl.pallas_call(
            functools.partial(shared_kernel, count),
            out_shape=[jax.ShapeDtypeStruct((rows, columns), bf16)] * count,
            in_specs=[smem(), vmem(), vmem()],
            out_specs=[vmem()] * count,
            compiler_params=pltpu.CompilerParams(vmem_limit_bytes=36 << 20),
            cost_estimate=brief(),
            name="shared_shares",
        )(table, normed, grads)
    )


def unpack_kernel(base, count, parts, packed, table, *refs):
    pieces = refs[:count]
    outs, buffers = refs[-1 - 2 * len(parts) : -1 - len(parts)], refs[-1 - len(parts) : -1]
    sems = refs[-1]
    rows = buffers[0].shape[1]
    tall = rows * 3 // 4
    columns = parts[-1][1]
    third = columns // 3
    flying = []
    for r in range(count):
        slot = r % 2
        if r >= 2:
            for copy in flying[r - 2]:
                copy.wait()
        there = pl.ds(pl.multiple_of(table[base + r] * rows, rows), rows)
        copies = []
        for k, (low, high) in enumerate(parts):
            if packed:
                buffers[k][slot, :tall, :] = pieces[r][:, low:high].astype(f32)
                for j in range(3):
                    first, last = max(low, j * third), min(high, (j + 1) * third)
                    if first < last:
                        start = columns - j * third
                        buffers[k][slot, tall:, first - low : last - low] = pieces[r][
                            j * (rows - tall) : (j + 1) * (rows - tall),
                            start + first : start + last,
                        ].astype(f32)
            else:
                buffers[k][slot] = pieces[r][:, low:high].astype(f32)
            copy = pltpu.make_async_copy(
                buffers[k].at[slot], outs[k].at[there, :], sems.at[k, slot]
            )
            copy.start()
            copies.append(copy)
        flying.append(copies)
    for copies in flying[-2:]:
        for copy in copies:
            copy.wait()


def unpack(table, pieces, parts, packed, first=0, past=None):
    count = len(pieces)
    rows = pieces[0].shape[0]
    if packed:
        rows = rows * 4 // 3
    past = [] if past is None else list(past)
    return pl.pallas_call(
        functools.partial(unpack_kernel, first, count, parts, packed),
        out_shape=[
            jax.ShapeDtypeStruct((table.shape[0] * rows, high - low), f32) for low, high in parts
        ],
        in_specs=[smem()] + [vmem()] * count + [any_space()] * len(past),
        out_specs=[any_space()] * len(parts),
        scratch_shapes=[pltpu.VMEM((2, rows, high - low), f32) for low, high in parts]
        + [pltpu.SemaphoreType.DMA((len(parts), 2))],
        input_output_aliases={1 + count + k: k for k in range(len(past))},
        compiler_params=pltpu.CompilerParams(vmem_limit_bytes=24 << 20),
        cost_estimate=brief(),
        name="unpack",
    )(table, *pieces, *past)


def body(
    packs,
    group,
    block_input,
    segment_ids,
    positions,
    attention_gain,
    query_down,
    query_gain,
    query_up,
    key_proj,
    value_proj,
    out_proj,
    feed_gain,
    gate_weight,
    up_weight,
    down_weight,
    out_grad,
):
    plane = Plane(group)
    line = Line(packs)
    rows = block_input.shape[1]
    segments = segment_ids[0]
    places = positions[0]
    width = key_proj.shape[1]
    rank = query_down.shape[1]
    heads = query_up.shape[1] // width
    scale = 1.0 / math.sqrt(width)
    first_row = plane.me * rows

    gate_rows, up_rows = gate_weight.T, up_weight.T
    clock = Clock()
    belt = Belt(line, clock)
    fast = plane.fast
    move = plane.move
    hop_a, hop_b, hop_c = (plane.hop_a, plane.hop_b, plane.hop_c) if fast else (None,) * 3
    cotangent_rows = out_grad[0]

    x = block_input[0]
    dim = x.shape[1]
    always = (segments[0] & 1) <= 1

    def stage(run):
        def inside():
            inner = Clock()
            inner.last = clock.last
            return tuple(run(inner))

        if not fast:
            return inside()
        shapes = jax.eval_shape(inside)
        result = lax.cond(
            always, inside, lambda: tuple(jnp.zeros(one.shape, one.dtype) for one in shapes)
        )
        return clock.all(*result)

    def hops(values, ways, filler=None, apart=False):
        def run(clock):
            held = clock.all(*values)
            came = [move(value, way) for value, way in zip(held, ways)]
            more = list(filler(clock, *came)) if filler else []
            return [*clock.all(*came), *more]

        result = stage(run) if apart else run(clock)
        return list(result[: len(values)]), list(result[len(values) :])

    def gather(rows, first=None, second=None, apart=False, between=None, last=False):
        def beside(clock, a, b, s_o):
            return first(clock, [rows, clock(s_o)]) if first else []

        (a, b, s_o), more = hops([rows, rows, rows], [hop_a, hop_b, hop_c], beside, apart)
        if between:
            between()

        def beside(clock, c, a_o, b_o):
            if not second:
                return []
            a_o, b_o = clock(a_o, b_o)
            return second(clock, [a, a_o, b, b_o], more)

        (c, a_o, b_o), later = hops([a, a, b], [hop_b, hop_c, hop_c], beside, apart)
        (c_o,), _ = hops([c], [hop_c], None, apart or last)
        return [rows, s_o, a, a_o, b, b_o, c, c_o], more, later

    def scatter(share, filler=None, apart=False, between=None, head=False):
        c, c_send = clock(*share(clock, 6, 8))
        (c_came,), near = hops(
            [c_send], [hop_c], lambda clock, came: clock(*share(clock, 2, 6)), apart or head
        )
        a, a_send, b, b_send = near
        c = clock(add_rows(c, c_came))
        (c_in, a_came, b_came), (own, own_send) = hops(
            [c, a_send, b_send],
            [hop_b, hop_c, hop_c],
            lambda clock, *came: clock(*share(clock, 0, 2)),
            apart,
        )
        a, b = clock(add_rows(a, a_came, c_in), add_rows(b, b_came))
        if between:
            between()
        (a_in, b_in, own_came), more = hops(
            [a, b, own_send],
            [hop_a, hop_b, hop_c],
            (lambda clock, *came: filler(clock)) if filler else None,
            apart,
        )
        return [own, own_came, b_in, a_in], more

    own_places = lax.dynamic_slice_in_dim(places, first_row, rows, 0)
    own_cosine, own_sine = rotation(own_places, width)

    def enter_rows():
        return enter(
            x, attention_gain, query_down, query_gain, key_proj, value_proj, own_cosine, own_sine
        )

    def attend(pieces, cosine, sine):
        return attend_forward(
            plane.table, pieces, query_up, cosine, sine, segments, heads, width, scale
        )

    def attend_back(outer):
        return attend_backward(
            plane.table, outer, queries, keys, values, cosine, sine, segments, heads, scale
        )

    def leave_rows(packed_grad):
        return leave(
            packed_grad, query_down, key_proj, value_proj, x, attention_gain, middle_grad
        )

    def sum_gains(parts, total):
        return total(jnp.concatenate(parts, axis=1))

    units = gate_rows.shape[0]
    size = heads * width
    columns = ((0, rank), (rank, rank + width), (rank + width, rank + 2 * width))
    add = lambda left, right: left + right

    if not fast:
        normed_rows, latent, packed = enter_rows()
        cosine, sine = rotation(places, width)
        pieces = plane.gather(packed)
        latents, queries, keys, values, mixed_there = attend(pieces, cosine, sine)
        share = shares([mixed_there], [out_proj], group)
        parts = [plane.scatter(share(clock, 0, group))]
        middle, normed_mid_rows = middle_rows(x, feed_gain, parts)
        cot_pieces = plane.gather(cotangent_rows)
        hidden_grad = rows_product(cot_pieces, down_weight, f32)
        mid_pieces = plane.gather(normed_mid_rows)
        hidden, gate_grad, upward_grad = feed(
            mid_pieces, 0, group, hidden_grad, gate_rows, up_rows, group, None
        )
        cotangent, normed_mid = join(cot_pieces), join(mid_pieces)
        share = shares([gate_grad, upward_grad], [gate_rows, up_rows], group)
        parts = [plane.scatter(share(clock, 0, group))]
        middle_grad, attention_grad, feed_gain_part = middle_back(
            middle, feed_gain, cotangent_rows, parts
        )
        grad_pieces = plane.gather(attention_grad)
        outer = [rows_product(grad_pieces, out_proj, bf16)]
        query_pre_grad, pair_grads = attend_back(outer)
        share = latent_shares(plane.table, query_pre_grad, pair_grads, query_up)
        parts = [plane.scatter(share(clock, 0, group))]
        packed_grad, query_gain_part = latent_back(latent, query_gain, own_cosine, own_sine, parts)
        shared_pieces = shared_shares(plane.table, normed_rows, packed_grad)
        shared = line.total(plane.scatter(list(shared_pieces)).astype(bf16))
        query_down_gradient, key_proj_gradient, value_proj_gradient = unpack(
            plane.table, plane.gather(shared), columns, False
        )
        input_gradient, attention_gain_part = leave_rows(packed_grad)
        share = shares([hidden], [down_weight], group)
        block_output = add_rows(middle, plane.scatter(share(clock, 0, group)))
        gains = sum_gains([attention_gain_part, query_gain_part, feed_gain_part], plane.total)
        gains = line.total(gains, add)[0]
        down_gradient, gate_gradient, up_gradient, proj_gradient, query_up_gradient = (
            line.total(weight_product(left, right, [left.shape[1]])[0]).astype(f32)
            for left, right in (
                (hidden, cotangent),
                (gate_grad, normed_mid),
                (upward_grad, normed_mid),
                (mixed_there, join(grad_pieces)),
                (latents, query_pre_grad),
            )
        )
    else:
        half = units // 2
        cot_a = move(cotangent_rows, hop_a)
        normed_rows, latent, packed = enter_rows()
        packed = clock(packed)

        def angles(clock, own):
            return clock(*rotation(clock(places), width))

        pieces, (cosine, sine), _ = gather(packed, angles, apart=True)
        cot_now, cot_a = clock(cotangent_rows, cot_a)
        cot_b, cot_c = move(cot_now, hop_b), move(cot_a, hop_b)
        cot_o, cot_ao = move(cot_now, hop_c), move(cot_a, hop_c)
        pieces[0] = clock(packed)

        latents, queries, keys, values, mixed_there = clock(*attend(pieces, cosine, sine))
        share = shares([mixed_there], [out_proj], group)
        c, c_send = clock(*share(clock, 6, 8))

        def other_shares(clock, came):
            return [*clock(*share(clock, 2, 6)), *clock(*share(clock, 0, 2))]

        (c_came,), (a, a_send, b, b_send, own, own_send) = hops(
            [c_send], [hop_c], other_shares, True
        )
        cot_b, cot_c, cot_o, cot_ao = clock(cot_b, cot_c, cot_o, cot_ao)
        c = clock(add_rows(c, c_came))
        (c_in, a_came, b_came), _ = hops([c, a_send, b_send], [hop_b, hop_c, hop_c])
        a, b = clock(add_rows(a, a_came, c_in), add_rows(b, b_came))

        def beside_last(clock, a_in, b_in, own_came, cot_bo, cot_co):
            cot_bo, cot_co = clock(cot_bo, cot_co)
            cot_pieces = [cotangent_rows, cot_o, cot_a, cot_ao, cot_b, cot_bo, cot_c, cot_co]
            hidden_grad = clock(rows_product(cot_pieces, down_weight, f32))
            return [hidden_grad]

        (a_in, b_in, own_came, cot_bo, cot_co), (hidden_grad,) = hops(
            [a, b, own_send, cot_b, cot_c], [hop_a, hop_b, hop_c, hop_c, hop_c], beside_last
        )
        cot_pieces = [cotangent_rows, cot_o, cot_a, cot_ao, cot_b, cot_bo, cot_c, cot_co]
        middle, normed_mid_rows = clock(*middle_rows(x, feed_gain, [own, own_came, b_in, a_in]))

        def feed_group(clock, pieces, low, high, past):
            pieces = [None] * low + [clock(pieces[0]), *pieces[1:]]
            return clock(
                *feed(pieces, low, high, hidden_grad, gate_rows, up_rows, group, past)
            )

        def near_feed(clock, near):
            return feed_group(clock, near, 0, 2, None)

        (a, b, s_o), past = hops(
            [normed_mid_rows] * 3,
            [hop_a, hop_b, hop_c],
            lambda clock, a, b, s_o: near_feed(clock, [normed_mid_rows, clock(s_o)]),
        )

        def next_feed(clock, c, a_o, b_o):
            a_o, b_o = clock(a_o, b_o)
            more = feed_group(clock, [a, a_o], 2, 4, past)
            return [a_o, b_o, *feed_group(clock, [b, b_o], 4, 6, more)]

        (c, a_o, b_o), past = hops([a, a, b], [hop_b, hop_c, hop_c], next_feed)
        a_o, b_o, *past = past
        (c_o,), _ = hops([c], [hop_c])
        hidden, gate_grad, upward_grad = feed_group(clock, [c, c_o], 6, 8, past)
        mid_pieces = [normed_mid_rows, s_o, a, a_o, b, b_o, c, c_o]
        chunk = units * 3 // 4
        tall = dim * 3 // (4 * group)
        beside = chunk - tall
        one, tail = clock(*weight_product(clock(hidden), cot_pieces, [chunk, units - chunk]))
        one = belt.begin(one)
        two = []

        def middle_filler(clock):
            part, rest = clock(
                *weight_product(clock(gate_grad), mid_pieces, [chunk, units - half], tail)
            )
            two.append(belt.begin(part))
            belt.cross(one)
            return [rest]

        share = shares([gate_grad, upward_grad], [gate_rows, up_rows], group)
        parts, (tail,) = scatter(share, middle_filler, head=True)
        two = two[0]
        middle_grad, attention_grad, feed_gain_part = clock(
            *middle_back(middle, feed_gain, cotangent_rows, parts)
        )

        def near_grad(clock, near):
            outer = clock(rows_product([clock(near[0]), near[1]], out_proj, bf16))
            pair = clock(*weight_product(clock(upward_grad), mid_pieces, [chunk, chunk], tail))
            return [outer, *pair]

        def next_grad(clock, near, more):
            return [clock(rows_product([clock(near[0]), *near[1:]], out_proj, bf16))]

        grad_pieces, (outer_near, three, four), (outer_next,) = gather(
            attention_grad, near_grad, next_grad, last=True
        )
        outer_last = clock(rows_product([clock(grad_pieces[6]), grad_pieces[7]], out_proj, bf16))
        three = belt.back(one, three)
        belt.cross(two)

        query_pre_grad, pair_grads = clock(*attend_back([outer_near, outer_next, clock(outer_last)]))

        def latent_filler(clock):
            return clock(
                *weight_product(clock(mixed_there), grad_pieces, [beside, size - beside])
            )

        share = latent_shares(plane.table, query_pre_grad, pair_grads, query_up)
        parts, (five, six) = scatter(share, latent_filler)
        packed_grad, query_gain_part = clock(
            *latent_back(latent, query_gain, own_cosine, own_sine, parts)
        )
        belt.cross(three)
        four = belt.back(two, four)

        shared_pieces = clock(*shared_shares(plane.table, normed_rows, packed_grad))

        def shared_filler(clock):
            leaving = clock(*leave_rows(clock(packed_grad)))
            product = clock(weight_product(clock(latents), query_pre_grad, [rank])[0])
            belt.land(one)
            return [*leaving, product, clock(belt.end(one, units))]

        parts, (input_gradient, attention_gain_part, query_sum, down_gradient) = scatter(
            lambda clock, low, high: shared_pieces[low:high], shared_filler
        )
        five = clock(pack(parts, five))
        five = belt.back(three, five)
        belt.cross(four)
        fill = -(2 * dim + rank) % (16 * dim)

        def gain_rows(clock):
            gains = sum_gains(
                [clock(attention_gain_part), query_gain_part, feed_gain_part], plane.total
            )
            gains = jnp.concatenate([gains[0], jnp.zeros((fill,), f32)]).reshape(-1, dim)
            return [pack_last(six, query_sum, gains.astype(bf16))]

        (six,) = stage(gain_rows)

        settled = []

        def turn():
            belt.cross(five)
            belt.back(four)
            begun = belt.begin(six)
            belt.land(two)
            down = clock(belt.end(two, units, chunk, down_gradient, 0, units - chunk))
            gate = clock(belt.end(two, units, 0, None, units - chunk))
            belt.land(three)
            gate = clock(belt.end(three, units, half, gate, 0, half))
            up = clock(belt.end(three, units, 0, None, half))
            belt.land(four)
            belt.back(five)
            belt.cross(begun)
            settled.extend([begun, down, gate, up])

        share = shares([hidden], [down_weight], group)
        parts, _ = scatter(share, None, True, turn)
        block_output = clock(add_rows(middle, *parts))
        six, down_gradient, gate_gradient, up_gradient = settled
        up_gradient = clock(belt.end(four, units, chunk - half, up_gradient))
        belt.meet(six)
        belt.land(five)
        belt.send(six)
        shared_rows = clock(pick(belt.inner, five["own"], five["came"], tall))

        def five_end(clock, own):
            held = dict(five, came=clock(five["came"]))
            return [clock(belt.end(held, size, 0, None, tall))]

        def near_unpack(clock, near, more):
            pieces = [shared_rows, s_one, *near]
            return clock(*unpack(plane.table, pieces, columns, True))

        (a, b, s_one), (proj_gradient,) = hops(
            [shared_rows] * 3, [hop_a, hop_b, hop_c], lambda clock, *came: five_end(clock, None), True
        )

        def beside_next(clock, c, a_o, b_o):
            a_o, b_o = clock(a_o, b_o)
            return near_unpack(clock, [a, a_o, b, b_o], None)

        (c, a_o, b_o), past = hops([a, a, b], [hop_b, hop_c, hop_c], beside_next, True)
        (c_o,), _ = hops([c], [hop_c], None, True)
        query_down_gradient, key_proj_gradient, value_proj_gradient = clock(
            *unpack(plane.table, [c, c_o], columns, True, 6, past)
        )
        belt.land(six)
        query_up_gradient, gains, proj_gradient = settle_last(
            belt.inner, six["own"], six["came"], size - beside, rank, size, proj_gradient, beside
        )
        gains = gains.reshape(-1)
    return (
        block_output[None],
        input_gradient[None],
        gains[:dim],
        query_down_gradient,
        gains[dim : dim + rank],
        query_up_gradient,
        key_proj_gradient,
        value_proj_gradient,
        proj_gradient,
        gains[dim + rank : dim + rank + dim],
        gate_gradient.T,
        up_gradient.T,
        down_gradient,
    )


def solution(mesh):
    in_specs = (
        P("tok", "head", None),
        P("tok", None),
        P("tok", None),
        P(),
        P(),
        P(),
        P(None, "head"),
        P(),
        P(),
        P("head", None),
        P(),
        P(None, "head"),
        P(None, "head"),
        P("head", None),
        P("tok", "head", None),
    )
    out_specs = (
        P("tok", "head", None),
        P("tok", "head", None),
        P(),
        P(),
        P(),
        P(None, "head"),
        P(),
        P(),
        P("head", None),
        P(),
        P(None, "head"),
        P(None, "head"),
        P("head", None),
    )
    sizes = dict(mesh.shape)
    return jax.shard_map(
        functools.partial(body, sizes["tok"], sizes["head"]),
        mesh=mesh,
        in_specs=in_specs,
        out_specs=out_specs,
        check_vma=False,
    )
```

```python
import functools
import math

import jax
import jax.numpy as jnp
from jax import lax
from jax.experimental import pallas as pl
from jax.experimental.pallas import tpu as pltpu
from jax.sharding import PartitionSpec as P

norm_epsilon = 1e-05
rope_base = 10000.0
first_document = 1024
bf16 = jnp.bfloat16
f32 = jnp.float32


def inverse_rms(value):
    return lax.rsqrt(jnp.mean(value * value, axis=-1, keepdims=True) + norm_epsilon)


def norm_backward(value, gain, upper):
    scale = inverse_rms(value)
    scaled = upper * gain
    lower = scale * scaled - value * (scale * scale * scale) * jnp.mean(
        scaled * value, axis=-1, keepdims=True
    )
    return (lower, jnp.sum(upper * value * scale, axis=0))


def rotation(places, head_width):
    half = head_width // 2
    steps = jnp.arange(half).astype(f32) * (2.0 / head_width)
    inverse = jnp.exp(steps * -math.log(rope_base))
    angles = places.astype(f32)[:, None] * inverse[None, :]
    return (jnp.cos(angles), jnp.sin(angles))


def rotate(value, cosine, sine):
    half = value.shape[-1] // 2
    first = value[..., :half]
    second = value[..., half:]
    return jnp.concatenate(
        [first * cosine - second * sine, second * cosine + first * sine], axis=-1
    )


def dot(left, right):
    return jnp.dot(left, right, preferred_element_type=f32)


def right_transposed(left, right):
    return lax.dot_general(left, right, (((1,), (1,)), ((), ())), preferred_element_type=f32)


def left_transposed(left, right):
    return lax.dot_general(left, right, (((0,), (0,)), ((), ())), preferred_element_type=f32)


def add_low(left, right):
    return (left.astype(f32) + right.astype(f32)).astype(bf16)


class Clock:
    def __init__(self):
        self.last = ()

    def all(self, *values):
        held = lax.optimization_barrier(values + self.last)
        self.last = (held[0],)
        return held[: len(values)]

    def __call__(self, *values):
        held = self.all(*values)
        return held[0] if len(values) == 1 else held


class Plane:
    def __init__(self, size):
        self.size = size
        self.fast = size == 8 and lax.axis_size("tok") == 4
        self.me = lax.axis_index("head")
        if self.fast:
            even = [index % 2 == 0 for index in range(size)]
            self.hop_a = [(i, i ^ (2 if even[i] else 4)) for i in range(size)]
            self.hop_b = [(i, i ^ (4 if even[i] else 2)) for i in range(size)]
            self.hop_c = [(i, i ^ 1) for i in range(size)]
            mask_a = jnp.where(self.me % 2 == 0, 2, 4)
            other = self.me ^ 1
            order = [
                self.me,
                other,
                self.me ^ mask_a,
                other ^ (6 - mask_a),
                self.me ^ (6 - mask_a),
                other ^ mask_a,
                self.me ^ 6,
                other ^ 6,
            ]
            self.table = jnp.stack(order).astype(jnp.int32)
            self.groups = [(0, 2), (2, 6), (6, 8)]
        else:
            self.table = jnp.arange(size, dtype=jnp.int32)
            self.groups = [(0, size)]

    def move(self, value, hop):
        return lax.ppermute(value, "head", hop)

    def gather(self, rows):
        whole = lax.all_gather(rows, "head", axis=0, tiled=True)
        return list(jnp.split(whole, self.size, axis=0))

    def scatter(self, pieces):
        whole = jnp.concatenate(pieces, axis=0)
        return lax.psum_scatter(whole, "head", scatter_dimension=0, tiled=True).astype(f32)

    def total(self, value):
        if not self.fast:
            return lax.psum(value, "head")
        for bit in (1, 2, 4):
            value = value + self.move(value, [(i, i ^ bit) for i in range(8)])
        return value


class Line:
    def __init__(self, size):
        self.size = size
        self.me = lax.axis_index("tok")
        half = size // 2
        self.stages = [([(k, k + 1), (size - 1 - k, size - 2 - k)], None) for k in range(half - 1)]
        self.stages.append(([(half - 1, half), (half, half - 1)], None))
        for k in reversed(range(half - 1)):
            self.stages.append(([(k + 1, k), (size - 2 - k, size - 1 - k)], k))

    def start(self, stage, value):
        return lax.ppermute(value, "tok", self.stages[stage][0])

    def finish(self, stage, value, came, plus=add_low):
        outward = self.stages[stage][1]
        if outward is None:
            return plus(value, came)
        mine = (self.me == outward) | (self.me == self.size - 1 - outward)
        return jnp.where(mine, came, value)

    def total(self, value, plus=add_low):
        for stage in range(len(self.stages)):
            value = self.finish(stage, value, self.start(stage, value), plus)
        return value


class Belt:
    inward = [(0, 1), (3, 2)]
    middle = [(1, 2), (2, 1)]
    outward = [(1, 0), (2, 3)]

    def __init__(self, line, clock):
        self.clock = clock
        self.inner = jnp.where((line.me == 1) | (line.me == 2), 1, 0).astype(jnp.int32).reshape(1)

    def move(self, value, pairs):
        return lax.ppermute(value, "tok", pairs)

    def begin(self, value):
        value = self.clock(value)
        return {"own": value, "came": self.move(value, self.inward)}

    def cross(self, item):
        item["came"] = self.clock(item["came"])
        item["own"] = self.clock(add_rows(item["own"], item["came"]))
        item["came"] = self.move(item["own"], self.middle)

    def meet(self, item):
        item["came"] = self.clock(item["came"])
        item["own"] = self.clock(add_rows(item["own"], item["came"]))

    def send(self, item):
        item["own"] = self.clock(item["own"])
        item["came"] = self.move(item["own"], self.outward)

    def back(self, item, value=None):
        if value is None:
            self.meet(item)
            self.send(item)
            return None
        item["came"] = self.clock(item["came"])
        both = self.clock(add_or_begin(self.inner, item["own"], item["came"], value))
        came = self.move(both, self.inward + self.outward)
        item["own"], item["came"] = both, came
        return {"own": value, "came": came}

    def land(self, item):
        item["came"] = self.clock(item["came"])

    def end(self, item, size, at=0, past=None, low=0, high=None):
        return settle(self.inner, item["own"], item["came"], size, at, past, low, high)


def query_blocks(length):
    first = min(length, max(first_document, length // 2))
    block = 256
    return [
        (start, min(block, length - start), 0 if start < first else first)
        for start in range(0, length, block)
    ]


def allowed(seg_column, seg_row, start, rows, low, high):
    query_order = start + lax.broadcasted_iota(jnp.int32, (rows, high - low), 0)
    key_order = low + lax.broadcasted_iota(jnp.int32, (rows, high - low), 1)
    same = seg_column[start : start + rows, :] == seg_row[:, low:high]
    return (key_order <= query_order) & same


def weights_of(stacked, keys, permit, heads, scale):
    scores = right_transposed(stacked, keys) * scale
    scores = jnp.where(jnp.concatenate([permit] * heads, axis=0), scores, -1e30)
    top = jnp.max(scores, axis=-1, keepdims=True)
    weights = jnp.exp(scores - top)
    return weights, jnp.sum(weights, axis=-1, keepdims=True)


def stack_heads(ref, start, rows, heads, width):
    return jnp.concatenate(
        [ref[start : start + rows, h * width : (h + 1) * width] for h in range(heads)], axis=0
    )


def attend_forward_kernel(count, heads, width, rank, scale, *refs):
    table = refs[0]
    pieces = refs[1 : 1 + count]
    weight, cosine, sine, seg_column, seg_row = refs[1 + count : 6 + count]
    latents, queries_out, keys_out, values_out, mixed_there = refs[6 + count : 11 + count]
    queries, keys, values, mixed, sems = refs[11 + count :]
    length = queries.shape[0]
    leaving = []

    def leave_now(source, target):
        copy = pltpu.make_async_copy(source, target, sems.at[len(leaving)])
        copy.start()
        leaving.append(copy)

    rows = length // count
    half = width // 2
    for r in range(count):
        there = pl.ds(pl.multiple_of(table[r] * rows, rows), rows)
        leave_now(pieces[r].at[:, :rank], latents.at[there, :])
        keys[there, :] = pieces[r][:, rank : rank + width]
        values[there, :] = pieces[r][:, rank + width :]
        flat = dot(pieces[r][:, :rank], weight[...])
        cos = cosine[there, :]
        sin = sine[there, :]
        for h in range(heads):
            first = flat[:, h * width : h * width + half]
            second = flat[:, h * width + half : (h + 1) * width]
            queries[there, h * width : h * width + half] = (first * cos - second * sin).astype(bf16)
            queries[there, h * width + half : (h + 1) * width] = (
                second * cos + first * sin
            ).astype(bf16)
    leave_now(queries, queries_out)
    leave_now(keys, keys_out)
    leave_now(values, values_out)
    for start, size, low in query_blocks(length):
        high = start + size
        stacked = stack_heads(queries, start, size, heads, width)
        permit = allowed(seg_column, seg_row, start, size, low, high)
        weights, total = weights_of(stacked, keys[low:high, :], permit, heads, scale)
        probs = (weights / total).astype(bf16)
        result = dot(probs, values[low:high, :]).astype(bf16)
        for h in range(heads):
            mixed[start:high, h * width : (h + 1) * width] = result[h * size : (h + 1) * size]
    for r in range(count):
        there = pl.ds(pl.multiple_of(table[r] * rows, rows), rows)
        mixed_there[r * rows : (r + 1) * rows, :] = mixed[there, :]
    for copy in leaving:
        copy.wait()


def brief():
    return pl.CostEstimate(flops=1024, bytes_accessed=1024, transcendentals=0)


def vmem():
    return pl.BlockSpec(memory_space=pltpu.VMEM)


def smem():
    return pl.BlockSpec(memory_space=pltpu.SMEM)


def attend_forward(table, pieces, weight, cosine, sine, segments, heads, width, scale):
    count = len(pieces)
    length = cosine.shape[0]
    rank = weight.shape[0]
    shapes = [
        jax.ShapeDtypeStruct((length, rank), bf16),
        jax.ShapeDtypeStruct((length, heads * width), bf16),
        jax.ShapeDtypeStruct((length, width), bf16),
        jax.ShapeDtypeStruct((length, width), bf16),
        jax.ShapeDtypeStruct((length, heads * width), bf16),
    ]
    return pl.pallas_call(
        functools.partial(attend_forward_kernel, count, heads, width, rank, scale),
        out_shape=shapes,
        in_specs=[smem()] + [vmem()] * (count + 5),
        out_specs=[any_space()] * 4 + [vmem()],
        scratch_shapes=[
            pltpu.VMEM((length, heads * width), bf16),
            pltpu.VMEM((length, width), bf16),
            pltpu.VMEM((length, width), bf16),
            pltpu.VMEM((length, heads * width), bf16),
            pltpu.SemaphoreType.DMA((count + 3,)),
        ],
        compiler_params=pltpu.CompilerParams(vmem_limit_bytes=48 << 20),
        cost_estimate=brief(),
        name="attend_forward",
    )(table, *pieces, weight, cosine, sine, segments[:, None], segments[None, :])


def attend_backward_kernel(parts, heads, width, scale, *refs):
    table = refs[0]
    grads_in = refs[1 : 1 + parts]
    queries, keys, values, cosine, sine, seg_column, seg_row = refs[1 + parts : 8 + parts]
    query_out, pair_out, outer, key_total, value_total = refs[8 + parts :]
    length = queries.shape[0]
    count = table.shape[0]
    rows = length // count
    half = width // 2

    def there(r):
        return pl.ds(pl.multiple_of(table[r] * rows, rows), rows)

    r = 0
    for part in grads_in:
        for k in range(part.shape[0] // rows):
            outer[there(r), :] = part[k * rows : (k + 1) * rows, :]
            r += 1
    key_total[...] = jnp.zeros_like(key_total)
    value_total[...] = jnp.zeros_like(value_total)
    for start, size, low in query_blocks(length):
        high = start + size
        stacked = stack_heads(queries, start, size, heads, width)
        grads = stack_heads(outer, start, size, heads, width)
        permit = allowed(seg_column, seg_row, start, size, low, high)
        weights, total = weights_of(stacked, keys[low:high, :], permit, heads, scale)
        probs = weights / total
        prob_grad = right_transposed(grads, values[low:high, :])
        centre = jnp.sum(probs * prob_grad, axis=-1, keepdims=True)
        score_grad = (probs * (prob_grad - centre)).astype(bf16)
        query_grad = dot(score_grad, keys[low:high, :]) * scale
        key_total[low:high, :] += left_transposed(score_grad, stacked) * scale
        value_total[low:high, :] += left_transposed(probs.astype(bf16), grads)
        cos = cosine[start:high, :]
        sin = sine[start:high, :]
        for h in range(heads):
            first = query_grad[h * size : (h + 1) * size, :half]
            second = query_grad[h * size : (h + 1) * size, half:]
            query_out[start:high, h * width : h * width + half] = (
                first * cos + second * sin
            ).astype(bf16)
            query_out[start:high, h * width + half : (h + 1) * width] = (
                second * cos - first * sin
            ).astype(bf16)
    pair_out[:, :width] = key_total[...].astype(bf16)
    pair_out[:, width:] = value_total[...].astype(bf16)


def attend_backward(table, grads, queries, keys, values, cosine, sine, segments, heads, scale):
    parts = len(grads)
    length, width = keys.shape
    shapes = [
        jax.ShapeDtypeStruct((length, heads * width), bf16),
        jax.ShapeDtypeStruct((length, 2 * width), bf16),
    ]
    return pl.pallas_call(
        functools.partial(attend_backward_kernel, parts, heads, width, scale),
        out_shape=shapes,
        in_specs=[smem()] + [vmem()] * (parts + 7),
        out_specs=[vmem()] * 2,
        scratch_shapes=[
            pltpu.VMEM((length, heads * width), bf16),
            pltpu.VMEM((length, width), f32),
            pltpu.VMEM((length, width), f32),
        ],
        compiler_params=pltpu.CompilerParams(vmem_limit_bytes=44 << 20),
        cost_estimate=brief(),
        name="attend_backward",
    )(
        table,
        *grads,
        queries,
        keys,
        values,
        cosine,
        sine,
        segments[:, None],
        segments[None, :],
    )


def rows_product_kernel(*refs):
    pieces, weight, out = refs[:-2], refs[-2], refs[-1]
    rows = pieces[0].shape[0]
    for p in range(0, len(pieces), 2):
        here = jnp.concatenate([pieces[p][...], pieces[p + 1][...]], axis=0)
        out[p * rows : (p + 2) * rows, :] = right_transposed(here, weight[...]).astype(out.dtype)


def rows_product(pieces, weight, kind):
    return pl.pallas_call(
        rows_product_kernel,
        out_shape=jax.ShapeDtypeStruct(
            (len(pieces) * pieces[0].shape[0], weight.shape[0]), kind
        ),
        in_specs=[vmem()] * (len(pieces) + 1),
        out_specs=vmem(),
        compiler_params=pltpu.CompilerParams(vmem_limit_bytes=36 << 20),
        cost_estimate=brief(),
        name="rows_product",
    )(*pieces, weight)


def latent_share_kernel(low, size, table, query_grads, pairs, weight, *refs):
    outs = refs[:-3]
    held, beside, sems = refs[-3:]
    rows = outs[0].shape[0]
    rank = weight.shape[0]
    copies = []
    for k in range(size // rows):
        there = pl.ds(pl.multiple_of(table[low + k] * rows, rows), rows)
        here = pl.ds(k * rows, rows)
        copies += [
            pltpu.make_async_copy(query_grads.at[there, :], held.at[here, :], sems.at[0, k]),
            pltpu.make_async_copy(pairs.at[there, :], beside.at[here, :], sems.at[1, k]),
        ]
    for copy in copies:
        copy.start()
    for copy in copies:
        copy.wait()
    for p in range(0, size // rows, 2):
        total = right_transposed(held[p * rows : (p + 2) * rows, :], weight[...])
        for k in range(2):
            outs[p + k][:, :rank] = total[k * rows : (k + 1) * rows].astype(bf16)
            outs[p + k][:, rank:] = beside[(p + k) * rows : (p + k + 1) * rows, :]


def latent_shares(table, query_grads, pairs, weight):
    count = table.shape[0]
    rows = query_grads.shape[0] // count
    rank, inner = weight.shape
    extra = pairs.shape[1]

    def share(clock, low, high):
        size = (high - low) * rows
        return pl.pallas_call(
            functools.partial(latent_share_kernel, low, size),
            out_shape=[jax.ShapeDtypeStruct((rows, rank + extra), bf16)] * (high - low),
            in_specs=[smem(), any_space(), any_space(), vmem()],
            out_specs=[vmem()] * (high - low),
            scratch_shapes=[
                pltpu.VMEM((size, inner), bf16),
                pltpu.VMEM((size, extra), bf16),
                pltpu.SemaphoreType.DMA((2, high - low)),
            ],
            compiler_params=pltpu.CompilerParams(vmem_limit_bytes=36 << 20),
            cost_estimate=brief(),
            name="latent_share",
        )(table, *clock(query_grads, pairs), weight)

    return share


def join_kernel(count, *refs):
    pieces, whole = refs[:count], refs[count]
    rows = pieces[0].shape[0]
    for r in range(count):
        whole[r * rows : (r + 1) * rows, :] = pieces[r][...]


def join(pieces):
    count = len(pieces)
    rows, columns = pieces[0].shape
    step = min(columns, 512)
    return pl.pallas_call(
        functools.partial(join_kernel, count),
        grid=(columns // step,),
        out_shape=jax.ShapeDtypeStruct((count * rows, columns), bf16),
        in_specs=[pl.BlockSpec((rows, step), lambda j: (0, j))] * count,
        out_specs=pl.BlockSpec((count * rows, step), lambda j: (0, j)),
        compiler_params=pltpu.CompilerParams(vmem_limit_bytes=17 << 20),
        cost_estimate=brief(),
        name="join",
    )(*pieces)


def any_space():
    return pl.BlockSpec(memory_space=pl.ANY)


def share_kernel(low, size, terms, *refs):
    lefts = refs[:terms]
    weights = refs[terms : 2 * terms]
    outs = refs[2 * terms : -terms - 1]
    held, sems = refs[-terms - 1 : -1], refs[-1]
    rows = outs[0].shape[0]
    copies = []
    for t in range(terms):
        copy = pltpu.make_async_copy(lefts[t].at[pl.ds(low * rows, size), :], held[t], sems.at[t])
        copy.start()
        copies.append(copy)
    for copy in copies:
        copy.wait()
    for p in range(size // (2 * rows)):
        here = pl.ds(2 * p * rows, 2 * rows)
        total = dot(held[0][here, :], weights[0][...])
        for t in range(1, terms):
            total = total + dot(held[t][here, :], weights[t][...])
        outs[2 * p][...] = total[:rows].astype(bf16)
        outs[2 * p + 1][...] = total[rows:].astype(bf16)


def shares(lefts, weights, count):
    rows = lefts[0].shape[0] // count
    inner = lefts[0].shape[1]
    columns = weights[0].shape[1]
    terms = len(lefts)

    def share(clock, low, high):
        size = (high - low) * rows
        return pl.pallas_call(
            functools.partial(share_kernel, low, size, terms),
            out_shape=[jax.ShapeDtypeStruct((rows, columns), bf16)] * (high - low),
            in_specs=[any_space()] * terms + [vmem()] * terms,
            out_specs=[vmem()] * (high - low),
            scratch_shapes=[pltpu.VMEM((size, inner), bf16)] * terms
            + [pltpu.SemaphoreType.DMA((terms,))],
            compiler_params=pltpu.CompilerParams(vmem_limit_bytes=36 << 20),
            cost_estimate=brief(),
            name="share",
        )(*clock.all(*lefts), *weights)

    return share


def feed_kernel(pairs, first, *refs):
    pieces = refs[: 2 * pairs]
    upper, gate_weight, up_weight = refs[2 * pairs : 2 * pairs + 3]
    rest = refs[2 * pairs + 3 :]
    outs, held, buffers, sems = rest[-8:-5], rest[-5], rest[-4:-1], rest[-1]
    rows = pieces[0].shape[0]

    def rows_of(p):
        return pl.ds((first + p) * 2 * rows, 2 * rows)

    loads = []
    for p in range(pairs):
        load = pltpu.make_async_copy(upper.at[rows_of(p), :], held.at[p], sems.at[3, p])
        load.start()
        loads.append(load)
    copies = []
    for p in range(pairs):
        here = jnp.concatenate([pieces[2 * p][...], pieces[2 * p + 1][...]], axis=0)
        gate = right_transposed(here, gate_weight[...])
        upward = right_transposed(here, up_weight[...])
        loads[p].wait()
        hidden_grad = held[p].astype(f32)
        sigmoid = jax.nn.sigmoid(gate)
        swish = gate * sigmoid
        results = (
            swish * upward,
            hidden_grad * upward * sigmoid * (1.0 + gate * (1.0 - sigmoid)),
            hidden_grad * swish,
        )
        for k, result in enumerate(results):
            buffers[k][p] = result.astype(bf16)
            copy = pltpu.make_async_copy(buffers[k].at[p], outs[k].at[rows_of(p), :], sems.at[k, p])
            copy.start()
            copies.append(copy)
    for copy in copies:
        copy.wait()


def feed(pieces, low, high, upper, gate_weight, up_weight, count, past):
    rows, dim = pieces[low].shape
    units = gate_weight.shape[0]
    pairs = (high - low) // 2
    operands = list(pieces[low:high]) + [upper, gate_weight, up_weight]
    specs = [vmem()] * (high - low) + [any_space()] + [vmem()] * 2
    aliases = {}
    if past is not None:
        aliases = {len(operands) + k: k for k in range(3)}
        operands += list(past)
        specs += [any_space()] * 3
    size = (high - low) * rows
    return pl.pallas_call(
        functools.partial(feed_kernel, pairs, low // 2),
        out_shape=[jax.ShapeDtypeStruct((count * rows, units), bf16)] * 3,
        in_specs=specs,
        out_specs=[any_space()] * 3,
        scratch_shapes=[pltpu.VMEM((pairs, 2 * rows, units), bf16)]
        + [pltpu.VMEM((pairs, 2 * rows, units), bf16)] * 3
        + [pltpu.SemaphoreType.DMA((4, pairs))],
        input_output_aliases=aliases,
        compiler_params=pltpu.CompilerParams(vmem_limit_bytes=28 << 20),
        cost_estimate=brief(),
        name="feed",
    )(*operands)


def sum_kernel(*refs):
    total = refs[0][...].astype(f32)
    for ref in refs[1:-1]:
        total = total + ref[...].astype(f32)
    refs[-1][...] = total.astype(bf16)


def call(kernel, shapes, operands, name, scalars=0, limit=24, scratch=()):
    single = not isinstance(shapes, list)
    return pl.pallas_call(
        kernel,
        out_shape=shapes,
        in_specs=[smem()] * scalars + [vmem()] * (len(operands) - scalars),
        out_specs=vmem() if single else [vmem()] * len(shapes),
        scratch_shapes=list(scratch),
        compiler_params=pltpu.CompilerParams(vmem_limit_bytes=limit << 20),
        cost_estimate=brief(),
        name=name,
    )(*operands)


def shaped(shape, kind):
    return jax.ShapeDtypeStruct(shape, kind)


def add_rows(*values):
    return call(sum_kernel, shaped(values[0].shape, bf16), values, "add_rows")


def add_or_begin_kernel(inner, own, came, value, out):
    @pl.when(inner[0] == 1)
    def _():
        out[...] = (own[...].astype(f32) + came[...].astype(f32)).astype(bf16)

    @pl.when(inner[0] == 0)
    def _():
        out[...] = value[...]


def add_or_begin(inner, own, came, value):
    return call(
        add_or_begin_kernel,
        shaped(own.shape, bf16),
        [inner, own, came, value],
        "add_or_begin",
        scalars=1,
    )


def settle_kernel(low, at, *refs):
    inner, own, came = refs[:3]
    out, buffer, sem = refs[-3:]
    rows = buffer.shape[0]

    @pl.when(inner[0] == 1)
    def _():
        buffer[...] = own[low : low + rows, :].astype(f32)

    @pl.when(inner[0] == 0)
    def _():
        buffer[...] = came[low : low + rows, :].astype(f32)

    copy = pltpu.make_async_copy(buffer, out.at[pl.ds(at, rows), :], sem)
    copy.start()
    copy.wait()


def settle(inner, own, came, size, at=0, past=None, low=0, high=None):
    columns = own.shape[1]
    rows = (high or own.shape[0]) - low
    operands = [inner, own, came]
    specs = [smem(), vmem(), vmem()]
    aliases = {}
    if past is not None:
        aliases = {3: 0}
        operands.append(past)
        specs.append(any_space())
    return pl.pallas_call(
        functools.partial(settle_kernel, low, at),
        out_shape=shaped((size, columns), f32),
        in_specs=specs,
        out_specs=any_space(),
        scratch_shapes=[pltpu.VMEM((rows, columns), f32), pltpu.SemaphoreType.DMA],
        input_output_aliases=aliases,
        compiler_params=pltpu.CompilerParams(vmem_limit_bytes=16 << 20),
        cost_estimate=brief(),
        name="settle",
    )(*operands)


def product_kernel(count, first, step, left, *refs):
    pieces = refs[:count]
    outs, held, sems = refs[count + first : -2], refs[-2], refs[-1]
    rows = pieces[0].shape[0]
    here = pl.program_id(0)
    steps = pl.num_programs(0)

    def copies(j, slot):
        there = pl.ds(pl.multiple_of(j * step, step), step)
        return [
            pltpu.make_async_copy(
                pieces[r].at[:, there], held.at[slot, pl.ds(r * rows, rows), :], sems.at[slot, r]
            )
            for r in range(count)
        ]

    slot = lax.rem(here, 2)

    @pl.when(here == 0)
    def _():
        for copy in copies(0, 0):
            copy.start()

    @pl.when(here + 1 < steps)
    def _():
        for copy in copies(here + 1, 1 - slot):
            copy.start()

    for copy in copies(here, slot):
        copy.wait()
    total = left_transposed(left[...], held[slot]).astype(bf16)
    if first:
        total = jnp.concatenate([refs[count][...], total], axis=0)
    low = 0
    for out in outs:
        size = out.shape[0]
        out[...] = total[low : low + size]
        low += size


def weight_product(left, right, rows, above=None, step=1024):
    right = list(right) if isinstance(right, (list, tuple)) else [right]
    count = len(right)
    tokens, units = left.shape
    columns = right[0].shape[1]
    step = min(step, columns)
    operands = [left, *right]
    specs = [pl.BlockSpec((tokens, units), lambda j: (0, 0))] + [any_space()] * count
    if above is not None:
        operands.append(above)
        specs.append(pl.BlockSpec((above.shape[0], step), lambda j: (0, j)))
    return pl.pallas_call(
        functools.partial(product_kernel, count, len(operands) - 1 - count, step),
        grid=(columns // step,),
        out_shape=[shaped((one, columns), bf16) for one in rows],
        in_specs=specs,
        out_specs=[pl.BlockSpec((one, step), lambda j: (0, j)) for one in rows],
        scratch_shapes=[
            pltpu.VMEM((2, tokens, step), bf16),
            pltpu.SemaphoreType.DMA((2, count)),
        ],
        compiler_params=pltpu.CompilerParams(vmem_limit_bytes=30 << 20),
        cost_estimate=brief(),
        name="weight_product",
    )(*operands)


def pack_last_kernel(above, wide, below, out):
    top = above.shape[0]
    rows, columns = wide.shape
    parts = out.shape[1] // columns
    step = rows // parts
    out[:top, :] = above[...]
    for j in range(parts):
        out[top : top + step, j * columns : (j + 1) * columns] = wide[j * step : (j + 1) * step, :]
    out[top + step :, :] = below[...]


def pack_last(above, wide, below):
    columns = above.shape[1]
    rows = above.shape[0] + wide.size // columns + below.shape[0]
    return call(
        pack_last_kernel, shaped((rows, columns), bf16), [above, wide, below], "pack_last"
    )


def settle_last_kernel(top, at, inner, own, came, past, wide, below, whole, buffer, sem):
    rows, columns = wide.shape
    parts = own.shape[1] // columns
    step = rows // parts

    def write(source):
        buffer[...] = source[:top, :].astype(f32)
        copy = pltpu.make_async_copy(buffer, whole.at[pl.ds(at, top), :], sem)
        copy.start()
        for j in range(parts):
            wide[j * step : (j + 1) * step, :] = source[
                top : top + step, j * columns : (j + 1) * columns
            ].astype(f32)
        below[...] = source[top + step :, :].astype(f32)
        copy.wait()

    @pl.when(inner[0] == 1)
    def _():
        write(own)

    @pl.when(inner[0] == 0)
    def _():
        write(came)


def settle_last(inner, own, came, top, rows, columns, past, at):
    total, dim = own.shape
    left = total - top - rows * columns // dim
    return pl.pallas_call(
        functools.partial(settle_last_kernel, top, at),
        out_shape=[
            shaped((rows, columns), f32),
            shaped((left, dim), f32),
            shaped(past.shape, f32),
        ],
        in_specs=[smem(), vmem(), vmem(), any_space()],
        out_specs=[vmem(), vmem(), any_space()],
        scratch_shapes=[pltpu.VMEM((top, dim), f32), pltpu.SemaphoreType.DMA],
        input_output_aliases={3: 2},
        compiler_params=pltpu.CompilerParams(vmem_limit_bytes=24 << 20),
        cost_estimate=brief(),
        name="settle_last",
    )(inner, own, came, past)


def pack_kernel(count, *refs):
    total = summed(refs[:count]).astype(bf16)
    beside, out = refs[count:]
    rows, columns = total.shape
    tall = rows * 3 // 4
    out[:tall, :columns] = total[:tall]
    third = columns // 3
    for j in range(3):
        low = j * (rows - tall)
        out[low : low + rows - tall, columns:] = total[tall:, j * third : (j + 1) * third]
    out[tall:, :] = beside[...]


def pack(parts, beside):
    rows, columns = parts[0].shape
    tall = rows * 3 // 4
    return call(
        functools.partial(pack_kernel, len(parts)),
        shaped((tall + beside.shape[0], beside.shape[1]), bf16),
        [*parts, beside],
        "pack",
    )


def pick_kernel(inner, own, came, out):
    rows = out.shape[0]

    @pl.when(inner[0] == 1)
    def _():
        out[...] = own[:rows, :]

    @pl.when(inner[0] == 0)
    def _():
        out[...] = came[:rows, :]


def pick(inner, own, came, rows):
    return call(
        pick_kernel,
        shaped((rows, own.shape[1]), bf16),
        [inner, own, came],
        "pick",
        scalars=1,
    )


def widen_kernel(*refs):
    out = refs[-1]
    low = 0
    for x in refs[:-1]:
        rows = x.shape[0]
        out[low : low + rows, :] = x[...].astype(f32)
        low += rows


def widen(parts, step=512):
    rows = sum(part.shape[0] for part in parts)
    columns = parts[0].shape[1]
    return pl.pallas_call(
        widen_kernel,
        grid=(columns // step,),
        out_shape=shaped((rows, columns), f32),
        in_specs=[pl.BlockSpec((part.shape[0], step), lambda j: (0, j)) for part in parts],
        out_specs=pl.BlockSpec((rows, step), lambda j: (0, j)),
        compiler_params=pltpu.CompilerParams(vmem_limit_bytes=16 << 20),
        cost_estimate=brief(),
        name="widen",
    )(*parts)


def settle_two_kernel(inner, own, came, above, below):
    rows = above.shape[0]

    @pl.when(inner[0] == 1)
    def _():
        above[...] = own[:rows, :].astype(f32)
        below[...] = own[rows:, :].astype(f32)

    @pl.when(inner[0] == 0)
    def _():
        above[...] = came[:rows, :].astype(f32)
        below[...] = came[rows:, :].astype(f32)


def settle_two(inner, own, came, rows):
    total, columns = own.shape
    return call(
        settle_two_kernel,
        [shaped((rows, columns), f32), shaped((total - rows, columns), f32)],
        [inner, own, came],
        "settle_two",
        scalars=1,
    )


def rotated(first, second, cosine, sine):
    return first * cosine - second * sine, second * cosine + first * sine


def enter_kernel(rank, width, x, gain, down, latent_gain, key, value, cosine, sine, *outs):
    normed, latent, packed = outs
    half = width // 2
    rows = x[...].astype(f32)
    low = (rows * inverse_rms(rows) * gain[...]).astype(bf16)
    normed[...] = low
    inner = dot(low, down[...])
    latent[...] = inner
    packed[:, :rank] = (inner * inverse_rms(inner) * latent_gain[...]).astype(bf16)
    keys = dot(low, key[...])
    first, second = rotated(keys[:, :half], keys[:, half:], cosine[...], sine[...])
    packed[:, rank : rank + half] = first.astype(bf16)
    packed[:, rank + half : rank + width] = second.astype(bf16)
    packed[:, rank + width :] = dot(low, value[...]).astype(bf16)


def enter(x, gain, down, latent_gain, key, value, cosine, sine):
    rows, dim = x.shape
    rank, width = down.shape[1], key.shape[1]
    return call(
        functools.partial(enter_kernel, rank, width),
        [shaped((rows, dim), bf16), shaped((rows, rank), f32), shaped((rows, rank + 2 * width), bf16)],
        [x, gain[None], down, latent_gain[None], key, value, cosine, sine],
        "enter",
        limit=60,
    )


def summed(parts):
    total = parts[0][...].astype(f32)
    for part in parts[1:]:
        total = total + part[...].astype(f32)
    return total


def middle_kernel(x, gain, *refs):
    parts, (middle, normed) = refs[:-2], refs[-2:]
    total = x[...].astype(f32) + summed(parts)
    middle[...] = total
    normed[...] = (total * inverse_rms(total) * gain[...]).astype(bf16)


def middle_rows(x, gain, parts):
    shape = x.shape
    return call(
        middle_kernel,
        [shaped(shape, f32), shaped(shape, bf16)],
        [x, gain[None], *parts],
        "middle_rows",
    )


def lower_norm(value, gain, upper):
    scale = inverse_rms(value)
    scaled = upper * gain
    lower = scale * scaled - value * (scale * scale * scale) * jnp.mean(
        scaled * value, axis=-1, keepdims=True
    )
    return lower, jnp.sum(upper * value * scale, axis=0, keepdims=True)


def middle_back_kernel(middle, gain, cotangent, *refs):
    parts, (total, low, gain_part) = refs[:-3], refs[-3:]
    lower, gain_part[...] = lower_norm(middle[...], gain[...], summed(parts))
    result = cotangent[...].astype(f32) + lower
    total[...] = result
    low[...] = result.astype(bf16)


def middle_back(middle, gain, cotangent, parts):
    shape = middle.shape
    return call(
        middle_back_kernel,
        [shaped(shape, f32), shaped(shape, bf16), shaped((1, shape[1]), f32)],
        [middle, gain[None], cotangent, *parts],
        "middle_back",
    )


def latent_back_kernel(latent, gain, cosine, sine, *refs):
    parts, (packed, gain_part) = refs[:-2], refs[-2:]
    rank = latent.shape[1]
    total = summed(parts)
    lower, gain_part[...] = lower_norm(latent[...], gain[...], total[:, :rank])
    width = (total.shape[1] - rank) // 2
    half = width // 2
    packed[:, :rank] = lower.astype(bf16)
    first, second = rotated(
        total[:, rank : rank + half], total[:, rank + half : rank + width], cosine[...], -sine[...]
    )
    packed[:, rank : rank + half] = first.astype(bf16)
    packed[:, rank + half : rank + width] = second.astype(bf16)
    packed[:, rank + width :] = total[:, rank + width :].astype(bf16)


def latent_back(latent, gain, cosine, sine, parts):
    shape = parts[0].shape
    return call(
        latent_back_kernel,
        [shaped(shape, bf16), shaped((1, latent.shape[1]), f32)],
        [latent, gain[None], cosine, sine, *parts],
        "latent_back",
    )


def leave_kernel(packed, down, key, value, x, gain, upper, result, gain_part):
    rank, width = down.shape[1], key.shape[1]
    total = right_transposed(packed[:, :rank], down[...])
    total = total + right_transposed(packed[:, rank : rank + width], key[...])
    total = total + right_transposed(packed[:, rank + width :], value[...])
    lower, gain_part[...] = lower_norm(x[...].astype(f32), gain[...], total)
    result[...] = upper[...] + lower


def leave(packed, down, key, value, x, gain, upper):
    return call(
        leave_kernel,
        [shaped(x.shape, f32), shaped((1, x.shape[1]), f32)],
        [packed, down, key, value, x, gain[None], upper],
        "leave",
    )


def shared_kernel(count, table, normed, grads, *outs):
    rows = outs[0].shape[0]
    for r in range(count):
        there = pl.ds(pl.multiple_of(table[r] * rows, rows), rows)
        outs[r][...] = left_transposed(normed[:, there], grads[...]).astype(bf16)


def shared_shares(table, normed, grads):
    count = table.shape[0]
    rows = normed.shape[1] // count
    columns = grads.shape[1]
    return list(
        pl.pallas_call(
            functools.partial(shared_kernel, count),
            out_shape=[jax.ShapeDtypeStruct((rows, columns), bf16)] * count,
            in_specs=[smem(), vmem(), vmem()],
            out_specs=[vmem()] * count,
            compiler_params=pltpu.CompilerParams(vmem_limit_bytes=36 << 20),
            cost_estimate=brief(),
            name="shared_shares",
        )(table, normed, grads)
    )


def unpack_kernel(base, count, parts, packed, table, *refs):
    pieces = refs[:count]
    outs, buffers = refs[-1 - 2 * len(parts) : -1 - len(parts)], refs[-1 - len(parts) : -1]
    sems = refs[-1]
    rows = buffers[0].shape[1]
    tall = rows * 3 // 4
    columns = parts[-1][1]
    third = columns // 3
    flying = []
    for r in range(count):
        slot = r % 2
        if r >= 2:
            for copy in flying[r - 2]:
                copy.wait()
        there = pl.ds(pl.multiple_of(table[base + r] * rows, rows), rows)
        copies = []
        for k, (low, high) in enumerate(parts):
            if packed:
                buffers[k][slot, :tall, :] = pieces[r][:, low:high].astype(f32)
                for j in range(3):
                    first, last = max(low, j * third), min(high, (j + 1) * third)
                    if first < last:
                        start = columns - j * third
                        buffers[k][slot, tall:, first - low : last - low] = pieces[r][
                            j * (rows - tall) : (j + 1) * (rows - tall),
                            start + first : start + last,
                        ].astype(f32)
            else:
                buffers[k][slot] = pieces[r][:, low:high].astype(f32)
            copy = pltpu.make_async_copy(
                buffers[k].at[slot], outs[k].at[there, :], sems.at[k, slot]
            )
            copy.start()
            copies.append(copy)
        flying.append(copies)
    for copies in flying[-2:]:
        for copy in copies:
            copy.wait()


def unpack(table, pieces, parts, packed, first=0, past=None):
    count = len(pieces)
    rows = pieces[0].shape[0]
    if packed:
        rows = rows * 4 // 3
    past = [] if past is None else list(past)
    return pl.pallas_call(
        functools.partial(unpack_kernel, first, count, parts, packed),
        out_shape=[
            jax.ShapeDtypeStruct((table.shape[0] * rows, high - low), f32) for low, high in parts
        ],
        in_specs=[smem()] + [vmem()] * count + [any_space()] * len(past),
        out_specs=[any_space()] * len(parts),
        scratch_shapes=[pltpu.VMEM((2, rows, high - low), f32) for low, high in parts]
        + [pltpu.SemaphoreType.DMA((len(parts), 2))],
        input_output_aliases={1 + count + k: k for k in range(len(past))},
        compiler_params=pltpu.CompilerParams(vmem_limit_bytes=24 << 20),
        cost_estimate=brief(),
        name="unpack",
    )(table, *pieces, *past)


def body(
    packs,
    group,
    block_input,
    segment_ids,
    positions,
    attention_gain,
    query_down,
    query_gain,
    query_up,
    key_proj,
    value_proj,
    out_proj,
    feed_gain,
    gate_weight,
    up_weight,
    down_weight,
    out_grad,
):
    plane = Plane(group)
    line = Line(packs)
    rows = block_input.shape[1]
    segments = segment_ids[0]
    places = positions[0]
    width = key_proj.shape[1]
    rank = query_down.shape[1]
    heads = query_up.shape[1] // width
    scale = 1.0 / math.sqrt(width)
    first_row = plane.me * rows

    gate_rows, up_rows = gate_weight.T, up_weight.T
    clock = Clock()
    belt = Belt(line, clock)
    fast = plane.fast
    move = plane.move
    hop_a, hop_b, hop_c = (plane.hop_a, plane.hop_b, plane.hop_c) if fast else (None,) * 3
    cotangent_rows = out_grad[0]

    x = block_input[0]
    dim = x.shape[1]
    always = (segments[0] & 1) <= 1

    def stage(run):
        def inside():
            inner = Clock()
            inner.last = clock.last
            return tuple(run(inner))

        if not fast:
            return inside()
        shapes = jax.eval_shape(inside)
        result = lax.cond(
            always, inside, lambda: tuple(jnp.zeros(one.shape, one.dtype) for one in shapes)
        )
        return clock.all(*result)

    def hops(values, ways, filler=None, apart=False):
        def run(clock):
            held = clock.all(*values)
            came = [move(value, way) for value, way in zip(held, ways)]
            more = list(filler(clock, *came)) if filler else []
            return [*clock.all(*came), *more]

        result = stage(run) if apart else run(clock)
        return list(result[: len(values)]), list(result[len(values) :])

    def gather(rows, first=None, second=None, apart=False, between=None, last=False):
        def beside(clock, a, b, s_o):
            return first(clock, [rows, clock(s_o)]) if first else []

        (a, b, s_o), more = hops([rows, rows, rows], [hop_a, hop_b, hop_c], beside, apart)
        if between:
            between()

        def beside(clock, c, a_o, b_o):
            if not second:
                return []
            a_o, b_o = clock(a_o, b_o)
            return second(clock, [a, a_o, b, b_o], more)

        (c, a_o, b_o), later = hops([a, a, b], [hop_b, hop_c, hop_c], beside, apart)
        (c_o,), _ = hops([c], [hop_c], None, apart or last)
        return [rows, s_o, a, a_o, b, b_o, c, c_o], more, later

    def scatter(share, filler=None, apart=False, between=None, head=False):
        c, c_send = clock(*share(clock, 6, 8))
        (c_came,), near = hops(
            [c_send], [hop_c], lambda clock, came: clock(*share(clock, 2, 6)), apart or head
        )
        a, a_send, b, b_send = near
        c = clock(add_rows(c, c_came))
        (c_in, a_came, b_came), (own, own_send) = hops(
            [c, a_send, b_send],
            [hop_b, hop_c, hop_c],
            lambda clock, *came: clock(*share(clock, 0, 2)),
            apart,
        )
        a, b = clock(add_rows(a, a_came, c_in), add_rows(b, b_came))
        if between:
            between()
        (a_in, b_in, own_came), more = hops(
            [a, b, own_send],
            [hop_a, hop_b, hop_c],
            (lambda clock, *came: filler(clock)) if filler else None,
            apart,
        )
        return [own, own_came, b_in, a_in], more

    own_places = lax.dynamic_slice_in_dim(places, first_row, rows, 0)
    own_cosine, own_sine = rotation(own_places, width)

    def enter_rows():
        return enter(
            x, attention_gain, query_down, query_gain, key_proj, value_proj, own_cosine, own_sine
        )

    def attend(pieces, cosine, sine):
        return attend_forward(
            plane.table, pieces, query_up, cosine, sine, segments, heads, width, scale
        )

    def attend_back(outer):
        return attend_backward(
            plane.table, outer, queries, keys, values, cosine, sine, segments, heads, scale
        )

    def leave_rows(packed_grad):
        return leave(
            packed_grad, query_down, key_proj, value_proj, x, attention_gain, middle_grad
        )

    def sum_gains(parts, total):
        return total(jnp.concatenate(parts, axis=1))

    units = gate_rows.shape[0]
    size = heads * width
    columns = ((0, rank), (rank, rank + width), (rank + width, rank + 2 * width))
    add = lambda left, right: left + right

    if not fast:
        normed_rows, latent, packed = enter_rows()
        cosine, sine = rotation(places, width)
        pieces = plane.gather(packed)
        latents, queries, keys, values, mixed_there = attend(pieces, cosine, sine)
        share = shares([mixed_there], [out_proj], group)
        parts = [plane.scatter(share(clock, 0, group))]
        middle, normed_mid_rows = middle_rows(x, feed_gain, parts)
        cot_pieces = plane.gather(cotangent_rows)
        hidden_grad = rows_product(cot_pieces, down_weight, bf16)
        mid_pieces = plane.gather(normed_mid_rows)
        hidden, gate_grad, upward_grad = feed(
            mid_pieces, 0, group, hidden_grad, gate_rows, up_rows, group, None
        )
        cotangent, normed_mid = join(cot_pieces), join(mid_pieces)
        share = shares([gate_grad, upward_grad], [gate_rows, up_rows], group)
        parts = [plane.scatter(share(clock, 0, group))]
        middle_grad, attention_grad, feed_gain_part = middle_back(
            middle, feed_gain, cotangent_rows, parts
        )
        grad_pieces = plane.gather(attention_grad)
        outer = [rows_product(grad_pieces, out_proj, bf16)]
        query_pre_grad, pair_grads = attend_back(outer)
        share = latent_shares(plane.table, query_pre_grad, pair_grads, query_up)
        parts = [plane.scatter(share(clock, 0, group))]
        packed_grad, query_gain_part = latent_back(latent, query_gain, own_cosine, own_sine, parts)
        shared_pieces = shared_shares(plane.table, normed_rows, packed_grad)
        shared = line.total(plane.scatter(list(shared_pieces)).astype(bf16))
        query_down_gradient, key_proj_gradient, value_proj_gradient = unpack(
            plane.table, plane.gather(shared), columns, False
        )
        input_gradient, attention_gain_part = leave_rows(packed_grad)
        share = shares([hidden], [down_weight], group)
        block_output = add_rows(middle, plane.scatter(share(clock, 0, group)))
        gains = sum_gains([attention_gain_part, query_gain_part, feed_gain_part], plane.total)
        gains = line.total(gains, add)[0]
        down_gradient, gate_gradient, up_gradient, proj_gradient, query_up_gradient = (
            line.total(weight_product(left, right, [left.shape[1]])[0]).astype(f32)
            for left, right in (
                (hidden, cotangent),
                (gate_grad, normed_mid),
                (upward_grad, normed_mid),
                (mixed_there, join(grad_pieces)),
                (latents, query_pre_grad),
            )
        )
    else:
        half = units // 2
        cot_a = move(cotangent_rows, hop_a)
        normed_rows, latent, packed = enter_rows()
        packed = clock(packed)

        def angles(clock, own):
            return clock(*rotation(clock(places), width))

        pieces, (cosine, sine), _ = gather(packed, angles, apart=True)
        cot_now, cot_a = clock(cotangent_rows, cot_a)
        cot_b, cot_c = move(cot_now, hop_b), move(cot_a, hop_b)
        cot_o, cot_ao = move(cot_now, hop_c), move(cot_a, hop_c)
        pieces[0] = clock(packed)

        latents, queries, keys, values, mixed_there = clock(*attend(pieces, cosine, sine))
        share = shares([mixed_there], [out_proj], group)
        c, c_send = clock(*share(clock, 6, 8))

        def other_shares(clock, came):
            return [*clock(*share(clock, 2, 6)), *clock(*share(clock, 0, 2))]

        (c_came,), (a, a_send, b, b_send, own, own_send) = hops(
            [c_send], [hop_c], other_shares, True
        )
        cot_b, cot_c, cot_o, cot_ao = clock(cot_b, cot_c, cot_o, cot_ao)
        c = clock(add_rows(c, c_came))
        (c_in, a_came, b_came), _ = hops([c, a_send, b_send], [hop_b, hop_c, hop_c])
        a, b = clock(add_rows(a, a_came, c_in), add_rows(b, b_came))

        def beside_last(clock, a_in, b_in, own_came, cot_bo, cot_co):
            cot_bo, cot_co = clock(cot_bo, cot_co)
            cot_pieces = [cotangent_rows, cot_o, cot_a, cot_ao, cot_b, cot_bo, cot_c, cot_co]
            hidden_grad = clock(rows_product(cot_pieces, down_weight, bf16))
            return [hidden_grad]

        (a_in, b_in, own_came, cot_bo, cot_co), (hidden_grad,) = hops(
            [a, b, own_send, cot_b, cot_c], [hop_a, hop_b, hop_c, hop_c, hop_c], beside_last
        )
        cot_pieces = [cotangent_rows, cot_o, cot_a, cot_ao, cot_b, cot_bo, cot_c, cot_co]
        middle, normed_mid_rows = clock(*middle_rows(x, feed_gain, [own, own_came, b_in, a_in]))

        def feed_group(clock, pieces, low, high, past):
            pieces = [None] * low + [clock(pieces[0]), *pieces[1:]]
            return clock(
                *feed(pieces, low, high, hidden_grad, gate_rows, up_rows, group, past)
            )

        def near_feed(clock, near):
            return feed_group(clock, near, 0, 2, None)

        (a, b, s_o), past = hops(
            [normed_mid_rows] * 3,
            [hop_a, hop_b, hop_c],
            lambda clock, a, b, s_o: near_feed(clock, [normed_mid_rows, clock(s_o)]),
        )

        def next_feed(clock, c, a_o, b_o):
            a_o, b_o = clock(a_o, b_o)
            more = feed_group(clock, [a, a_o], 2, 4, past)
            return [a_o, b_o, *feed_group(clock, [b, b_o], 4, 6, more)]

        (c, a_o, b_o), past = hops([a, a, b], [hop_b, hop_c, hop_c], next_feed)
        a_o, b_o, *past = past
        (c_o,), _ = hops([c], [hop_c])
        hidden, gate_grad, upward_grad = feed_group(clock, [c, c_o], 6, 8, past)
        mid_pieces = [normed_mid_rows, s_o, a, a_o, b, b_o, c, c_o]
        chunk = units * 3 // 4
        tall = dim * 3 // (4 * group)
        beside = chunk - tall
        one, tail = clock(*weight_product(clock(hidden), cot_pieces, [chunk, units - chunk]))
        one = belt.begin(one)
        two = []

        def middle_filler(clock):
            part, rest = clock(
                *weight_product(clock(gate_grad), mid_pieces, [chunk, units - half], tail)
            )
            two.append(belt.begin(part))
            belt.cross(one)
            return [rest]

        share = shares([gate_grad, upward_grad], [gate_rows, up_rows], group)
        parts, (tail,) = scatter(share, middle_filler, head=True)
        two = two[0]
        middle_grad, attention_grad, feed_gain_part = clock(
            *middle_back(middle, feed_gain, cotangent_rows, parts)
        )

        def near_grad(clock, near):
            outer = clock(rows_product([clock(near[0]), near[1]], out_proj, bf16))
            pair = clock(*weight_product(clock(upward_grad), mid_pieces, [chunk, chunk], tail))
            return [outer, *pair]

        def next_grad(clock, near, more):
            return [clock(rows_product([clock(near[0]), *near[1:]], out_proj, bf16))]

        grad_pieces, (outer_near, three, four), (outer_next,) = gather(
            attention_grad, near_grad, next_grad, last=True
        )
        outer_last = clock(rows_product([clock(grad_pieces[6]), grad_pieces[7]], out_proj, bf16))
        three = belt.back(one, three)
        belt.cross(two)

        query_pre_grad, pair_grads = clock(*attend_back([outer_near, outer_next, clock(outer_last)]))

        def latent_filler(clock):
            return clock(
                *weight_product(clock(mixed_there), grad_pieces, [beside, size - beside])
            )

        share = latent_shares(plane.table, query_pre_grad, pair_grads, query_up)
        parts, (five, six) = scatter(share, latent_filler)
        packed_grad, query_gain_part = clock(
            *latent_back(latent, query_gain, own_cosine, own_sine, parts)
        )
        belt.cross(three)
        four = belt.back(two, four)

        shared_pieces = clock(*shared_shares(plane.table, normed_rows, packed_grad))

        def shared_filler(clock):
            leaving = clock(*leave_rows(clock(packed_grad)))
            product = clock(weight_product(clock(latents), query_pre_grad, [rank])[0])
            belt.land(one)
            return [*leaving, product, clock(belt.end(one, units))]

        parts, (input_gradient, attention_gain_part, query_sum, down_gradient) = scatter(
            lambda clock, low, high: shared_pieces[low:high], shared_filler
        )
        five = clock(pack(parts, five))
        five = belt.back(three, five)
        belt.cross(four)
        fill = -(2 * dim + rank) % (16 * dim)

        def gain_rows(clock):
            gains = sum_gains(
                [clock(attention_gain_part), query_gain_part, feed_gain_part], plane.total
            )
            gains = jnp.concatenate([gains[0], jnp.zeros((fill,), f32)]).reshape(-1, dim)
            return [pack_last(six, query_sum, gains.astype(bf16))]

        (six,) = stage(gain_rows)

        settled = []

        def turn():
            belt.cross(five)
            belt.back(four)
            begun = belt.begin(six)
            belt.land(two)
            down = clock(belt.end(two, units, chunk, down_gradient, 0, units - chunk))
            gate = clock(belt.end(two, units, 0, None, units - chunk))
            belt.land(three)
            gate = clock(belt.end(three, units, half, gate, 0, half))
            up = clock(belt.end(three, units, 0, None, half))
            belt.land(four)
            belt.back(five)
            belt.cross(begun)
            settled.extend([begun, down, gate, up])

        share = shares([hidden], [down_weight], group)
        parts, _ = scatter(share, None, True, turn)
        block_output = clock(add_rows(middle, *parts))
        six, down_gradient, gate_gradient, up_gradient = settled
        up_gradient = clock(belt.end(four, units, chunk - half, up_gradient))
        belt.meet(six)
        belt.land(five)
        belt.send(six)
        shared_rows = clock(pick(belt.inner, five["own"], five["came"], tall))

        def five_end(clock, own):
            held = dict(five, came=clock(five["came"]))
            return [clock(belt.end(held, size, 0, None, tall))]

        def near_unpack(clock, near, more):
            pieces = [shared_rows, s_one, *near]
            return clock(*unpack(plane.table, pieces, columns, True))

        (a, b, s_one), (proj_gradient,) = hops(
            [shared_rows] * 3, [hop_a, hop_b, hop_c], lambda clock, *came: five_end(clock, None), True
        )

        def beside_next(clock, c, a_o, b_o):
            a_o, b_o = clock(a_o, b_o)
            return near_unpack(clock, [a, a_o, b, b_o], None)

        (c, a_o, b_o), past = hops([a, a, b], [hop_b, hop_c, hop_c], beside_next, True)
        (c_o,), _ = hops([c], [hop_c], None, True)
        query_down_gradient, key_proj_gradient, value_proj_gradient = clock(
            *unpack(plane.table, [c, c_o], columns, True, 6, past)
        )
        belt.land(six)
        query_up_gradient, gains, proj_gradient = settle_last(
            belt.inner, six["own"], six["came"], size - beside, rank, size, proj_gradient, beside
        )
        gains = gains.reshape(-1)
    return (
        block_output[None],
        input_gradient[None],
        gains[:dim],
        query_down_gradient,
        gains[dim : dim + rank],
        query_up_gradient,
        key_proj_gradient,
        value_proj_gradient,
        proj_gradient,
        gains[dim + rank : dim + rank + dim],
        gate_gradient.T,
        up_gradient.T,
        down_gradient,
    )


def solution(mesh):
    in_specs = (
        P("tok", "head", None),
        P("tok", None),
        P("tok", None),
        P(),
        P(),
        P(),
        P(None, "head"),
        P(),
        P(),
        P("head", None),
        P(),
        P(None, "head"),
        P(None, "head"),
        P("head", None),
        P("tok", "head", None),
    )
    out_specs = (
        P("tok", "head", None),
        P("tok", "head", None),
        P(),
        P(),
        P(),
        P(None, "head"),
        P(),
        P(),
        P("head", None),
        P(),
        P(None, "head"),
        P(None, "head"),
        P("head", None),
    )
    sizes = dict(mesh.shape)
    return jax.shard_map(
        functools.partial(body, sizes["tok"], sizes["head"]),
        mesh=mesh,
        in_specs=in_specs,
        out_specs=out_specs,
        check_vma=False,
    )
```
